32 devices in a mesh: dp: 16 (over z, y, core), tensor: 2 (over x).
Axes of the slice: x: 2, y: 2, z: 4, core: 2. Of those that a mesh axis runs over, the one named last changes fastest.
Arguments:
- block_input: float32 [8192, 1152], P(('dp', 'tensor')), may hold values from -6 to 6
- cotangent: float32 [8192, 1152], P(('dp', 'tensor')), may hold values from -6 to 6
- master: float32 [1152, 20736], P('dp', 'tensor')
- left_stats: float32 [16, 432, 72, 72], P('dp', 'tensor')
- right_stats: float32 [16, 432, 48, 48], P('dp', 'tensor')
- left_roots: float32 [16, 432, 72, 72], P('dp', 'tensor'), as said below
- right_roots: float32 [16, 432, 48, 48], P('dp', 'tensor'), as said below
- vec: float32 [7056], replicated
- vec_mom: float32 [7056], replicated, may hold values from -640 to 640
- time_table: float32 [1000, 1152], replicated, may hold values from -6 to 6
- class_table: float32 [1000, 1152], replicated, may hold values from -6 to 6
- bucket: int32 [32], P('dp'), may hold values from 0 to 999
- label: int32 [32], P('dp'), may hold values from 0 to 999
- owner: int32 [6], replicated, may hold values from 0 to 15
Outputs:
- block_output: float32 [8192, 1152], P(('dp', 'tensor'))
- dx: float32 [8192, 1152], P(('dp', 'tensor'))
- dc: float32 [32, 1152], P('dp', 'tensor')
- grad: float32 [1152, 20736], P('dp', 'tensor')
- left_new: float32 [16, 432, 72, 72], P('dp', 'tensor')
- right_new: float32 [16, 432, 48, 48], P('dp', 'tensor')
- master_new: float32 [1152, 20736], P('dp', 'tensor')
- weights_low: bfloat16 [1152, 20736], P('dp', 'tensor')
- vec_new: float32 [7056], replicated
- mom_new: float32 [7056], replicated
The draws below stay inside these ranges and needn't reach their ends.
Inputs may be any that keep to these rules, and one draw needn't show every extreme that they name: Matrix k (order A, Q, P, W1, W3, W2) keeps its row block b in owner row block (b + owner[k]) mod 16. `left_roots`: Symmetric. `right_roots`: Symmetric.
All inputs are finite; a program needn't handle non-finite values.
Results may differ from the reference program's by a relative error of at most 0.018.
Values may be sent and summed in bfloat16 or wider, within the bound.
No kernel may reach another device: no remote copies, remote signals or barrier semaphores. Data moves between devices by JAX's collectives and lax.ppermute only.
A program may use at most 192 MiB of HBM per device.

```python
import jax
import jax.numpy as jnp
from jax import lax

D = 1152
HEADS = 16
HEAD_DIM = 72
FF = 3072
CLASSES = 1000
TSTEPS = 1000
PATCHES = 256
GRID = 16
BLOCK_WIDTH = 48
TOKENS = 8192
IMAGES = 32
OWN_ROWS = 72
FLAT_COLS = 10368
BLOCKS = 216
VEC_LEN = 7056
N_DP = 16
N_TENSOR = 2


def draw_master(key, part):
    head_cols = D // N_TENSOR
    hidden_cols = FF // N_TENSOR
    column = jnp.arange(N_TENSOR * FLAT_COLS) % FLAT_COLS
    base = D ** (-0.5)
    scale = jnp.where(column < 9 * head_cols, base, jnp.where(column < 10 * head_cols, 6.0 * base, jnp.where(column < 10 * head_cols + 2 * hidden_cols, base, FF ** (-0.5))))
    return jax.random.normal(key, (D, N_TENSOR * FLAT_COLS), jnp.float32) * scale[None, :]


def symmetric(key, size, spread):
    lead = (N_DP, N_TENSOR * BLOCKS)
    base = jax.random.normal(key, lead + (size, size), jnp.float32)
    noise = (base + jnp.swapaxes(base, -1, -2)) * (spread / (2.0 * size) ** 0.5)
    return jnp.eye(size, dtype=jnp.float32) + noise


def levels(key, low_end, high_end):
    lead = (N_DP, N_TENSOR * BLOCKS)
    return jax.random.uniform(key, lead + (1, 1), jnp.float32, minval=low_end, maxval=high_end)


def draw_left_stats(key, part):
    level = levels(jax.random.fold_in(key, 11), 1.0, 4.0)
    return level * (0.5 * BLOCK_WIDTH * TOKENS) * symmetric(jax.random.fold_in(key, 12), OWN_ROWS, 0.3)


def draw_right_stats(key, part):
    level = levels(jax.random.fold_in(key, 21), 1.0, 4.0)
    return level * (0.5 * OWN_ROWS * TOKENS) * symmetric(jax.random.fold_in(key, 22), BLOCK_WIDTH, 0.3)


def draw_left_roots(key, part):
    level = levels(jax.random.fold_in(key, 31), 0.7, 1.4)
    return level * (BLOCK_WIDTH * TOKENS) ** (-0.25) * symmetric(jax.random.fold_in(key, 32), OWN_ROWS, 0.3)


def draw_right_roots(key, part):
    level = levels(jax.random.fold_in(key, 41), 0.7, 1.4)
    return level * (OWN_ROWS * TOKENS) ** (-0.25) * symmetric(jax.random.fold_in(key, 42), BLOCK_WIDTH, 0.3)


def draw_vec(key, part):
    bias = 0.5 * jax.random.normal(jax.random.fold_in(key, 51), (6 * D,), jnp.float32)
    gains = 1.0 + 0.2 * jax.random.normal(jax.random.fold_in(key, 52), (2 * HEAD_DIM,), jnp.float32)
    return jnp.concatenate([bias, gains])


def plant(array, key, least, largest):
    shape = array.shape
    index_at = [jax.random.randint(jax.random.fold_in(key, axis), (), 0, shape[axis]) for axis in range(len(shape))]
    array = array.at[tuple(index_at)].set(least)
    longest = shape.index(max(shape))
    index_at[longest] = (index_at[longest] + 1) % shape[longest]
    return array.at[tuple(index_at)].set(largest)


def steps_of(rng, extent, cuts, least, high):
    loudness = 1.0
    for dim, parts in cuts:
        draws = jax.random.uniform(jax.random.fold_in(jax.random.fold_in(rng, 6), dim), (parts,), jnp.float32, least / len(cuts), high / len(cuts))
        loudness = loudness * jnp.repeat(jnp.exp(draws), extent[dim] // parts).reshape((-1,) + (1,) * (len(extent) - 1 - dim))
    return loudness


def scatter_about(rng, shape, width, limit, split=(), kind=jnp.bfloat16):
    values = jax.random.normal(rng, shape, jnp.float32) * width
    if len(split) > 0:
        values = steps_of(rng, shape, split, -0.22, 0.18) * values
    return jnp.clip(values, min=-limit, max=limit).astype(kind)


def setup_inputs(seed: int = 0) -> dict:
    key_list = jax.random.split(jax.random.key(seed), 15)
    return {
        "block_input": scatter_about(key_list[0], (TOKENS, D), 1.0, 6.0, ((0, 32),), jnp.float32),
        "cotangent": scatter_about(key_list[1], (TOKENS, D), 1.0, 6.0, ((0, 32),), jnp.float32),
        "master": draw_master(jax.random.fold_in(key_list[14], 71), 0),
        "left_stats": draw_left_stats(jax.random.fold_in(key_list[14], 71), 0),
        "right_stats": draw_right_stats(jax.random.fold_in(key_list[14], 71), 0),
        "left_roots": draw_left_roots(jax.random.fold_in(key_list[14], 71), 0),
        "right_roots": draw_right_roots(jax.random.fold_in(key_list[14], 71), 0),
        "vec": draw_vec(jax.random.fold_in(key_list[14], 71), 0),
        "vec_mom": scatter_about(key_list[8], (VEC_LEN,), (1.1 * TOKENS ** 0.5), 640.0, (), jnp.float32),
        "time_table": scatter_about(key_list[9], (TSTEPS, D), 0.7, 6.0, (), jnp.float32),
        "class_table": scatter_about(key_list[10], (CLASSES, D), 0.7, 6.0, (), jnp.float32),
        "bucket": plant(jax.random.randint(key_list[11], (IMAGES,), 0, TSTEPS), jax.random.fold_in(key_list[11], 1), 0, TSTEPS - 1).astype(jnp.int32),
        "label": plant(jax.random.randint(key_list[12], (IMAGES,), 0, CLASSES), jax.random.fold_in(key_list[12], 1), 0, CLASSES - 1).astype(jnp.int32),
        "owner": plant(jax.random.randint(key_list[13], (6,), 0, N_DP), jax.random.fold_in(key_list[13], 1), 0, N_DP - 1).astype(jnp.int32),
    }


epsilon = 1e-06
precise = lax.Precision.HIGHEST
shampoo_rate = 0.25
momentum = 0.9

@jax.custom_vjp
def low(v):
    return lax.optimization_barrier(v.astype(jnp.bfloat16)).astype(jnp.float32)

@jax.custom_vjp
def low_back(v):
    return v

def low_keep(v):
    return (low(v), None)

def low_pass(kept, grad):
    return (grad,)

def back_keep(v):
    return (v, None)

def back_low(kept, grad):
    return (low(grad),)
low.defvjp(low_keep, low_pass)
low_back.defvjp(back_keep, back_low)

def product(form, left, right):
    return jnp.einsum(form, left, right, precision=precise)

def rms_norm(values):
    return values * lax.rsqrt(lax.optimization_barrier(jnp.mean(values * values, axis=-1, keepdims=True)) + epsilon)

def rope_tables():
    quarter = HEAD_DIM // 4
    freqs = 10000.0 ** (-jnp.arange(quarter, dtype=jnp.float32) / quarter)
    places = jnp.arange(PATCHES)
    coords = jnp.stack([places // GRID, places % GRID], axis=1).astype(jnp.float32)
    angles = coords[:, :, None] * freqs[None, None, :]
    return (jnp.cos(angles), jnp.sin(angles))

def rotate(values, cosine, sine):
    shape = values.shape
    halves = values.reshape(shape[:-1] + (2, 2, shape[-1] // 4))
    first_part = halves[..., 0, :]
    second_part = halves[..., 1, :]
    cosine = cosine[:, None]
    sine = sine[:, None]
    turned = jnp.stack([first_part * cosine - second_part * sine, second_part * cosine + first_part * sine], axis=-2)
    return turned.reshape(shape)

def matrices(master, owner):
    head_cols = D // N_TENSOR
    hidden_cols = FF // N_TENSOR
    widths = [6 * head_cols, 3 * head_cols, head_cols, hidden_cols, hidden_cols, hidden_cols]
    layout = master.reshape(D, N_TENSOR, FLAT_COLS)
    pieces = []
    offset = 0
    for index in range(6):
        segment = layout[:, :, offset:offset + widths[index]].reshape(N_DP, OWN_ROWS, N_TENSOR, widths[index])
        segment = jnp.roll(segment, -owner[index], axis=0).reshape(D, N_TENSOR, widths[index])
        pieces.append(low(segment))
        offset += widths[index]
    ada_w = pieces[0].reshape(D, N_TENSOR, 6, head_cols).transpose(0, 2, 1, 3).reshape(D, 6, D)
    qkv_w = pieces[1].reshape(D, N_TENSOR, 3, head_cols).transpose(0, 2, 1, 3).reshape(D, 3, D)
    proj_t = pieces[2].reshape(D, D)
    w_one = pieces[3].reshape(D, FF)
    w_three = pieces[4].reshape(D, FF)
    w_two = pieces[5].reshape(D, FF)
    return (ada_w, qkv_w, proj_t, w_one, w_three, w_two)

def forward(rows_all, cond, master, vec, owner):
    ada_w, qkv_w, proj_t, w_one, w_three, w_two = matrices(master, owner)
    bias = vec[:6 * D].reshape(6, D)
    gains = vec[6 * D:].reshape(2, HEAD_DIM)
    lifted = low(jax.nn.silu(cond))
    mod = product('gi,oji->gjo', lifted, ada_w) + bias
    cosine, sine = rope_tables()
    group = 16
    count = IMAGES // group
    scale_dot = HEAD_DIM ** (-0.5)
    inputs = rows_all.reshape(count, group, PATCHES, D)
    mods = mod.reshape(count, group, 6, D)

    def block(pair):
        rows_in, mod_block = pair
        shift_one, scale_one, gate_one, shift_two, scale_two, gate_two = [mod_block[:, j][:, None, :] for j in range(6)]
        normed_one = rms_norm(rows_in)
        lifted_one = low(normed_one * (1.0 + scale_one) + shift_one)
        qkv = low_back(product('gpi,ico->gpco', lifted_one, qkv_w))
        heads = qkv.reshape(group, PATCHES, 3, HEADS, HEAD_DIM)
        query = low(rotate(rms_norm(heads[:, :, 0]) * gains[0], cosine, sine))
        keys = low(rotate(rms_norm(heads[:, :, 1]) * gains[1], cosine, sine))
        values = low(heads[:, :, 2])
        scores = low_back(product('gphd,gqhd->ghpq', query, keys) * scale_dot)
        expo = jnp.exp(scores - lax.optimization_barrier(jnp.max(scores, axis=-1, keepdims=True)))
        probs = low(expo / lax.optimization_barrier(jnp.sum(expo, axis=-1, keepdims=True)))
        attended = low(low_back(product('ghpq,gqhd->gphd', probs, values))).reshape(group, PATCHES, D)
        branch_one = low_back(product('gpi,oi->gpo', attended, proj_t))
        middle = rows_in + gate_one * branch_one
        normed_two = rms_norm(middle)
        lifted_two = low(normed_two * (1.0 + scale_two) + shift_two)
        gate_pre = low_back(product('gpi,if->gpf', lifted_two, w_one))
        up_pre = low_back(product('gpi,if->gpf', lifted_two, w_three))
        hidden = low(jax.nn.silu(gate_pre) * up_pre)
        branch_two = low_back(product('gpf,of->gpo', hidden, w_two))
        return middle + gate_two * branch_two
    result = lax.map(jax.checkpoint(block), (inputs, mods))
    return result.reshape(TOKENS, D)

def reference(block_input, cotangent, master, left_stats, right_stats, left_roots, right_roots, vec, vec_mom, time_table, class_table, bucket, label, owner):
    cond = time_table[bucket] + class_table[label]

    def wrapped(rows_in, cond_in, master_in, vec_in):
        return forward(rows_in, cond_in, master_in, vec_in, owner)
    output, pullback = jax.vjp(wrapped, block_input, cond, master, vec)
    d_input, d_cond, grad, vec_grad = pullback(cotangent)
    pieces = grad.reshape(N_DP, OWN_ROWS, N_TENSOR, BLOCKS, BLOCK_WIDTH).transpose(0, 2, 3, 1, 4)
    pieces = pieces.reshape(N_DP, N_TENSOR * BLOCKS, OWN_ROWS, BLOCK_WIDTH)
    left_new = 0.5 * left_stats + 0.5 * product('abij,abkj->abik', pieces, pieces)
    right_new = 0.5 * right_stats + 0.5 * product('abji,abjk->abik', pieces, pieces)
    update = product('abik,abkl->abil', product('abij,abjk->abik', left_roots, pieces), right_roots)
    update = update.reshape(N_DP, N_TENSOR, BLOCKS, OWN_ROWS, BLOCK_WIDTH).transpose(0, 3, 1, 2, 4)
    update = update.reshape(D, N_TENSOR * FLAT_COLS)
    master_new = master - shampoo_rate * update
    mom_new = momentum * vec_mom + vec_grad
    vec_new = vec - 0.1 / TOKENS ** 0.5 * mom_new
    return (output, d_input, d_cond, grad, left_new, right_new, master_new, master_new.astype(jnp.bfloat16), vec_new, mom_new)
```

```python
import functools

import jax
import jax.numpy as jnp
from jax import lax
from jax.experimental import pallas as pl
from jax.experimental.pallas import tpu as pltpu
from jax.sharding import PartitionSpec as P

HEAD_DIM = 72
FF = 3072
PATCHES = 256
GRID = 16
BLOCK_WIDTH = 48
RING = (0, 1, 3, 5, 7, 6, 4, 2)

epsilon = 1e-06
precise = lax.Precision.HIGHEST
shampoo_rate = 0.25
momentum = 0.9
low = jnp.bfloat16
wide = jnp.float32


def rms_norm(values):
    return values * lax.rsqrt(jnp.mean(values * values, axis=-1, keepdims=True) + epsilon)


def norm_back(values, normed, upstream):
    factor = lax.rsqrt(jnp.mean(values * values, axis=-1, keepdims=True) + epsilon)
    return factor * (upstream - normed * jnp.mean(upstream * normed, axis=-1, keepdims=True))


def rope_tables():
    quarter = HEAD_DIM // 4
    freqs = 10000.0 ** (-jnp.arange(quarter, dtype=jnp.float32) / quarter)
    places = jnp.arange(PATCHES)
    coords = jnp.stack([places // GRID, places % GRID], axis=1).astype(jnp.float32)
    angles = coords[:, :, None] * freqs[None, None, :]
    return (jnp.cos(angles), jnp.sin(angles))


def rotate(values, cosine, sine):
    shape = values.shape
    halves = values.reshape(shape[:-1] + (2, 2, shape[-1] // 4))
    first_part = halves[..., 0, :]
    second_part = halves[..., 1, :]
    cosine = cosine[:, None]
    sine = sine[:, None]
    turned = jnp.stack(
        [first_part * cosine - second_part * sine, second_part * cosine + first_part * sine],
        axis=-2,
    )
    return turned.reshape(shape)


def roll_blocks(matrix, shift, groups):
    blocks = matrix.reshape((groups, matrix.shape[0] // groups) + matrix.shape[1:])
    return jnp.roll(blocks, shift, axis=0).reshape(matrix.shape)


def silu_slope(values):
    sigma = jax.nn.sigmoid(values)
    return sigma * (1.0 + values * (1.0 - sigma))


def ring_pairs(step):
    pairs = []
    for place, chip in enumerate(RING):
        goal = RING[(place + step) % len(RING)]
        pairs += [(chip * 2 + core, goal * 2 + core) for core in range(2)]
    return pairs


def around(value, step):
    return lax.ppermute(value, "dp", ring_pairs(step))


def across_cores(value):
    return lax.ppermute(value, "dp", [(i, i ^ 1) for i in range(2 * len(RING))])


def across_tensor(value):
    return lax.ppermute(value, "tensor", [(0, 1), (1, 0)])


def relative_order():
    rows = []
    for device in range(2 * len(RING)):
        place, core = RING.index(device // 2), device % 2
        chips = [RING[(place + offset) % len(RING)] for offset in range(len(RING))]
        rows.append([chip * 2 + core for chip in chips] + [chip * 2 + 1 - core for chip in chips])
    return jnp.array(rows, jnp.int32)


def ring_gather(shard):
    half = shard.shape[1] // 2
    pieces = [shard] + [None] * 7
    right, left = shard, shard
    for hop in range(1, 4):
        right, left = around(right, 1), around(left, -1)
        pieces[8 - hop], pieces[hop] = right, left
    pieces[4] = jnp.concatenate([around(right[:, :half], 1), around(left[:, half:], -1)], axis=1)
    own = jnp.stack(pieces)
    return own, across_cores(own)


def ring_scatter(own, other):
    half = own.shape[2] // 2
    partner = across_cores(other)

    def term(offset):
        return own[offset].astype(wide) + partner[offset].astype(wide)

    start = term(4).astype(low)
    right = around(start[:, :half], 1)
    left = around(start[:, half:], -1)
    third, fifth = term(3), term(5)
    right = jnp.concatenate([third[:, :half] + right.astype(wide), third[:, half:]], axis=1)
    left = jnp.concatenate([fifth[:, :half], fifth[:, half:] + left.astype(wide)], axis=1)
    for offset in (2, 1):
        right = around(right.astype(low), 1).astype(wide) + term(offset)
        left = around(left.astype(low), -1).astype(wide) + term(8 - offset)
    return term(0) + around(right.astype(low), 1).astype(wide) + around(left.astype(low), -1).astype(wide)


def assemble(own, other, table, widths):
    offsets, rows = own.shape[0], own.shape[1]
    total = own.shape[2]
    starts = [sum(widths[:i]) for i in range(len(widths))]

    def body(table_ref, own_ref, other_ref, *outs):
        def put(source):
            for out, start, width in zip(outs, starts, widths, strict=True):
                out[0] = source[0, :, start : start + width]

        step = pl.program_id(0)
        pl.when(step < offsets)(lambda: put(own_ref))
        pl.when(step >= offsets)(lambda: put(other_ref))

    def place(index):
        return lambda step, table: (table[index * 2 * offsets + step], 0, 0)

    outs = pl.pallas_call(
        body,
        grid_spec=pltpu.PrefetchScalarGridSpec(
            num_scalar_prefetch=1,
            grid=(2 * offsets,),
            in_specs=[
                pl.BlockSpec((1, rows, total), lambda step, table: (jnp.minimum(step, offsets - 1), 0, 0)),
                pl.BlockSpec((1, rows, total), lambda step, table: (jnp.maximum(step - offsets, 0), 0, 0)),
            ],
            out_specs=[pl.BlockSpec((1, rows, width), place(i)) for i, width in enumerate(widths)],
        ),
        out_shape=[jax.ShapeDtypeStruct((2 * offsets, rows, width), own.dtype) for width in widths],
        cost_estimate=pl.CostEstimate(flops=0, transcendentals=0, bytes_accessed=4 * own.size * 2),
        name="assemble",
    )(table.reshape(-1), own, other)
    return [out.reshape(2 * offsets * rows, width) for out, width in zip(outs, widths, strict=True)]


def pick(matrices, table, first):
    blocks = table.shape[1]
    offsets = blocks // 2
    rows = matrices[0].shape[0] // blocks
    widths = [matrix.shape[1] for matrix in matrices]
    starts = [sum(widths[:i]) for i in range(len(widths))]
    total = sum(widths)

    def body(table_ref, *refs):
        for ref, start, width in zip(refs[:-1], starts, widths, strict=True):
            refs[-1][0, :, start : start + width] = ref[0]

    def place(index):
        return lambda step, table: (table[index * blocks + first + step], 0, 0)

    return pl.pallas_call(
        body,
        grid_spec=pltpu.PrefetchScalarGridSpec(
            num_scalar_prefetch=1,
            grid=(offsets,),
            in_specs=[pl.BlockSpec((1, rows, width), place(i)) for i, width in enumerate(widths)],
            out_specs=pl.BlockSpec((1, rows, total), lambda step, table: (step, 0, 0)),
        ),
        out_shape=jax.ShapeDtypeStruct((offsets, rows, total), matrices[0].dtype),
        cost_estimate=pl.CostEstimate(flops=0, transcendentals=0, bytes_accessed=4 * offsets * rows * total),
        name="pick",
    )(table.reshape(-1), *[matrix.reshape(blocks, rows, matrix.shape[1]) for matrix in matrices])


def local(
    block_input,
    cotangent,
    master,
    left_stats,
    right_stats,
    left_roots,
    right_roots,
    vec,
    vec_mom,
    time_table,
    class_table,
    bucket,
    label,
    owner,
):
    tensor_size = lax.axis_size("tensor")
    data_size = lax.axis_size("dp")
    rings = tensor_size == 2 and data_size == 2 * len(RING)
    tensor_index = lax.axis_index("tensor")
    data_index = lax.axis_index("dp")
    row_count, width = block_input.shape
    own_rows = master.shape[0]
    head_cols = width // tensor_size
    local_heads = head_cols // HEAD_DIM
    hidden_cols = FF // tensor_size
    group_images = row_count // PATCHES * tensor_size
    images_all = group_images * data_size
    scale_dot = HEAD_DIM ** (-0.5)
    widths = [6 * head_cols, 3 * head_cols, head_cols, hidden_cols, hidden_cols, hidden_cols]
    bounds = [0]
    for piece_width in widths:
        bounds.append(bounds[-1] + piece_width)
    devices = ("dp", "tensor")

    if rings:
        order = lax.dynamic_index_in_dim(relative_order(), data_index, 0, keepdims=False)
        tables = (order[None, :] - owner[:, None]) % data_size

        def weights(first, last):
            own, other = ring_gather(master[:, bounds[first] : bounds[last]].astype(low))
            return assemble(own, other, tables[first:last], widths[first:last])

        def to_owners(grads, first):
            table = tables[first : first + len(grads)]
            return ring_scatter(pick(grads, table, 0), pick(grads, table, len(RING)))

        def spread(rows):
            return [rows, across_tensor(rows)]

        def gathered_sum(parts):
            return parts[0] + across_tensor(parts[1].astype(low)).astype(wide)
    else:

        def weights(first, last):
            own = master[:, bounds[first] : bounds[last]].astype(low)
            gathered = lax.all_gather(own, "dp", axis=0, tiled=True)
            natural, at = [], 0
            for index in range(first, last):
                piece = gathered[:, at : at + widths[index]]
                natural.append(roll_blocks(piece, -owner[index], data_size))
                at += widths[index]
            return natural

        def to_owners(grads, first):
            flat = [roll_blocks(grad, owner[first + i], data_size) for i, grad in enumerate(grads)]
            flat = jnp.concatenate(flat, axis=1)
            return lax.psum_scatter(flat, "dp", scatter_dimension=0, tiled=True).astype(wide)

        def spread(rows):
            return [lax.all_gather(rows, "tensor", axis=0, tiled=True)]

        def gathered_sum(parts):
            summed = lax.psum_scatter(
                parts[0].astype(low), "tensor", scatter_dimension=0, tiled=True
            )
            return summed.astype(wide)

    n_own = rms_norm(block_input)
    if rings:
        n_low = n_own.astype(low)
        n_partner = across_tensor(n_low)
    marks = lax.all_gather(jnp.stack([bucket, label], axis=1), "dp", axis=0, tiled=True)
    cond = time_table[marks[:, 0]] + class_table[marks[:, 1]]
    cond = lax.dynamic_slice_in_dim(cond, tensor_index * head_cols, head_cols, 1)
    lifted = jax.nn.silu(cond).astype(low)
    ada = master[:, : bounds[1]].astype(low)
    row_map = lax.broadcasted_iota(jnp.int32, (6 * images_all, 6 * head_cols), 0) // images_all
    col_map = lax.broadcasted_iota(jnp.int32, (6 * images_all, 6 * head_cols), 1) // head_cols
    on_map = row_map == col_map
    lifted_maps = jnp.where(on_map, jnp.tile(lifted, (6, 6)), jnp.zeros((), low))
    partial_mod = lax.dot_general(
        lifted_maps, ada, (((1,), (1,)), ((), ())), preferred_element_type=wide
    )
    send = partial_mod.reshape(6, data_size, group_images, own_rows).transpose(1, 0, 2, 3)
    send = jnp.broadcast_to(send[:, None], (data_size, tensor_size) + send.shape[1:])
    send = send.reshape((data_size * tensor_size,) + send.shape[2:])
    got = lax.all_to_all(send, devices, 0, 0, tiled=True)
    got = got.reshape((data_size, tensor_size) + got.shape[1:]).sum(axis=1)
    got = jnp.roll(got, -owner[0], axis=0).transpose(2, 1, 0, 3)
    mods = got.reshape(group_images, 6, width) + vec[: 6 * width].reshape(6, width)

    mod = lax.dynamic_index_in_dim(mods, tensor_index, 0, keepdims=False)
    shift_one, scale_one, gate_one, shift_two, scale_two, gate_two = [
        mod[index][None, :] for index in range(6)
    ]
    gains = vec[6 * width :].reshape(2, HEAD_DIM)

    qkv_cols, proj_cols = weights(1, 3)
    w_one, w_three, w_two = weights(3, 6)

    h_one = (n_own * (1.0 + scale_one) + shift_one).astype(low)
    if rings:
        mod_partner = lax.dynamic_index_in_dim(mods, 1 - tensor_index, 0, keepdims=False)
        h_partner = n_partner.astype(wide) * (1.0 + mod_partner[1][None]) + mod_partner[0][None]
        rows_one = [h_one, h_partner.astype(low)]
    else:
        rows_one = spread(h_one)
    send_two = (gate_two * cotangent).astype(low)
    back_two = spread(send_two)

    cosine, sine = rope_tables()
    kept = []
    branch_parts = []
    for rows in rows_one:
        raw = jnp.dot(rows, qkv_cols, preferred_element_type=wide)
        raw = raw.reshape(rows.shape[0] // PATCHES, PATCHES, 3, local_heads, HEAD_DIM)
        query_norm = rms_norm(raw[:, :, 0])
        key_norm = rms_norm(raw[:, :, 1])
        query = rotate(query_norm * gains[0], cosine, sine).astype(low)
        keys = rotate(key_norm * gains[1], cosine, sine).astype(low)
        values = raw[:, :, 2].astype(low)
        scores = jnp.einsum("gphd,gqhd->ghpq", query, keys, preferred_element_type=wide) * scale_dot
        peak = jnp.max(scores, axis=-1, keepdims=True)
        expo = jnp.exp(scores - peak)
        total = jnp.sum(expo, axis=-1, keepdims=True)
        logsum = peak + jnp.log(total)
        probs = (expo / total).astype(low)
        attended = jnp.einsum("ghpq,gqhd->gphd", probs, values, preferred_element_type=wide)
        attended = attended.astype(low).reshape(rows.shape[0], head_cols)
        kept.append((raw, query_norm, key_norm, query, keys, values, logsum, attended))
        branch_parts.append(
            jnp.einsum("rh,oh->ro", attended, proj_cols, preferred_element_type=wide)
        )
    branch_one = gathered_sum(branch_parts)
    middle = block_input + gate_one * branch_one
    n_two = rms_norm(middle)
    h_two = (n_two * (1.0 + scale_two) + shift_two).astype(low)
    rows_two = spread(h_two)

    branch_parts, hidden_parts, gate_parts, up_parts, d_parts = [], [], [], [], []
    for rows, back in zip(rows_two, back_two, strict=True):
        gate_pre = jnp.dot(rows, w_one, preferred_element_type=wide)
        up_pre = jnp.dot(rows, w_three, preferred_element_type=wide)
        d_hidden = jnp.dot(back, w_two, preferred_element_type=wide)
        sigma = jax.nn.sigmoid(gate_pre)
        silu_gate = gate_pre * sigma
        hidden = (silu_gate * up_pre).astype(low)
        d_gate_pre = (d_hidden * up_pre * sigma * (1.0 + gate_pre * (1.0 - sigma))).astype(low)
        d_up_pre = (d_hidden * silu_gate).astype(low)
        hidden_parts.append(hidden)
        gate_parts.append(d_gate_pre)
        up_parts.append(d_up_pre)
        d_parts.append(
            jnp.einsum("rf,df->rd", d_gate_pre, w_one, preferred_element_type=wide)
            + jnp.einsum("rf,df->rd", d_up_pre, w_three, preferred_element_type=wide)
        )
        branch_parts.append(
            jnp.einsum("rf,of->ro", hidden, w_two, preferred_element_type=wide)
        )

    def grad_of(lefts, rights):
        left, right = jnp.concatenate(lefts, axis=0), jnp.concatenate(rights, axis=0)
        grad = lax.dot_general(left, right, (((0,), (0,)), ((), ())), preferred_element_type=wide)
        return grad.astype(low)

    grad_mlp = to_owners(
        [
            grad_of(rows_two, gate_parts),
            grad_of(rows_two, up_parts),
            grad_of(back_two, hidden_parts),
        ],
        3,
    )
    d_h_two = gathered_sum(d_parts)
    branch_two = gathered_sum(branch_parts)
    output = middle + gate_two * branch_two
    d_gate_two = jnp.sum(cotangent * branch_two, axis=0)
    d_shift_two = jnp.sum(d_h_two, axis=0)
    d_scale_two = jnp.sum(d_h_two * n_two, axis=0)
    d_middle = cotangent + norm_back(middle, n_two, d_h_two * (1.0 + scale_two))
    d_gate_one = jnp.sum(d_middle * branch_one, axis=0)
    send_one = (gate_one * d_middle).astype(low)
    back_one = spread(send_one)

    d_parts, raw_parts = [], []
    gain_grads = jnp.zeros((2, HEAD_DIM), wide)
    for back, saved in zip(back_one, kept, strict=True):
        raw, query_norm, key_norm, query, keys, values, logsum, attended = saved
        d_attended = jnp.dot(back, proj_cols, preferred_element_type=wide).astype(low)
        d_attended = d_attended.reshape(values.shape)
        scores = jnp.einsum("gphd,gqhd->ghpq", query, keys, preferred_element_type=wide) * scale_dot
        probs_full = jnp.exp(scores - logsum)
        d_values = jnp.einsum(
            "ghpq,gphd->gqhd", probs_full.astype(low), d_attended, preferred_element_type=wide
        )
        d_probs = jnp.einsum("gphd,gqhd->ghpq", d_attended, values, preferred_element_type=wide)
        d_scores = probs_full * (d_probs - jnp.sum(probs_full * d_probs, axis=-1, keepdims=True))
        d_scores = d_scores.astype(low)
        d_query = (
            jnp.einsum("ghpq,gqhd->gphd", d_scores, keys, preferred_element_type=wide) * scale_dot
        )
        d_keys = (
            jnp.einsum("ghpq,gphd->gqhd", d_scores, query, preferred_element_type=wide) * scale_dot
        )
        d_query_norm = rotate(d_query, cosine, -sine)
        d_key_norm = rotate(d_keys, cosine, -sine)
        gain_grads += jnp.stack(
            [
                jnp.sum(d_query_norm * query_norm, axis=(0, 1, 2)),
                jnp.sum(d_key_norm * key_norm, axis=(0, 1, 2)),
            ]
        )
        d_raw_query = norm_back(raw[:, :, 0], query_norm, d_query_norm * gains[0])
        d_raw_key = norm_back(raw[:, :, 1], key_norm, d_key_norm * gains[1])
        d_raw = jnp.stack([d_raw_query, d_raw_key, d_values], axis=2).astype(low)
        d_raw = d_raw.reshape(back.shape[0], 3 * head_cols)
        raw_parts.append(d_raw)
        d_parts.append(jnp.einsum("rc,dc->rd", d_raw, qkv_cols, preferred_element_type=wide))
    grad_att = to_owners(
        [grad_of(rows_one, raw_parts), grad_of(back_one, [saved[-1] for saved in kept])], 1
    )
    d_h_one = gathered_sum(d_parts)
    d_shift_one = jnp.sum(d_h_one, axis=0)
    d_scale_one = jnp.sum(d_h_one * n_own, axis=0)
    d_inputs = d_middle + norm_back(block_input, n_own, d_h_one * (1.0 + scale_one))

    d_mod = jnp.stack([d_shift_one, d_scale_one, d_gate_one, d_shift_two, d_scale_two, d_gate_two])
    d_mod = d_mod.reshape(6, data_size, own_rows).transpose(1, 0, 2)
    d_mod = jnp.roll(d_mod, owner[0], axis=0).reshape(data_size, 6 * own_rows)
    gain_row = jnp.broadcast_to(gain_grads.reshape(1, -1), (data_size, 2 * HEAD_DIM))
    send = jnp.concatenate([d_mod, gain_row], axis=1)
    send = jnp.broadcast_to(send[:, None], (data_size, tensor_size, send.shape[1]))
    send = send.reshape(data_size * tensor_size, send.shape[2])
    got = lax.all_to_all(send, devices, 0, 0, tiled=True)
    gain_sum = jnp.sum(got[:, 6 * own_rows :], axis=0)
    d_own = got[:, : 6 * own_rows].reshape(images_all, 6, own_rows).transpose(1, 0, 2)
    row_sum = jnp.sum(d_own, axis=1).reshape(-1)
    d_own = d_own.reshape(6 * images_all, own_rows)
    grad_ada = lax.dot_general(
        d_own,
        lifted_maps.astype(wide),
        (((0,), (0,)), ((), ())),
        precision=precise,
        preferred_element_type=wide,
    )
    d_lifted = lax.dot_general(
        d_own,
        ada.astype(wide),
        (((1,), (0,)), ((), ())),
        precision=precise,
        preferred_element_type=wide,
    )
    d_lifted = jnp.where(on_map, d_lifted, 0.0).reshape(6, images_all, 6 * head_cols).sum(axis=0)
    d_lifted = sum(d_lifted[:, j * head_cols : (j + 1) * head_cols] for j in range(6))
    send = jnp.concatenate(
        [
            d_lifted.reshape(data_size, group_images * head_cols),
            jnp.broadcast_to(row_sum[None, :], (data_size, 6 * own_rows)),
        ],
        axis=1,
    )
    got = lax.all_to_all(send, "dp", 0, 0, tiled=True)
    d_lifted = jnp.sum(got[:, : group_images * head_cols], axis=0).reshape(group_images, head_cols)
    cond_here = lax.dynamic_slice_in_dim(cond, data_index * group_images, group_images, 0)
    d_cond = d_lifted * silu_slope(cond_here)
    vec_rows = got[:, group_images * head_cols :].reshape(data_size, 6, own_rows)
    vec_rows = jnp.roll(vec_rows, -owner[0], axis=0).transpose(1, 0, 2).reshape(-1)
    vec_grad = jnp.concatenate([vec_rows, gain_sum])

    grad_mine = jnp.concatenate([grad_ada, grad_att, grad_mlp], axis=1)
    block_count = grad_mine.shape[1] // BLOCK_WIDTH
    pieces = grad_mine.astype(low).reshape(own_rows, block_count, BLOCK_WIDTH).transpose(1, 0, 2)
    left_new = 0.5 * left_stats[0] + 0.5 * jnp.einsum(
        "bij,bkj->bik", pieces, pieces, preferred_element_type=wide
    )
    right_new = 0.5 * right_stats[0] + 0.5 * jnp.einsum(
        "bji,bjk->bik", pieces, pieces, preferred_element_type=wide
    )
    update = jnp.einsum(
        "bij,bjk->bik", left_roots[0].astype(low), pieces, preferred_element_type=wide
    )
    update = jnp.einsum(
        "bik,bkl->bil",
        update.astype(low),
        right_roots[0].astype(low),
        preferred_element_type=wide,
    )
    update = update.transpose(1, 0, 2).reshape(own_rows, block_count * BLOCK_WIDTH)
    master_new = master - shampoo_rate * update
    tokens_all = row_count * data_size * tensor_size
    mom_new = momentum * vec_mom + vec_grad
    vec_new = vec - 0.1 / tokens_all**0.5 * mom_new
    return (
        output,
        d_inputs,
        d_cond,
        grad_mine,
        left_new[None],
        right_new[None],
        master_new,
        master_new.astype(low),
        vec_new,
        mom_new,
    )


def solution(mesh):
    placed = (
        P(("dp", "tensor"), None),
        P(("dp", "tensor"), None),
        P("dp", "tensor"),
        P("dp", "tensor", None, None),
        P("dp", "tensor", None, None),
        P("dp", "tensor", None, None),
        P("dp", "tensor", None, None),
        P(),
        P(),
        P(),
        P(),
        P("dp"),
        P("dp"),
        P(),
    )
    return jax.shard_map(
        local,
        mesh=mesh,
        in_specs=placed,
        out_specs=(
            P(("dp", "tensor"), None),
            P(("dp", "tensor"), None),
            P("dp", "tensor"),
            P("dp", "tensor"),
            P("dp", "tensor", None, None),
            P("dp", "tensor", None, None),
            P("dp", "tensor"),
            P("dp", "tensor"),
            P(),
            P(),
        ),
        check_vma=False,
    )
```

```python
import functools

import jax
import jax.numpy as jnp
from jax import lax
from jax.experimental import pallas as pl
from jax.experimental.pallas import tpu as pltpu
from jax.sharding import PartitionSpec as P

HEAD_DIM = 72
FF = 3072
PATCHES = 256
GRID = 16
BLOCK_WIDTH = 48
RING = (0, 1, 3, 5, 7, 6, 4, 2)

epsilon = 1e-06
precise = lax.Precision.HIGHEST
shampoo_rate = 0.25
momentum = 0.9
low = jnp.bfloat16
wide = jnp.float32


def rms_norm(values):
    return values * lax.rsqrt(jnp.mean(values * values, axis=-1, keepdims=True) + epsilon)


def norm_back(values, normed, upstream):
    factor = lax.rsqrt(jnp.mean(values * values, axis=-1, keepdims=True) + epsilon)
    return factor * (upstream - normed * jnp.mean(upstream * normed, axis=-1, keepdims=True))


def rope_tables():
    quarter = HEAD_DIM // 4
    freqs = 10000.0 ** (-jnp.arange(quarter, dtype=jnp.float32) / quarter)
    places = jnp.arange(PATCHES)
    coords = jnp.stack([places // GRID, places % GRID], axis=1).astype(jnp.float32)
    angles = coords[:, :, None] * freqs[None, None, :]
    return (jnp.cos(angles), jnp.sin(angles))


def rotate(values, cosine, sine):
    shape = values.shape
    halves = values.reshape(shape[:-1] + (2, 2, shape[-1] // 4))
    first_part = halves[..., 0, :]
    second_part = halves[..., 1, :]
    cosine = cosine[:, None]
    sine = sine[:, None]
    turned = jnp.stack(
        [first_part * cosine - second_part * sine, second_part * cosine + first_part * sine],
        axis=-2,
    )
    return turned.reshape(shape)


def roll_blocks(matrix, shift, groups):
    blocks = matrix.reshape((groups, matrix.shape[0] // groups) + matrix.shape[1:])
    return jnp.roll(blocks, shift, axis=0).reshape(matrix.shape)


def silu_slope(values):
    sigma = jax.nn.sigmoid(values)
    return sigma * (1.0 + values * (1.0 - sigma))


def ring_pairs(step):
    pairs = []
    for place, chip in enumerate(RING):
        goal = RING[(place + step) % len(RING)]
        pairs += [(chip * 2 + core, goal * 2 + core) for core in range(2)]
    return pairs


def around(value, step):
    return lax.ppermute(value, "dp", ring_pairs(step))


def across_cores(value):
    return lax.ppermute(value, "dp", [(i, i ^ 1) for i in range(2 * len(RING))])


def across_tensor(value):
    return lax.ppermute(value, "tensor", [(0, 1), (1, 0)])


def relative_order():
    rows = []
    for device in range(2 * len(RING)):
        place, core = RING.index(device // 2), device % 2
        chips = [RING[(place + offset) % len(RING)] for offset in range(len(RING))]
        rows.append([chip * 2 + core for chip in chips] + [chip * 2 + 1 - core for chip in chips])
    return jnp.array(rows, jnp.int32)


def after(value, *others):
    return lax.optimization_barrier((value, others))[0]


class RingGather:
    def __init__(self, shard):
        self.half = shard.shape[1] // 2
        self.right = self.left = shard
        self.hops = 0
        self.pieces = []
        self.keep(0, 0, shard)

    def keep(self, offset, start, piece):
        self.pieces.append((offset, start, piece))
        self.pieces.append((offset + len(RING), start, across_cores(piece)))

    def hop(self, *ready):
        self.hops += 1
        if self.hops < 4:
            self.right = around(after(self.right, *ready), 1)
            self.left = around(after(self.left, *ready), -1)
            self.keep(8 - self.hops, 0, self.right)
            self.keep(self.hops, 0, self.left)
        else:
            self.right = around(after(self.right[:, : self.half], *ready), 1)
            self.left = around(after(self.left[:, self.half :], *ready), -1)
            self.keep(4, 0, self.right)
            self.keep(4, self.half, self.left)
        return self.right, self.left


class RingScatter:
    def __init__(self, own, other):
        self.own = own
        self.half = own.shape[2] // 2
        self.partner = across_cores(other)
        self.hops = 0

    def term(self, offset):
        return self.own[offset].astype(wide) + self.partner[offset].astype(wide)

    def hop(self, *ready):
        half = self.half
        if self.hops == 0:
            start = self.term(4).astype(low)
            right, left = start[:, :half], start[:, half:]
        else:
            mine, other = self.term(4 - self.hops), self.term(4 + self.hops)
            right, left = self.right.astype(wide), self.left.astype(wide)
            if self.hops == 1:
                right = jnp.concatenate([mine[:, :half] + right, mine[:, half:]], axis=1)
                left = jnp.concatenate([other[:, :half], other[:, half:] + left], axis=1)
            else:
                right, left = right + mine, left + other
            right, left = right.astype(low), left.astype(low)
        self.hops += 1
        self.right = around(after(right, *ready), 1)
        self.left = around(after(left, *ready), -1)
        return self.right, self.left

    def total(self):
        return self.term(0) + self.right.astype(wide) + self.left.astype(wide)


def assemble(pieces, table, first, widths, blocks):
    rows = pieces[0][2].shape[0]
    starts = [sum(widths[:i]) for i in range(len(widths))]

    def body(table_ref, *refs):
        outs = refs[len(pieces) :]
        for (place, at, _), ref in zip(pieces, refs, strict=False):
            for index, (out, start, width) in enumerate(zip(outs, starts, widths, strict=True)):
                low_end = max(start, at)
                high_end = min(start + width, at + ref.shape[1])
                if low_end < high_end:
                    goal = table_ref[(first + index) * blocks + place]
                    out[goal, :, low_end - start : high_end - start] = ref[
                        :, low_end - at : high_end - at
                    ]

    whole = pl.BlockSpec(memory_space=pltpu.VMEM)
    outs = pl.pallas_call(
        body,
        in_specs=[pl.BlockSpec(memory_space=pltpu.SMEM)] + [whole for _ in pieces],
        out_specs=[whole for _ in widths],
        out_shape=[jax.ShapeDtypeStruct((blocks, rows, width), low) for width in widths],
        cost_estimate=pl.CostEstimate(
            flops=0, transcendentals=0, bytes_accessed=4 * blocks * rows * sum(widths)
        ),
        name="assemble",
    )(table, *[piece for _, _, piece in pieces])
    return [out.reshape(blocks * rows, width) for out, width in zip(outs, widths, strict=True)]


def turn(parts, flat_ref):
    at = 0
    for part in parts:
        flat_ref[:, at : at + part.shape[0]] = part[...].astype(wide).T
        at += part.shape[0]


def sort_rows(flat_ref, left_ref, table_ref, base, rows):
    for place in range(left_ref.shape[0] // rows):
        source = pl.multiple_of(table_ref[base + place] * rows, 8)
        left_ref[place * rows : (place + 1) * rows, :] = flat_ref[pl.ds(source, rows), :].astype(low)


def product_rows(left, rights, at, columns):
    total, start = None, 0
    for right in rights:
        piece = right[:, at : at + columns]
        term = jnp.dot(
            left[:, start : start + right.shape[0]], piece, preferred_element_type=wide
        )
        total = term if total is None else total + term
        start += right.shape[0]
    return total


def grads_mlp(rows_two, back_two, gates, ups, hiddens, table, blocks):
    count, width = rows_two[0].shape
    rows, cols = width // blocks, gates[0].shape[1]
    tile = 512
    steps = cols // tile

    def body(table_ref, h0, h1, b0, b1, g0, g1, u0, u1, v0, v1, own_ref, other_ref, flat, left):
        step = pl.program_id(0)

        @pl.when(step == 0)
        def _():
            turn((h0, h1), flat)
            sort_rows(flat, left, table_ref, 3 * blocks, rows)

        @pl.when(step == steps)
        def _():
            sort_rows(flat, left, table_ref, 4 * blocks, rows)

        @pl.when(step == 2 * steps)
        def _():
            turn((b0, b1), flat)
            sort_rows(flat, left, table_ref, 5 * blocks, rows)

        def work(rights):
            for side, out in enumerate((own_ref, other_ref)):
                half = left[side * (width // 2) : (side + 1) * (width // 2), :]
                total = product_rows(half, rights, 0, tile)
                out[...] = total.reshape(blocks // 2, rows, tile).astype(low)

        pl.when(step < steps)(lambda: work((g0, g1)))
        pl.when((step >= steps) & (step < 2 * steps))(lambda: work((u0, u1)))
        pl.when(step >= 2 * steps)(lambda: work((v0, v1)))

    def part_spec(first):
        return pl.BlockSpec(
            (count, tile), lambda step, table: (0, jnp.clip(step - first, 0, steps - 1))
        )

    whole = pl.BlockSpec((count, width), lambda step, table: (0, 0))
    out_spec = pl.BlockSpec((blocks // 2, rows, tile), lambda step, table: (0, 0, step))
    out = jax.ShapeDtypeStruct((blocks // 2, rows, 3 * cols), low)
    return pl.pallas_call(
        body,
        grid_spec=pltpu.PrefetchScalarGridSpec(
            num_scalar_prefetch=1,
            grid=(3 * steps,),
            in_specs=[whole] * 4
            + [part_spec(0)] * 2
            + [part_spec(steps)] * 2
            + [part_spec(2 * steps)] * 2,
            out_specs=[out_spec, out_spec],
            scratch_shapes=[
                pltpu.VMEM((width, 2 * count), wide),
                pltpu.VMEM((width, 2 * count), low),
            ],
        ),
        out_shape=[out, out],
        cost_estimate=pl.CostEstimate(
            flops=2 * 3 * 2 * count * width * cols,
            transcendentals=0,
            bytes_accessed=2 * (4 * count * width + 6 * count * cols + 3 * width * cols),
        ),
        name="grads_mlp",
    )(table, *rows_two, *back_two, *gates, *ups, *hiddens)


def grads_att(rows_one, back_one, raws, attendeds, table, blocks):
    count, width = rows_one[0].shape
    rows, cols = width // blocks, attendeds[0].shape[1]

    def body(table_ref, h0, h1, b0, b1, r0, r1, a0, a1, own_ref, other_ref, flat, left):
        def work(rights, at, goal):
            for side, out in enumerate((own_ref, other_ref)):
                half = left[side * (width // 2) : (side + 1) * (width // 2), :]
                total = product_rows(half, rights, at, cols)
                out[:, :, goal : goal + cols] = total.reshape(blocks // 2, rows, cols).astype(low)

        turn((h0, h1), flat)
        sort_rows(flat, left, table_ref, blocks, rows)
        for third in range(3):
            work((r0, r1), third * cols, third * cols)
        turn((b0, b1), flat)
        sort_rows(flat, left, table_ref, 2 * blocks, rows)
        work((a0, a1), 0, 3 * cols)

    whole = pl.BlockSpec(memory_space=pltpu.VMEM)
    out = jax.ShapeDtypeStruct((blocks // 2, rows, 4 * cols), low)
    return pl.pallas_call(
        body,
        in_specs=[pl.BlockSpec(memory_space=pltpu.SMEM)] + [whole] * 8,
        out_specs=[whole, whole],
        out_shape=[out, out],
        scratch_shapes=[
            pltpu.VMEM((width, 2 * count), wide),
            pltpu.VMEM((width, 2 * count), low),
        ],
        cost_estimate=pl.CostEstimate(
            flops=2 * 4 * 2 * count * width * cols,
            transcendentals=0,
            bytes_accessed=2 * (4 * count * width + 8 * count * cols + 4 * width * cols),
        ),
        name="grads_att",
    )(table, *rows_one, *back_one, *raws, *attendeds)


def local(
    block_input,
    cotangent,
    master,
    left_stats,
    right_stats,
    left_roots,
    right_roots,
    vec,
    vec_mom,
    time_table,
    class_table,
    bucket,
    label,
    owner,
):
    tensor_size = lax.axis_size("tensor")
    data_size = lax.axis_size("dp")
    rings = tensor_size == 2 and data_size == 2 * len(RING)
    tensor_index = lax.axis_index("tensor")
    data_index = lax.axis_index("dp")
    row_count, width = block_input.shape
    own_rows = master.shape[0]
    head_cols = width // tensor_size
    local_heads = head_cols // HEAD_DIM
    hidden_cols = FF // tensor_size
    group_images = row_count // PATCHES * tensor_size
    images_all = group_images * data_size
    scale_dot = HEAD_DIM ** (-0.5)
    widths = [6 * head_cols, 3 * head_cols, head_cols, hidden_cols, hidden_cols, hidden_cols]
    bounds = [0]
    for piece_width in widths:
        bounds.append(bounds[-1] + piece_width)
    devices = ("dp", "tensor")

    if rings:
        order = lax.dynamic_index_in_dim(relative_order(), data_index, 0, keepdims=False)
        table = ((order[None, :] - owner[:, None]) % data_size).reshape(-1)

        def ring_of(first, last, *ready):
            return RingGather(after(master[:, bounds[first] : bounds[last]].astype(low), *ready))

        def matrices(ring, first, last):
            return assemble(ring.pieces, table, first, widths[first:last], data_size)

        def spread(rows):
            return [rows, across_tensor(rows)]

        def gathered_sum(parts):
            return parts[0] + across_tensor(parts[1].astype(low)).astype(wide)
    else:

        def weights(first, last):
            own = master[:, bounds[first] : bounds[last]].astype(low)
            gathered = lax.all_gather(own, "dp", axis=0, tiled=True)
            natural, at = [], 0
            for index in range(first, last):
                piece = gathered[:, at : at + widths[index]]
                natural.append(roll_blocks(piece, -owner[index], data_size))
                at += widths[index]
            return natural

        def to_owners(pairs, first):
            grads = [
                lax.dot_general(
                    left[0], right[0], (((0,), (0,)), ((), ())), preferred_element_type=wide
                ).astype(low)
                for left, right in pairs
            ]
            flat = [roll_blocks(grad, owner[first + i], data_size) for i, grad in enumerate(grads)]
            flat = jnp.concatenate(flat, axis=1)
            return lax.psum_scatter(flat, "dp", scatter_dimension=0, tiled=True).astype(wide)

        def spread(rows):
            return [lax.all_gather(rows, "tensor", axis=0, tiled=True)]

        def gathered_sum(parts):
            summed = lax.psum_scatter(
                parts[0].astype(low), "tensor", scatter_dimension=0, tiled=True
            )
            return summed.astype(wide)

    n_own = rms_norm(block_input)
    if rings:
        n_low = n_own.astype(low)
        n_partner = across_tensor(n_low)
    marks = jnp.stack([bucket, label], axis=1)
    marks = jnp.broadcast_to(marks[None], (data_size,) + marks.shape)
    marks = lax.all_to_all(marks, "dp", 0, 0, tiled=True).reshape(images_all, 2)
    if rings:
        ring = ring_of(1, 3, marks)
        hop = ring.hop()
    cond = time_table[marks[:, 0]] + class_table[marks[:, 1]]
    cond = lax.dynamic_slice_in_dim(cond, tensor_index * head_cols, head_cols, 1)
    lifted = jax.nn.silu(cond).astype(low)
    ada = master[:, : bounds[1]].astype(low)
    row_map = lax.broadcasted_iota(jnp.int32, (6 * images_all, 6 * head_cols), 0) // images_all
    col_map = lax.broadcasted_iota(jnp.int32, (6 * images_all, 6 * head_cols), 1) // head_cols
    on_map = row_map == col_map
    lifted_maps = jnp.where(on_map, jnp.tile(lifted, (6, 6)), jnp.zeros((), low))
    partial_mod = lax.dot_general(
        lifted_maps, ada, (((1,), (1,)), ((), ())), preferred_element_type=wide
    )
    send = partial_mod.reshape(6, data_size, group_images, own_rows).transpose(1, 0, 2, 3)
    send = jnp.broadcast_to(send[:, None], (data_size, tensor_size) + send.shape[1:])
    send = send.reshape((data_size * tensor_size,) + send.shape[2:])
    if rings:
        send = after(send, hop)
        hop = ring.hop()
    got = lax.all_to_all(send, devices, 0, 0, tiled=True)
    if rings:
        got = after(got, hop)
        ring.hop()
    got = got.reshape((data_size, tensor_size) + got.shape[1:]).sum(axis=1)
    got = jnp.roll(got, -owner[0], axis=0).transpose(2, 1, 0, 3)
    mods = got.reshape(group_images, 6, width) + vec[: 6 * width].reshape(6, width)

    mod = lax.dynamic_index_in_dim(mods, tensor_index, 0, keepdims=False)
    shift_one, scale_one, gate_one, shift_two, scale_two, gate_two = [
        mod[index][None, :] for index in range(6)
    ]
    gains = vec[6 * width :].reshape(2, HEAD_DIM)

    h_one = (n_own * (1.0 + scale_one) + shift_one).astype(low)
    if rings:
        mod_partner = lax.dynamic_index_in_dim(mods, 1 - tensor_index, 0, keepdims=False)
        h_partner = n_partner.astype(wide) * (1.0 + mod_partner[1][None]) + mod_partner[0][None]
        rows_one = [h_one, h_partner.astype(low)]
        hop = ring.hop(rows_one[0])
        qkv_cols, proj_cols = matrices(ring, 1, 3)
        ring = ring_of(3, 6, hop)
        hop = ring.hop()
    else:
        rows_one = spread(h_one)
        qkv_cols, proj_cols = weights(1, 3)
        w_one, w_three, w_two = weights(3, 6)
    send_two = (gate_two * cotangent).astype(low)
    back_two = spread(send_two)

    cosine, sine = rope_tables()
    kept = []
    branch_parts = []
    for part, rows in enumerate(rows_one):
        if rings and part == 1:
            rows = after(rows, hop)
            hop = ring.hop(kept[0][0])
        raw = jnp.dot(rows, qkv_cols, preferred_element_type=wide)
        raw = raw.reshape(rows.shape[0] // PATCHES, PATCHES, 3, local_heads, HEAD_DIM)
        query_norm = rms_norm(raw[:, :, 0])
        key_norm = rms_norm(raw[:, :, 1])
        query = rotate(query_norm * gains[0], cosine, sine).astype(low)
        keys = rotate(key_norm * gains[1], cosine, sine).astype(low)
        values = raw[:, :, 2].astype(low)
        scores = jnp.einsum("gphd,gqhd->ghpq", query, keys, preferred_element_type=wide) * scale_dot
        peak = jnp.max(scores, axis=-1, keepdims=True)
        expo = jnp.exp(scores - peak)
        total = jnp.sum(expo, axis=-1, keepdims=True)
        logsum = peak + jnp.log(total)
        probs = (expo / total).astype(low)
        attended = jnp.einsum("ghpq,gqhd->gphd", probs, values, preferred_element_type=wide)
        attended = attended.astype(low).reshape(rows.shape[0], head_cols)
        kept.append((raw, query_norm, key_norm, query, keys, values, logsum, attended))
        branch_parts.append(
            jnp.einsum("rh,oh->ro", attended, proj_cols, preferred_element_type=wide)
        )
    branch_one = gathered_sum(branch_parts)
    if rings:
        branch_one = after(branch_one, hop)
        hop = ring.hop(branch_parts[1])
    middle = block_input + gate_one * branch_one
    n_two = rms_norm(middle)
    h_two = (n_two * (1.0 + scale_two) + shift_two).astype(low)
    rows_two = spread(h_two)
    if rings:
        rows_two[1] = after(rows_two[1], hop)
        ring.hop(h_two)
        w_one, w_three, w_two = matrices(ring, 3, 6)

    branch_parts, hidden_parts, gate_parts, up_parts, d_parts = [], [], [], [], []
    for rows, back in zip(rows_two, back_two, strict=True):
        gate_pre = jnp.dot(rows, w_one, preferred_element_type=wide)
        up_pre = jnp.dot(rows, w_three, preferred_element_type=wide)
        d_hidden = jnp.dot(back, w_two, preferred_element_type=wide)
        sigma = jax.nn.sigmoid(gate_pre)
        silu_gate = gate_pre * sigma
        hidden = (silu_gate * up_pre).astype(low)
        d_gate_pre = (d_hidden * up_pre * sigma * (1.0 + gate_pre * (1.0 - sigma))).astype(low)
        d_up_pre = (d_hidden * silu_gate).astype(low)
        hidden_parts.append(hidden)
        gate_parts.append(d_gate_pre)
        up_parts.append(d_up_pre)
        d_parts.append(
            jnp.einsum("rf,df->rd", d_gate_pre, w_one, preferred_element_type=wide)
            + jnp.einsum("rf,df->rd", d_up_pre, w_three, preferred_element_type=wide)
        )
        branch_parts.append(
            jnp.einsum("rf,of->ro", hidden, w_two, preferred_element_type=wide)
        )

    if rings:
        own, other = grads_mlp(
            rows_two, back_two, gate_parts, up_parts, hidden_parts, table, data_size
        )
        ring = RingScatter(own, other)
    else:
        grad_mlp = to_owners(
            [(rows_two, gate_parts), (rows_two, up_parts), (back_two, hidden_parts)], 3
        )
    d_h_two = gathered_sum(d_parts)
    d_shift_two = jnp.sum(d_h_two, axis=0)
    d_scale_two = jnp.sum(d_h_two * n_two, axis=0)
    d_middle = cotangent + norm_back(middle, n_two, d_h_two * (1.0 + scale_two))
    d_gate_one = jnp.sum(d_middle * branch_one, axis=0)
    send_one = (gate_one * d_middle).astype(low)
    back_one = spread(send_one)
    branch_parts[-1] = after(branch_parts[-1], back_one[-1])
    branch_two = gathered_sum(branch_parts)
    output = middle + gate_two * branch_two
    d_gate_two = jnp.sum(cotangent * branch_two, axis=0)
    if rings:
        back_one[0] = after(back_one[0], ring.partner)
        hop = ring.hop(send_one)

    d_parts, raw_parts = [], []
    gain_grads = jnp.zeros((2, HEAD_DIM), wide)
    for part, (back, saved) in enumerate(zip(back_one, kept, strict=True)):
        if rings and part == 1:
            back = after(back, hop)
            hop = ring.hop(raw_parts[0])
        raw, query_norm, key_norm, query, keys, values, logsum, attended = saved
        d_attended = jnp.dot(back, proj_cols, preferred_element_type=wide).astype(low)
        d_attended = d_attended.reshape(values.shape)
        scores = jnp.einsum("gphd,gqhd->ghpq", query, keys, preferred_element_type=wide) * scale_dot
        probs_full = jnp.exp(scores - logsum)
        d_values = jnp.einsum(
            "ghpq,gphd->gqhd", probs_full.astype(low), d_attended, preferred_element_type=wide
        )
        d_probs = jnp.einsum("gphd,gqhd->ghpq", d_attended, values, preferred_element_type=wide)
        d_scores = probs_full * (d_probs - jnp.sum(probs_full * d_probs, axis=-1, keepdims=True))
        d_scores = d_scores.astype(low)
        d_query = (
            jnp.einsum("ghpq,gqhd->gphd", d_scores, keys, preferred_element_type=wide) * scale_dot
        )
        d_keys = (
            jnp.einsum("ghpq,gphd->gqhd", d_scores, query, preferred_element_type=wide) * scale_dot
        )
        d_query_norm = rotate(d_query, cosine, -sine)
        d_key_norm = rotate(d_keys, cosine, -sine)
        gain_grads += jnp.stack(
            [
                jnp.sum(d_query_norm * query_norm, axis=(0, 1, 2)),
                jnp.sum(d_key_norm * key_norm, axis=(0, 1, 2)),
            ]
        )
        d_raw_query = norm_back(raw[:, :, 0], query_norm, d_query_norm * gains[0])
        d_raw_key = norm_back(raw[:, :, 1], key_norm, d_key_norm * gains[1])
        d_raw = jnp.stack([d_raw_query, d_raw_key, d_values], axis=2).astype(low)
        d_raw = d_raw.reshape(back.shape[0], 3 * head_cols)
        raw_parts.append(d_raw)
        d_parts.append(jnp.einsum("rc,dc->rd", d_raw, qkv_cols, preferred_element_type=wide))
    attended_parts = [saved[-1] for saved in kept]
    if rings:
        held = after(raw_parts[1], hop)
        hop = ring.hop(raw_parts[1])
        own, other = grads_att(
            rows_one, back_one, [raw_parts[0], held], attended_parts, table, data_size
        )
        ring_att = RingScatter(own, other)
        ring.hop(own)
        grad_mlp = ring.total()
        for _ in range(4):
            ring_att.hop()
        grad_att = ring_att.total()
    else:
        grad_att = to_owners([(rows_one, raw_parts), (back_one, attended_parts)], 1)
    d_h_one = gathered_sum(d_parts)
    d_shift_one = jnp.sum(d_h_one, axis=0)
    d_scale_one = jnp.sum(d_h_one * n_own, axis=0)
    d_inputs = d_middle + norm_back(block_input, n_own, d_h_one * (1.0 + scale_one))

    d_mod = jnp.stack([d_shift_one, d_scale_one, d_gate_one, d_shift_two, d_scale_two, d_gate_two])
    d_mod = d_mod.reshape(6, data_size, own_rows).transpose(1, 0, 2)
    d_mod = jnp.roll(d_mod, owner[0], axis=0).reshape(data_size, 6 * own_rows)
    gain_row = jnp.broadcast_to(gain_grads.reshape(1, -1), (data_size, 2 * HEAD_DIM))
    send = jnp.concatenate([d_mod, gain_row], axis=1)
    send = jnp.broadcast_to(send[:, None], (data_size, tensor_size, send.shape[1]))
    send = send.reshape(data_size * tensor_size, send.shape[2])
    got = lax.all_to_all(send, devices, 0, 0, tiled=True)
    gain_sum = jnp.sum(got[:, 6 * own_rows :], axis=0)
    d_own = got[:, : 6 * own_rows].reshape(images_all, 6, own_rows).transpose(1, 0, 2)
    row_sum = jnp.sum(d_own, axis=1).reshape(-1)
    d_own = d_own.reshape(6 * images_all, own_rows)
    grad_ada = lax.dot_general(
        d_own,
        lifted_maps.astype(wide),
        (((0,), (0,)), ((), ())),
        precision=precise,
        preferred_element_type=wide,
    )
    d_lifted = lax.dot_general(
        d_own,
        ada.astype(wide),
        (((1,), (0,)), ((), ())),
        precision=precise,
        preferred_element_type=wide,
    )
    d_lifted = jnp.where(on_map, d_lifted, 0.0).reshape(6, images_all, 6 * head_cols).sum(axis=0)
    d_lifted = sum(d_lifted[:, j * head_cols : (j + 1) * head_cols] for j in range(6))
    send = jnp.concatenate(
        [
            d_lifted.reshape(data_size, group_images * head_cols),
            jnp.broadcast_to(row_sum[None, :], (data_size, 6 * own_rows)),
        ],
        axis=1,
    )
    got = lax.all_to_all(send, "dp", 0, 0, tiled=True)
    d_lifted = jnp.sum(got[:, : group_images * head_cols], axis=0).reshape(group_images, head_cols)
    cond_here = lax.dynamic_slice_in_dim(cond, data_index * group_images, group_images, 0)
    d_cond = d_lifted * silu_slope(cond_here)
    vec_rows = got[:, group_images * head_cols :].reshape(data_size, 6, own_rows)
    vec_rows = jnp.roll(vec_rows, -owner[0], axis=0).transpose(1, 0, 2).reshape(-1)
    vec_grad = jnp.concatenate([vec_rows, gain_sum])

    grad_mine = jnp.concatenate([grad_ada, grad_att, grad_mlp], axis=1)
    block_count = grad_mine.shape[1] // BLOCK_WIDTH
    pieces = grad_mine.astype(low).reshape(own_rows, block_count, BLOCK_WIDTH).transpose(1, 0, 2)
    left_new = 0.5 * left_stats[0] + 0.5 * jnp.einsum(
        "bij,bkj->bik", pieces, pieces, preferred_element_type=wide
    )
    right_new = 0.5 * right_stats[0] + 0.5 * jnp.einsum(
        "bji,bjk->bik", pieces, pieces, preferred_element_type=wide
    )
    update = jnp.einsum(
        "bij,bjk->bik", left_roots[0].astype(low), pieces, preferred_element_type=wide
    )
    update = jnp.einsum(
        "bik,bkl->bil",
        update.astype(low),
        right_roots[0].astype(low),
        preferred_element_type=wide,
    )
    update = update.transpose(1, 0, 2).reshape(own_rows, block_count * BLOCK_WIDTH)
    master_new = master - shampoo_rate * update
    tokens_all = row_count * data_size * tensor_size
    mom_new = momentum * vec_mom + vec_grad
    vec_new = vec - 0.1 / tokens_all**0.5 * mom_new
    return (
        output,
        d_inputs,
        d_cond,
        grad_mine,
        left_new[None],
        right_new[None],
        master_new,
        master_new.astype(low),
        vec_new,
        mom_new,
    )


def solution(mesh):
    placed = (
        P(("dp", "tensor"), None),
        P(("dp", "tensor"), None),
        P("dp", "tensor"),
        P("dp", "tensor", None, None),
        P("dp", "tensor", None, None),
        P("dp", "tensor", None, None),
        P("dp", "tensor", None, None),
        P(),
        P(),
        P(),
        P(),
        P("dp"),
        P("dp"),
        P(),
    )
    return jax.shard_map(
        local,
        mesh=mesh,
        in_specs=placed,
        out_specs=(
            P(("dp", "tensor"), None),
            P(("dp", "tensor"), None),
            P("dp", "tensor"),
            P("dp", "tensor"),
            P("dp", "tensor", None, None),
            P("dp", "tensor", None, None),
            P("dp", "tensor"),
            P("dp", "tensor"),
            P(),
            P(),
        ),
        check_vma=False,
    )
```

```python
import functools

import jax
import jax.numpy as jnp
from jax import lax
from jax.experimental import pallas as pl
from jax.experimental.pallas import tpu as pltpu
from jax.sharding import PartitionSpec as P

HEAD_DIM = 72
FF = 3072
PATCHES = 256
GRID = 16
BLOCK_WIDTH = 48
RING = (0, 1, 3, 5, 7, 6, 4, 2)
LANES = 128

epsilon = 1e-06
precise = lax.Precision.HIGHEST
shampoo_rate = 0.25
momentum = 0.9
low = jnp.bfloat16
wide = jnp.float32


def rms_norm(values):
    return values * lax.rsqrt(jnp.mean(values * values, axis=-1, keepdims=True) + epsilon)


def norm_back(values, normed, upstream):
    factor = lax.rsqrt(jnp.mean(values * values, axis=-1, keepdims=True) + epsilon)
    return factor * (upstream - normed * jnp.mean(upstream * normed, axis=-1, keepdims=True))


def rope_tables():
    quarter = HEAD_DIM // 4
    freqs = 10000.0 ** (-jnp.arange(quarter, dtype=jnp.float32) / quarter)
    places = jnp.arange(PATCHES)
    coords = jnp.stack([places // GRID, places % GRID], axis=1).astype(jnp.float32)
    angles = coords[:, :, None] * freqs[None, None, :]
    return (jnp.cos(angles), jnp.sin(angles))


def rotate(values, cosine, sine):
    shape = values.shape
    halves = values.reshape(shape[:-1] + (2, 2, shape[-1] // 4))
    first_part = halves[..., 0, :]
    second_part = halves[..., 1, :]
    cosine = cosine[:, None]
    sine = sine[:, None]
    turned = jnp.stack(
        [first_part * cosine - second_part * sine, second_part * cosine + first_part * sine],
        axis=-2,
    )
    return turned.reshape(shape)


def roll_blocks(matrix, shift, groups):
    blocks = matrix.reshape((groups, matrix.shape[0] // groups) + matrix.shape[1:])
    return jnp.roll(blocks, shift, axis=0).reshape(matrix.shape)


def silu_slope(values):
    sigma = jax.nn.sigmoid(values)
    return sigma * (1.0 + values * (1.0 - sigma))


def ring_pairs(step):
    pairs = []
    for place, chip in enumerate(RING):
        goal = RING[(place + step) % len(RING)]
        pairs += [(chip * 2 + core, goal * 2 + core) for core in range(2)]
    return pairs


def around(value, step):
    return lax.ppermute(value, "dp", ring_pairs(step))


def across_cores(value):
    return lax.ppermute(value, "dp", [(i, i ^ 1) for i in range(2 * len(RING))])


def across_tensor(value):
    return lax.ppermute(value, "tensor", [(0, 1), (1, 0)])


def relative_order():
    rows = []
    for device in range(2 * len(RING)):
        place, core = RING.index(device // 2), device % 2
        chips = [RING[(place + offset) % len(RING)] for offset in range(len(RING))]
        rows.append([chip * 2 + core for chip in chips] + [chip * 2 + 1 - core for chip in chips])
    return jnp.array(rows, jnp.int32)


def after(value, *others):
    return lax.optimization_barrier((value, others))[0]


class RingGather:
    def __init__(self, shard):
        self.half = shard.shape[1] // 2
        self.right = self.left = shard
        self.hops = 0
        self.pieces = []
        self.keep(0, 0, shard)

    def keep(self, offset, start, piece):
        self.pieces.append((offset, start, piece))
        self.pieces.append((offset + len(RING), start, across_cores(piece)))

    def hop(self, *ready):
        self.hops += 1
        if self.hops < 4:
            self.right = around(after(self.right, *ready), 1)
            self.left = around(after(self.left, *ready), -1)
            self.keep(8 - self.hops, 0, self.right)
            self.keep(self.hops, 0, self.left)
        else:
            self.right = around(after(self.right[:, : self.half], *ready), 1)
            self.left = around(after(self.left[:, self.half :], *ready), -1)
            self.keep(4, 0, self.right)
            self.keep(4, self.half, self.left)
        return self.right, self.left


class RingScatter:
    def __init__(self, own, other):
        self.own = own
        self.half = own.shape[2] // 2
        self.partner = across_cores(other)
        self.hops = 0

    def term(self, offset):
        return self.own[offset].astype(wide) + self.partner[offset].astype(wide)

    def hop(self, *ready):
        half = self.half
        if self.hops == 0:
            start = self.term(4).astype(low)
            right, left = start[:, :half], start[:, half:]
        else:
            mine, other = self.term(4 - self.hops), self.term(4 + self.hops)
            right, left = self.right.astype(wide), self.left.astype(wide)
            if self.hops == 1:
                right = jnp.concatenate([mine[:, :half] + right, mine[:, half:]], axis=1)
                left = jnp.concatenate([other[:, :half], other[:, half:] + left], axis=1)
            else:
                right, left = right + mine, left + other
            right, left = right.astype(low), left.astype(low)
        self.hops += 1
        self.right = around(after(right, *ready), 1)
        self.left = around(after(left, *ready), -1)
        return self.right, self.left

    def total(self):
        return self.term(0) + self.right.astype(wide) + self.left.astype(wide)


def assemble(pieces, table, first, widths, blocks):
    rows = pieces[0][2].shape[0]
    starts = [sum(widths[:i]) for i in range(len(widths))]

    def body(table_ref, *refs):
        outs = refs[len(pieces) :]
        for (place, at, _), ref in zip(pieces, refs, strict=False):
            for index, (out, start, width) in enumerate(zip(outs, starts, widths, strict=True)):
                low_end = max(start, at)
                high_end = min(start + width, at + ref.shape[1])
                if low_end < high_end:
                    goal = table_ref[(first + index) * blocks + place]
                    out[goal, :, low_end - start : high_end - start] = ref[
                        :, low_end - at : high_end - at
                    ]

    whole = pl.BlockSpec(memory_space=pltpu.VMEM)
    outs = pl.pallas_call(
        body,
        in_specs=[pl.BlockSpec(memory_space=pltpu.SMEM)] + [whole for _ in pieces],
        out_specs=[whole for _ in widths],
        out_shape=[jax.ShapeDtypeStruct((blocks, rows, width), low) for width in widths],
        cost_estimate=pl.CostEstimate(
            flops=0, transcendentals=0, bytes_accessed=4 * blocks * rows * sum(widths)
        ),
        name="assemble",
    )(table, *[piece for _, _, piece in pieces])
    return [out.reshape(blocks * rows, width) for out, width in zip(outs, widths, strict=True)]


def turn(parts, flat_ref):
    at = 0
    for part in parts:
        flat_ref[:, at : at + part.shape[0]] = part[...].astype(wide).T
        at += part.shape[0]


def sort_rows(flat_ref, left_ref, table_ref, base, rows):
    for place in range(left_ref.shape[0] // rows):
        source = pl.multiple_of(table_ref[base + place] * rows, 8)
        left_ref[place * rows : (place + 1) * rows, :] = flat_ref[pl.ds(source, rows), :].astype(low)


def product_rows(left, rights, at, columns):
    total, start = None, 0
    for right in rights:
        piece = right[:, at : at + columns]
        term = jnp.dot(
            left[:, start : start + right.shape[0]], piece, preferred_element_type=wide
        )
        total = term if total is None else total + term
        start += right.shape[0]
    return total


def grads_mlp(rows_two, back_two, gates, ups, hiddens, table, blocks):
    count, width = rows_two[0].shape
    rows, cols = width // blocks, gates[0].shape[1]
    tile = 512
    steps = cols // tile

    def body(table_ref, h0, h1, b0, b1, g0, g1, u0, u1, v0, v1, own_ref, other_ref, flat, left):
        step = pl.program_id(0)

        @pl.when(step == 0)
        def _():
            turn((h0, h1), flat)
            sort_rows(flat, left, table_ref, 3 * blocks, rows)

        @pl.when(step == steps)
        def _():
            sort_rows(flat, left, table_ref, 4 * blocks, rows)

        @pl.when(step == 2 * steps)
        def _():
            turn((b0, b1), flat)
            sort_rows(flat, left, table_ref, 5 * blocks, rows)

        def work(rights):
            for side, out in enumerate((own_ref, other_ref)):
                half = left[side * (width // 2) : (side + 1) * (width // 2), :]
                total = product_rows(half, rights, 0, tile)
                out[...] = total.reshape(blocks // 2, rows, tile).astype(low)

        pl.when(step < steps)(lambda: work((g0, g1)))
        pl.when((step >= steps) & (step < 2 * steps))(lambda: work((u0, u1)))
        pl.when(step >= 2 * steps)(lambda: work((v0, v1)))

    def part_spec(first):
        return pl.BlockSpec(
            (count, tile), lambda step, table: (0, jnp.clip(step - first, 0, steps - 1))
        )

    whole = pl.BlockSpec((count, width), lambda step, table: (0, 0))
    out_spec = pl.BlockSpec((blocks // 2, rows, tile), lambda step, table: (0, 0, step))
    out = jax.ShapeDtypeStruct((blocks // 2, rows, 3 * cols), low)
    return pl.pallas_call(
        body,
        grid_spec=pltpu.PrefetchScalarGridSpec(
            num_scalar_prefetch=1,
            grid=(3 * steps,),
            in_specs=[whole] * 4
            + [part_spec(0)] * 2
            + [part_spec(steps)] * 2
            + [part_spec(2 * steps)] * 2,
            out_specs=[out_spec, out_spec],
            scratch_shapes=[
                pltpu.VMEM((width, 2 * count), wide),
                pltpu.VMEM((width, 2 * count), low),
            ],
        ),
        out_shape=[out, out],
        cost_estimate=pl.CostEstimate(
            flops=2 * 3 * 2 * count * width * cols,
            transcendentals=0,
            bytes_accessed=2 * (4 * count * width + 6 * count * cols + 3 * width * cols),
        ),
        name="grads_mlp",
    )(table, *rows_two, *back_two, *gates, *ups, *hiddens)


def grads_att(rows_one, back_one, raws, attendeds, table, blocks):
    count, width = rows_one[0].shape
    rows, cols = width // blocks, attendeds[0].shape[1]

    def body(table_ref, h0, h1, b0, b1, r0, r1, a0, a1, own_ref, other_ref, flat, left):
        def work(rights, at, goal):
            for side, out in enumerate((own_ref, other_ref)):
                half = left[side * (width // 2) : (side + 1) * (width // 2), :]
                total = product_rows(half, rights, at, cols)
                out[:, :, goal : goal + cols] = total.reshape(blocks // 2, rows, cols).astype(low)

        turn((h0, h1), flat)
        sort_rows(flat, left, table_ref, blocks, rows)
        for third in range(3):
            work((r0, r1), third * cols, third * cols)
        turn((b0, b1), flat)
        sort_rows(flat, left, table_ref, 2 * blocks, rows)
        work((a0, a1), 0, 3 * cols)

    whole = pl.BlockSpec(memory_space=pltpu.VMEM)
    out = jax.ShapeDtypeStruct((blocks // 2, rows, 4 * cols), low)
    return pl.pallas_call(
        body,
        in_specs=[pl.BlockSpec(memory_space=pltpu.SMEM)] + [whole] * 8,
        out_specs=[whole, whole],
        out_shape=[out, out],
        scratch_shapes=[
            pltpu.VMEM((width, 2 * count), wide),
            pltpu.VMEM((width, 2 * count), low),
        ],
        cost_estimate=pl.CostEstimate(
            flops=2 * 4 * 2 * count * width * cols,
            transcendentals=0,
            bytes_accessed=2 * (4 * count * width + 8 * count * cols + 4 * width * cols),
        ),
        name="grads_att",
    )(table, *rows_one, *back_one, *raws, *attendeds)


def to_matrices(left_roots, right_roots):
    count = left_roots.shape[2]

    def body(left_ref, right_ref, left_out, right_out, scratch):
        for source, goal in ((left_ref, left_out), (right_ref, right_out)):
            size = source.shape[0]

            @pl.loop(0, size, unroll=8)
            def _(i):
                slab = source[i]
                slab = jnp.concatenate([slab, jnp.zeros((LANES - size, LANES), wide)], axis=0)
                scratch[pl.ds(i, LANES, stride=size), :] = slab.T

            @pl.loop(0, LANES, unroll=8)
            def _(b):
                start = pl.multiple_of(b * size, 8)
                goal[b] = scratch[pl.ds(start, size), :size].astype(low)

    def sides(of):
        return [of(left_roots.shape[0]), of(right_roots.shape[0])]

    return pl.pallas_call(
        body,
        grid=(pl.cdiv(count, LANES),),
        in_specs=sides(lambda size: pl.BlockSpec((size, size, LANES), lambda g: (0, 0, g))),
        out_specs=sides(lambda size: pl.BlockSpec((LANES, size, size), lambda g: (g, 0, 0))),
        out_shape=sides(lambda size: jax.ShapeDtypeStruct((count, size, size), low)),
        scratch_shapes=[pltpu.VMEM((LANES * left_roots.shape[0], LANES), wide)],
        cost_estimate=pl.CostEstimate(
            flops=0, transcendentals=0, bytes_accessed=4 * (left_roots.size + right_roots.size)
        ),
        name="to_matrices",
    )(left_roots, right_roots)


def shampoo(sources, spans, master, mats, filled, group, stats=None, early=None):
    rows, cols = master.shape
    chunk = 8
    wide_cols = chunk * BLOCK_WIDTH
    start = group * LANES
    starts = [0]
    for _, _, number in spans:
        starts.append(starts[-1] + number // chunk)
    steps = starts[-1]
    early_spans, early_sums = early if early else ([], [])
    sizes = (rows, BLOCK_WIDTH)

    def place(step):
        index = step + spans[0][1] // chunk
        for at, (_, first, _) in zip(starts[1:], spans[1:]):
            index = jnp.where(step >= at, step - at + first // chunk, index)
        return index

    def body(*refs):
        source_refs, refs = refs[: len(sources)], refs[len(sources) :]
        master_ref, left_mat, right_mat = refs[:3]
        step = pl.program_id(0)
        if stats:
            stat_refs = refs[3:5]
            early_refs = refs[5 : 5 + len(early_sums)]
            tail = 4 if early_sums else 2
            grad_out, master_out, low_out, left_out, right_out = refs[-5 - tail : -tail]
            sums = refs[-tail:][:2]
            copies = []
            for sum_ref, early_ref, size, sem in zip(
                sums, early_refs, sizes, refs[-tail:][2:], strict=False
            ):
                at = 0
                for index, (_, first, number) in enumerate(early_spans):
                    copies.append(
                        pltpu.make_async_copy(
                            early_ref.at[pl.ds(at * size, number * size)],
                            sum_ref.at[pl.ds((first - start) * size, number * size)],
                            sem.at[index],
                        )
                    )
                    at += number

            @pl.when(step == 0)
            def _():
                for copy in copies:
                    copy.start()
        else:
            grad_out, master_out, low_out = refs[-5:-2]
            sums = refs[-2:]
        grad = source_refs[0][...]
        for at, ref in zip(starts[1:], source_refs[1:]):
            grad = jnp.where(step >= at, ref[...], grad)
        grad_out[...] = grad
        turned = grad.T.astype(low)
        grad = grad.astype(low)
        base = place(step) * chunk - start if stats else 0
        updates = []
        for b in range(chunk):
            side = turned[b * BLOCK_WIDTH : (b + 1) * BLOCK_WIDTH, :]
            upright = grad[:, b * BLOCK_WIDTH : (b + 1) * BLOCK_WIDTH]
            at = base + b
            if stats:
                left_rows = pl.ds(pl.multiple_of(at * rows, 8), rows)
                right_rows = pl.ds(pl.multiple_of(at * BLOCK_WIDTH, 8), BLOCK_WIDTH)
            else:
                left_rows = slice(b * rows, (b + 1) * rows)
                right_rows = slice(b * BLOCK_WIDTH, (b + 1) * BLOCK_WIDTH)
            sums[0][left_rows, :rows] = jnp.dot(upright, side, preferred_element_type=wide)
            sums[1][right_rows, :BLOCK_WIDTH] = lax.dot_general(
                side, side, (((1,), (1,)), ((), ())), preferred_element_type=wide
            )
            half = jnp.dot(right_mat[b], side, preferred_element_type=wide).astype(low)
            updates.append(jnp.dot(half, left_mat[b], preferred_element_type=wide))
        new = master_ref[...] - shampoo_rate * jnp.concatenate(updates, axis=0).T
        master_out[...] = new
        low_out[...] = new.astype(low)
        if stats:

            @pl.when(step == steps - 1)
            def _():
                for copy in copies:
                    copy.wait()
                for sum_ref, stat_ref, out in zip(
                    sums, stat_refs, (left_out, right_out), strict=True
                ):
                    size = out.shape[0]
                    here = min(LANES, stats[0].shape[2] - start)

                    @pl.loop(0, size, unroll=8)
                    def _(i):
                        slab = sum_ref[pl.ds(i, here, stride=size), :].T
                        out[i, :, :here] = 0.5 * stat_ref[i, :, :here] + 0.5 * slab[:size]

    def source_spec(index):
        first = spans[index][0] // chunk
        count = spans[index][2] // chunk

        def at(step):
            return (0, first + jnp.clip(step - starts[index], 0, count - 1))

        return pl.BlockSpec((rows, wide_cols), at)

    def lanes_spec(size):
        return pl.BlockSpec((size, size, LANES), lambda step: (0, 0, group))

    def mats_spec(size):
        return pl.BlockSpec((chunk, size, size), lambda step: (place(step), 0, 0))

    def sums_spec(size):
        return pl.BlockSpec((chunk * size, LANES), lambda step: (step, 0))

    own = pl.BlockSpec((rows, wide_cols), lambda step: (0, place(step)))
    anywhere = pl.BlockSpec(memory_space=pl.ANY)
    in_specs = [source_spec(i) for i in range(len(sources))] + [own] + [mats_spec(s) for s in sizes]
    out_specs = [own, own, own]
    outs = [jax.ShapeDtypeStruct((rows, cols), kind) for kind in (wide, wide, low)]
    scratch = []
    if stats:
        in_specs += [lanes_spec(s) for s in sizes] + [anywhere for _ in early_sums]
        out_specs += [lanes_spec(s) for s in sizes]
        outs += [jax.ShapeDtypeStruct(stat.shape, wide) for stat in stats]
        scratch = [pltpu.VMEM((LANES * s, LANES), wide) for s in sizes]
        if early_sums:
            scratch += [pltpu.SemaphoreType.DMA((len(early_spans),)) for _ in sizes]
    else:
        out_specs += [sums_spec(s) for s in sizes]
        outs += [jax.ShapeDtypeStruct((steps * chunk * s, LANES), wide) for s in sizes]
    operands = [*sources, master, *mats, *(stats or []), *early_sums]
    number = steps * chunk
    return pl.pallas_call(
        body,
        grid=(steps,),
        in_specs=in_specs + [anywhere for _ in filled],
        out_specs=out_specs,
        out_shape=outs,
        scratch_shapes=scratch,
        input_output_aliases={len(operands) + i: i for i in range(len(filled))},
        cost_estimate=pl.CostEstimate(
            flops=number * 8 * rows * rows * BLOCK_WIDTH,
            transcendentals=0,
            bytes_accessed=number * 4 * (3 * rows * rows + 4 * rows * BLOCK_WIDTH),
        ),
        name="shampoo",
    )(*operands, *filled)


def local(
    block_input,
    cotangent,
    master,
    left_stats,
    right_stats,
    left_roots,
    right_roots,
    vec,
    vec_mom,
    time_table,
    class_table,
    bucket,
    label,
    owner,
):
    tensor_size = lax.axis_size("tensor")
    data_size = lax.axis_size("dp")
    rings = tensor_size == 2 and data_size == 2 * len(RING)
    tensor_index = lax.axis_index("tensor")
    data_index = lax.axis_index("dp")
    row_count, width = block_input.shape
    own_rows = master.shape[0]
    head_cols = width // tensor_size
    local_heads = head_cols // HEAD_DIM
    hidden_cols = FF // tensor_size
    group_images = row_count // PATCHES * tensor_size
    images_all = group_images * data_size
    scale_dot = HEAD_DIM ** (-0.5)
    widths = [6 * head_cols, 3 * head_cols, head_cols, hidden_cols, hidden_cols, hidden_cols]
    bounds = [0]
    for piece_width in widths:
        bounds.append(bounds[-1] + piece_width)
    devices = ("dp", "tensor")

    if rings:
        order = lax.dynamic_index_in_dim(relative_order(), data_index, 0, keepdims=False)
        table = ((order[None, :] - owner[:, None]) % data_size).reshape(-1)

        def ring_of(first, last, *ready):
            return RingGather(after(master[:, bounds[first] : bounds[last]].astype(low), *ready))

        def matrices(ring, first, last):
            return assemble(ring.pieces, table, first, widths[first:last], data_size)

        def spread(rows):
            return [rows, across_tensor(rows)]

        def gathered_sum(parts):
            return parts[0] + across_tensor(parts[1].astype(low)).astype(wide)
    else:

        def weights(first, last):
            own = master[:, bounds[first] : bounds[last]].astype(low)
            gathered = lax.all_gather(own, "dp", axis=0, tiled=True)
            natural, at = [], 0
            for index in range(first, last):
                piece = gathered[:, at : at + widths[index]]
                natural.append(roll_blocks(piece, -owner[index], data_size))
                at += widths[index]
            return natural

        def to_owners(pairs, first):
            grads = [
                lax.dot_general(
                    left[0], right[0], (((0,), (0,)), ((), ())), preferred_element_type=wide
                ).astype(low)
                for left, right in pairs
            ]
            flat = [roll_blocks(grad, owner[first + i], data_size) for i, grad in enumerate(grads)]
            flat = jnp.concatenate(flat, axis=1)
            return lax.psum_scatter(flat, "dp", scatter_dimension=0, tiled=True).astype(wide)

        def spread(rows):
            return [lax.all_gather(rows, "tensor", axis=0, tiled=True)]

        def gathered_sum(parts):
            summed = lax.psum_scatter(
                parts[0].astype(low), "tensor", scatter_dimension=0, tiled=True
            )
            return summed.astype(wide)

    if rings:
        mats = to_matrices(left_roots[0].transpose(1, 2, 0), right_roots[0].transpose(1, 2, 0))
        stats = [left_stats[0].transpose(1, 2, 0), right_stats[0].transpose(1, 2, 0)]

    n_own = rms_norm(block_input)
    if rings:
        n_low = n_own.astype(low)
        n_partner = across_tensor(n_low)
    marks = jnp.stack([bucket, label], axis=1)
    marks = jnp.broadcast_to(marks[None], (data_size,) + marks.shape)
    marks = lax.all_to_all(marks, "dp", 0, 0, tiled=True).reshape(images_all, 2)
    if rings:
        ring = ring_of(1, 3, marks)
        hop = ring.hop()
    cond = time_table[marks[:, 0]] + class_table[marks[:, 1]]
    cond = lax.dynamic_slice_in_dim(cond, tensor_index * head_cols, head_cols, 1)
    lifted = jax.nn.silu(cond).astype(low)
    ada = master[:, : bounds[1]].astype(low)
    row_map = lax.broadcasted_iota(jnp.int32, (6 * images_all, 6 * head_cols), 0) // images_all
    col_map = lax.broadcasted_iota(jnp.int32, (6 * images_all, 6 * head_cols), 1) // head_cols
    on_map = row_map == col_map
    lifted_maps = jnp.where(on_map, jnp.tile(lifted, (6, 6)), jnp.zeros((), low))
    partial_mod = lax.dot_general(
        lifted_maps, ada, (((1,), (1,)), ((), ())), preferred_element_type=wide
    )
    send = partial_mod.reshape(6, data_size, group_images, own_rows).transpose(1, 0, 2, 3)
    send = jnp.broadcast_to(send[:, None], (data_size, tensor_size) + send.shape[1:])
    send = send.reshape((data_size * tensor_size,) + send.shape[2:])
    if rings:
        send = after(send, hop)
        hop = ring.hop()
    got = lax.all_to_all(send, devices, 0, 0, tiled=True)
    if rings:
        got = after(got, hop)
        ring.hop()
    got = got.reshape((data_size, tensor_size) + got.shape[1:]).sum(axis=1)
    got = jnp.roll(got, -owner[0], axis=0).transpose(2, 1, 0, 3)
    mods = got.reshape(group_images, 6, width) + vec[: 6 * width].reshape(6, width)

    mod = lax.dynamic_index_in_dim(mods, tensor_index, 0, keepdims=False)
    shift_one, scale_one, gate_one, shift_two, scale_two, gate_two = [
        mod[index][None, :] for index in range(6)
    ]
    gains = vec[6 * width :].reshape(2, HEAD_DIM)

    h_one = (n_own * (1.0 + scale_one) + shift_one).astype(low)
    if rings:
        mod_partner = lax.dynamic_index_in_dim(mods, 1 - tensor_index, 0, keepdims=False)
        h_partner = n_partner.astype(wide) * (1.0 + mod_partner[1][None]) + mod_partner[0][None]
        rows_one = [h_one, h_partner.astype(low)]
        hop = ring.hop(rows_one[0])
        qkv_cols, proj_cols = matrices(ring, 1, 3)
        ring = ring_of(3, 6, hop)
        hop = ring.hop()
    else:
        rows_one = spread(h_one)
        qkv_cols, proj_cols = weights(1, 3)
        w_one, w_three, w_two = weights(3, 6)
    send_two = (gate_two * cotangent).astype(low)
    back_two = spread(send_two)

    cosine, sine = rope_tables()
    kept = []
    branch_parts = []
    for part, rows in enumerate(rows_one):
        if rings and part == 1:
            rows = after(rows, hop)
            hop = ring.hop(kept[0][0])
        raw = jnp.dot(rows, qkv_cols, preferred_element_type=wide)
        raw = raw.reshape(rows.shape[0] // PATCHES, PATCHES, 3, local_heads, HEAD_DIM)
        query_norm = rms_norm(raw[:, :, 0])
        key_norm = rms_norm(raw[:, :, 1])
        query = rotate(query_norm * gains[0], cosine, sine).astype(low)
        keys = rotate(key_norm * gains[1], cosine, sine).astype(low)
        values = raw[:, :, 2].astype(low)
        scores = jnp.einsum("gphd,gqhd->ghpq", query, keys, preferred_element_type=wide) * scale_dot
        peak = jnp.max(scores, axis=-1, keepdims=True)
        expo = jnp.exp(scores - peak)
        total = jnp.sum(expo, axis=-1, keepdims=True)
        logsum = peak + jnp.log(total)
        probs = (expo / total).astype(low)
        attended = jnp.einsum("ghpq,gqhd->gphd", probs, values, preferred_element_type=wide)
        attended = attended.astype(low).reshape(rows.shape[0], head_cols)
        kept.append((raw, query_norm, key_norm, query, keys, values, logsum, attended))
        branch_parts.append(
            jnp.einsum("rh,oh->ro", attended, proj_cols, preferred_element_type=wide)
        )
    branch_one = gathered_sum(branch_parts)
    if rings:
        branch_one = after(branch_one, hop)
        hop = ring.hop(branch_parts[1])
    middle = block_input + gate_one * branch_one
    n_two = rms_norm(middle)
    h_two = (n_two * (1.0 + scale_two) + shift_two).astype(low)
    rows_two = spread(h_two)
    if rings:
        rows_two[1] = after(rows_two[1], hop)
        ring.hop(h_two)
        w_one, w_three, w_two = matrices(ring, 3, 6)

    branch_parts, hidden_parts, gate_parts, up_parts, d_parts = [], [], [], [], []
    for rows, back in zip(rows_two, back_two, strict=True):
        gate_pre = jnp.dot(rows, w_one, preferred_element_type=wide)
        up_pre = jnp.dot(rows, w_three, preferred_element_type=wide)
        d_hidden = jnp.dot(back, w_two, preferred_element_type=wide)
        sigma = jax.nn.sigmoid(gate_pre)
        silu_gate = gate_pre * sigma
        hidden = (silu_gate * up_pre).astype(low)
        d_gate_pre = (d_hidden * up_pre * sigma * (1.0 + gate_pre * (1.0 - sigma))).astype(low)
        d_up_pre = (d_hidden * silu_gate).astype(low)
        hidden_parts.append(hidden)
        gate_parts.append(d_gate_pre)
        up_parts.append(d_up_pre)
        d_parts.append(
            jnp.einsum("rf,df->rd", d_gate_pre, w_one, preferred_element_type=wide)
            + jnp.einsum("rf,df->rd", d_up_pre, w_three, preferred_element_type=wide)
        )
        branch_parts.append(
            jnp.einsum("rf,of->ro", hidden, w_two, preferred_element_type=wide)
        )

    if rings:
        hidden_parts[0] = after(hidden_parts[0], d_parts)
        own, other = grads_mlp(
            rows_two, back_two, gate_parts, up_parts, hidden_parts, table, data_size
        )
        ring = RingScatter(own, other)
    else:
        grad_mlp = to_owners(
            [(rows_two, gate_parts), (rows_two, up_parts), (back_two, hidden_parts)], 3
        )
    d_h_two = gathered_sum(d_parts)
    d_shift_two = jnp.sum(d_h_two, axis=0)
    d_scale_two = jnp.sum(d_h_two * n_two, axis=0)
    d_middle = cotangent + norm_back(middle, n_two, d_h_two * (1.0 + scale_two))
    d_gate_one = jnp.sum(d_middle * branch_one, axis=0)
    send_one = (gate_one * d_middle).astype(low)
    back_one = spread(send_one)
    branch_parts[-1] = after(branch_parts[-1], back_one[-1])
    branch_two = gathered_sum(branch_parts)
    output = middle + gate_two * branch_two
    d_gate_two = jnp.sum(cotangent * branch_two, axis=0)
    if rings:
        hop = ring.hop()
        back_one[0] = after(back_one[0], hop)

    d_parts, raw_parts = [], []
    gain_grads = jnp.zeros((2, HEAD_DIM), wide)
    for part, (back, saved) in enumerate(zip(back_one, kept, strict=True)):
        if rings and part == 1:
            back = after(back, hop)
            hop = ring.hop(raw_parts[0])
        raw, query_norm, key_norm, query, keys, values, logsum, attended = saved
        d_attended = jnp.dot(back, proj_cols, preferred_element_type=wide).astype(low)
        d_attended = d_attended.reshape(values.shape)
        scores = jnp.einsum("gphd,gqhd->ghpq", query, keys, preferred_element_type=wide) * scale_dot
        probs_full = jnp.exp(scores - logsum)
        d_values = jnp.einsum(
            "ghpq,gphd->gqhd", probs_full.astype(low), d_attended, preferred_element_type=wide
        )
        d_probs = jnp.einsum("gphd,gqhd->ghpq", d_attended, values, preferred_element_type=wide)
        d_scores = probs_full * (d_probs - jnp.sum(probs_full * d_probs, axis=-1, keepdims=True))
        d_scores = d_scores.astype(low)
        d_query = (
            jnp.einsum("ghpq,gqhd->gphd", d_scores, keys, preferred_element_type=wide) * scale_dot
        )
        d_keys = (
            jnp.einsum("ghpq,gphd->gqhd", d_scores, query, preferred_element_type=wide) * scale_dot
        )
        d_query_norm = rotate(d_query, cosine, -sine)
        d_key_norm = rotate(d_keys, cosine, -sine)
        gain_grads += jnp.stack(
            [
                jnp.sum(d_query_norm * query_norm, axis=(0, 1, 2)),
                jnp.sum(d_key_norm * key_norm, axis=(0, 1, 2)),
            ]
        )
        d_raw_query = norm_back(raw[:, :, 0], query_norm, d_query_norm * gains[0])
        d_raw_key = norm_back(raw[:, :, 1], key_norm, d_key_norm * gains[1])
        d_raw = jnp.stack([d_raw_query, d_raw_key, d_values], axis=2).astype(low)
        d_raw = d_raw.reshape(back.shape[0], 3 * head_cols)
        raw_parts.append(d_raw)
        d_parts.append(jnp.einsum("rc,dc->rd", d_raw, qkv_cols, preferred_element_type=wide))
    attended_parts = [saved[-1] for saved in kept]
    if rings:
        held = after(raw_parts[1], hop)
        hop = ring.hop(raw_parts[1])
        own, other = grads_att(
            rows_one, back_one, [raw_parts[0], held], attended_parts, table, data_size
        )
        ring_att = RingScatter(own, other)
        ring.hop(own)
        grad_mlp = ring.total()
        blocks_ada, blocks_att = bounds[1] // BLOCK_WIDTH, (bounds[3] - bounds[1]) // BLOCK_WIDTH
        skip = LANES - blocks_ada - blocks_att
        total = bounds[6] // BLOCK_WIDTH
        group_one = shampoo(
            [grad_mlp], [(skip, LANES, total - LANES)], master, mats, [], 1, stats=stats
        )
        for _ in range(4):
            ring_att.hop()
        grad_att = ring_att.total()
    else:
        grad_att = to_owners([(rows_one, raw_parts), (back_one, attended_parts)], 1)
    d_h_one = gathered_sum(d_parts)
    d_shift_one = jnp.sum(d_h_one, axis=0)
    d_scale_one = jnp.sum(d_h_one * n_own, axis=0)
    d_inputs = d_middle + norm_back(block_input, n_own, d_h_one * (1.0 + scale_one))

    d_mod = jnp.stack([d_shift_one, d_scale_one, d_gate_one, d_shift_two, d_scale_two, d_gate_two])
    d_mod = d_mod.reshape(6, data_size, own_rows).transpose(1, 0, 2)
    d_mod = jnp.roll(d_mod, owner[0], axis=0).reshape(data_size, 6 * own_rows)
    gain_row = jnp.broadcast_to(gain_grads.reshape(1, -1), (data_size, 2 * HEAD_DIM))
    send = jnp.concatenate([d_mod, gain_row], axis=1)
    send = jnp.broadcast_to(send[:, None], (data_size, tensor_size, send.shape[1]))
    send = send.reshape(data_size * tensor_size, send.shape[2])
    got = lax.all_to_all(send, devices, 0, 0, tiled=True)
    gain_sum = jnp.sum(got[:, 6 * own_rows :], axis=0)
    d_own = got[:, : 6 * own_rows].reshape(images_all, 6, own_rows).transpose(1, 0, 2)
    row_sum = jnp.sum(d_own, axis=1).reshape(-1)
    d_own = d_own.reshape(6 * images_all, own_rows)
    grad_ada = lax.dot_general(
        d_own,
        lifted_maps.astype(wide),
        (((0,), (0,)), ((), ())),
        precision=precise,
        preferred_element_type=wide,
    )
    d_lifted = lax.dot_general(
        d_own,
        ada.astype(wide),
        (((1,), (0,)), ((), ())),
        precision=precise,
        preferred_element_type=wide,
    )
    d_lifted = jnp.where(on_map, d_lifted, 0.0).reshape(6, images_all, 6 * head_cols).sum(axis=0)
    d_lifted = sum(d_lifted[:, j * head_cols : (j + 1) * head_cols] for j in range(6))
    send = jnp.concatenate(
        [
            d_lifted.reshape(data_size, group_images * head_cols),
            jnp.broadcast_to(row_sum[None, :], (data_size, 6 * own_rows)),
        ],
        axis=1,
    )
    got = lax.all_to_all(send, "dp", 0, 0, tiled=True)
    d_lifted = jnp.sum(got[:, : group_images * head_cols], axis=0).reshape(group_images, head_cols)
    cond_here = lax.dynamic_slice_in_dim(cond, data_index * group_images, group_images, 0)
    d_cond = d_lifted * silu_slope(cond_here)
    vec_rows = got[:, group_images * head_cols :].reshape(data_size, 6, own_rows)
    vec_rows = jnp.roll(vec_rows, -owner[0], axis=0).transpose(1, 0, 2).reshape(-1)
    vec_grad = jnp.concatenate([vec_rows, gain_sum])

    if rings:
        early = [(0, 0, blocks_ada), (0, blocks_ada + blocks_att, LANES - blocks_ada - blocks_att)]
        part = shampoo([grad_ada, grad_mlp], early, master, mats, group_one[:3], 0)
        outs = shampoo(
            [grad_att],
            [(0, blocks_ada, blocks_att)],
            master,
            mats,
            [*part[:3], *group_one[3:]],
            0,
            stats=stats,
            early=(early, part[3:]),
        )
        grad_mine, master_new, weights_low = outs[:3]
        left_new, right_new = outs[3].transpose(2, 0, 1), outs[4].transpose(2, 0, 1)
    else:
        grad_mine = jnp.concatenate([grad_ada, grad_att, grad_mlp], axis=1)
        block_count = grad_mine.shape[1] // BLOCK_WIDTH
        pieces = grad_mine.astype(low).reshape(own_rows, block_count, BLOCK_WIDTH).transpose(1, 0, 2)
        left_new = 0.5 * left_stats[0] + 0.5 * jnp.einsum(
            "bij,bkj->bik", pieces, pieces, preferred_element_type=wide
        )
        right_new = 0.5 * right_stats[0] + 0.5 * jnp.einsum(
            "bji,bjk->bik", pieces, pieces, preferred_element_type=wide
        )
        update = jnp.einsum(
            "bij,bjk->bik", left_roots[0].astype(low), pieces, preferred_element_type=wide
        )
        update = jnp.einsum(
            "bik,bkl->bil",
            update.astype(low),
            right_roots[0].astype(low),
            preferred_element_type=wide,
        )
        update = update.transpose(1, 0, 2).reshape(own_rows, block_count * BLOCK_WIDTH)
        master_new = master - shampoo_rate * update
        weights_low = master_new.astype(low)
    tokens_all = row_count * data_size * tensor_size
    mom_new = momentum * vec_mom + vec_grad
    vec_new = vec - 0.1 / tokens_all**0.5 * mom_new
    return (
        output,
        d_inputs,
        d_cond,
        grad_mine,
        left_new[None],
        right_new[None],
        master_new,
        weights_low,
        vec_new,
        mom_new,
    )


def solution(mesh):
    placed = (
        P(("dp", "tensor"), None),
        P(("dp", "tensor"), None),
        P("dp", "tensor"),
        P("dp", "tensor", None, None),
        P("dp", "tensor", None, None),
        P("dp", "tensor", None, None),
        P("dp", "tensor", None, None),
        P(),
        P(),
        P(),
        P(),
        P("dp"),
        P("dp"),
        P(),
    )
    return jax.shard_map(
        local,
        mesh=mesh,
        in_specs=placed,
        out_specs=(
            P(("dp", "tensor"), None),
            P(("dp", "tensor"), None),
            P("dp", "tensor"),
            P("dp", "tensor"),
            P("dp", "tensor", None, None),
            P("dp", "tensor", None, None),
            P("dp", "tensor"),
            P("dp", "tensor"),
            P(),
            P(),
        ),
        check_vma=False,
    )
```

```python
import functools

import jax
import jax.numpy as jnp
from jax import lax
from jax.experimental import pallas as pl
from jax.experimental.pallas import tpu as pltpu
from jax.sharding import PartitionSpec as P

HEAD_DIM = 72
FF = 3072
PATCHES = 256
GRID = 16
BLOCK_WIDTH = 48
RING = (0, 1, 3, 5, 7, 6, 4, 2)
LANES = 128

epsilon = 1e-06
precise = lax.Precision.HIGHEST
shampoo_rate = 0.25
momentum = 0.9
low = jnp.bfloat16
wide = jnp.float32
BYTES_PER_US = 3_500_000


def lasting(microseconds):
    moved = int(microseconds * BYTES_PER_US)
    return pl.CostEstimate(flops=0, transcendentals=0, bytes_accessed=moved)


def rms_norm(values):
    return values * lax.rsqrt(jnp.mean(values * values, axis=-1, keepdims=True) + epsilon)


def norm_back(values, normed, upstream):
    factor = lax.rsqrt(jnp.mean(values * values, axis=-1, keepdims=True) + epsilon)
    return factor * (upstream - normed * jnp.mean(upstream * normed, axis=-1, keepdims=True))


def rope_tables():
    quarter = HEAD_DIM // 4
    freqs = 10000.0 ** (-jnp.arange(quarter, dtype=jnp.float32) / quarter)
    places = jnp.arange(PATCHES)
    coords = jnp.stack([places // GRID, places % GRID], axis=1).astype(jnp.float32)
    angles = coords[:, :, None] * freqs[None, None, :]
    return (jnp.cos(angles), jnp.sin(angles))


def rotate(values, cosine, sine):
    shape = values.shape
    halves = values.reshape(shape[:-1] + (2, 2, shape[-1] // 4))
    first_part = halves[..., 0, :]
    second_part = halves[..., 1, :]
    cosine = cosine[:, None]
    sine = sine[:, None]
    turned = jnp.stack(
        [first_part * cosine - second_part * sine, second_part * cosine + first_part * sine],
        axis=-2,
    )
    return turned.reshape(shape)


def roll_blocks(matrix, shift, groups):
    blocks = matrix.reshape((groups, matrix.shape[0] // groups) + matrix.shape[1:])
    return jnp.roll(blocks, shift, axis=0).reshape(matrix.shape)


def silu_slope(values):
    sigma = jax.nn.sigmoid(values)
    return sigma * (1.0 + values * (1.0 - sigma))


def ring_pairs(step):
    pairs = []
    for place, chip in enumerate(RING):
        goal = RING[(place + step) % len(RING)]
        pairs += [(chip * 2 + core, goal * 2 + core) for core in range(2)]
    return pairs


def around(value, step):
    return lax.ppermute(value, "dp", ring_pairs(step))


def across_cores(value):
    return lax.ppermute(value, "dp", [(i, i ^ 1) for i in range(2 * len(RING))])


def across_tensor(value):
    return lax.ppermute(value, "tensor", [(0, 1), (1, 0)])


def relative_order():
    rows = []
    for device in range(2 * len(RING)):
        place, core = RING.index(device // 2), device % 2
        chips = [RING[(place + offset) % len(RING)] for offset in range(len(RING))]
        rows.append([chip * 2 + core for chip in chips] + [chip * 2 + 1 - core for chip in chips])
    return jnp.array(rows, jnp.int32)


def after(value, *others):
    return lax.optimization_barrier((value, others))[0]


class RingGather:
    def __init__(self, shard):
        self.half = shard.shape[1] // 2
        self.right = self.left = shard
        self.hops = 0
        self.pieces = []
        self.keep(0, 0, shard)

    def keep(self, offset, start, piece):
        self.pieces.append((offset, start, piece))
        self.pieces.append((offset + len(RING), start, across_cores(piece)))

    def hop(self, *ready):
        self.hops += 1
        ready = (*ready, self.right, self.left)
        if self.hops < 4:
            self.right = around(after(self.right, *ready), 1)
            self.left = around(after(self.left, *ready), -1)
            self.keep(8 - self.hops, 0, self.right)
            self.keep(self.hops, 0, self.left)
        else:
            self.right = around(after(self.right[:, : self.half], *ready), 1)
            self.left = around(after(self.left[:, self.half :], *ready), -1)
            self.keep(4, 0, self.right)
            self.keep(4, self.half, self.left)
        return self.right, self.left


class RingScatter:
    def __init__(self, own, other, ahead):
        self.own = own
        self.half = own.shape[2] // 2
        self.farthest = None
        if ahead:
            self.farthest = across_cores(other[4])
            other = after(other, self.farthest)
        self.partner = across_cores(other)
        self.hops = 0

    def term(self, offset):
        partner = self.partner[offset]
        if offset == 4 and self.farthest is not None:
            partner = self.farthest
        return self.own[offset].astype(wide) + partner.astype(wide)

    def hop(self, *ready):
        half = self.half
        if self.hops == 0:
            start = self.term(4).astype(low)
            right, left = start[:, :half], start[:, half:]
        else:
            mine, other = self.term(4 - self.hops), self.term(4 + self.hops)
            right, left = self.right.astype(wide), self.left.astype(wide)
            if self.hops == 1:
                right = jnp.concatenate([mine[:, :half] + right, mine[:, half:]], axis=1)
                left = jnp.concatenate([other[:, :half], other[:, half:] + left], axis=1)
            else:
                right, left = right + mine, left + other
            right, left = right.astype(low), left.astype(low)
        self.hops += 1
        self.sent = right, left
        ready = (*ready, *self.sent)
        self.right = around(after(right, *ready), 1)
        self.left = around(after(left, *ready), -1)
        return self.right, self.left

    def total(self):
        return self.term(0) + self.right.astype(wide) + self.left.astype(wide)


def assemble(pieces, table, first, widths, blocks):
    rows = pieces[0][2].shape[0]
    starts = [sum(widths[:i]) for i in range(len(widths))]

    def body(table_ref, *refs):
        outs = refs[len(pieces) :]
        for (place, at, _), ref in zip(pieces, refs, strict=False):
            for index, (out, start, width) in enumerate(zip(outs, starts, widths, strict=True)):
                low_end = max(start, at)
                high_end = min(start + width, at + ref.shape[1])
                if low_end < high_end:
                    goal = table_ref[(first + index) * blocks + place]
                    out[goal, :, low_end - start : high_end - start] = ref[
                        :, low_end - at : high_end - at
                    ]

    whole = pl.BlockSpec(memory_space=pltpu.VMEM)
    outs = pl.pallas_call(
        body,
        in_specs=[pl.BlockSpec(memory_space=pltpu.SMEM)] + [whole for _ in pieces],
        out_specs=[whole for _ in widths],
        out_shape=[jax.ShapeDtypeStruct((blocks, rows, width), low) for width in widths],
        cost_estimate=lasting(blocks * rows * sum(widths) / 1.2e6),
        name="assemble",
    )(table, *[piece for _, _, piece in pieces])
    return [out.reshape(blocks * rows, width) for out, width in zip(outs, widths, strict=True)]


def turn(parts, flat_ref):
    at = 0
    for part in parts:
        flat_ref[:, at : at + part.shape[0]] = part[...].astype(wide).T
        at += part.shape[0]


def sort_rows(flat_ref, left_ref, table_ref, base, rows):
    for place in range(left_ref.shape[0] // rows):
        source = pl.multiple_of(table_ref[base + place] * rows, 8)
        left_ref[place * rows : (place + 1) * rows, :] = flat_ref[pl.ds(source, rows), :].astype(low)


def product_rows(left, rights, at, columns):
    total, start = None, 0
    for right in rights:
        piece = right[:, at : at + columns]
        term = jnp.dot(
            left[:, start : start + right.shape[0]], piece, preferred_element_type=wide
        )
        total = term if total is None else total + term
        start += right.shape[0]
    return total


def grads_mlp(rows_two, back_two, gates, ups, hiddens, table, blocks):
    count, width = rows_two[0].shape
    rows, cols = width // blocks, gates[0].shape[1]
    tile = 512
    steps = cols // tile

    def body(table_ref, h0, h1, b0, b1, g0, g1, u0, u1, v0, v1, own_ref, other_ref, flat, left):
        step = pl.program_id(0)

        @pl.when(step == 0)
        def _():
            turn((h0, h1), flat)
            sort_rows(flat, left, table_ref, 3 * blocks, rows)

        @pl.when(step == steps)
        def _():
            sort_rows(flat, left, table_ref, 4 * blocks, rows)

        @pl.when(step == 2 * steps)
        def _():
            turn((b0, b1), flat)
            sort_rows(flat, left, table_ref, 5 * blocks, rows)

        def work(rights):
            for side, out in enumerate((own_ref, other_ref)):
                half = left[side * (width // 2) : (side + 1) * (width // 2), :]
                total = product_rows(half, rights, 0, tile)
                out[...] = total.reshape(blocks // 2, rows, tile).astype(low)

        pl.when(step < steps)(lambda: work((g0, g1)))
        pl.when((step >= steps) & (step < 2 * steps))(lambda: work((u0, u1)))
        pl.when(step >= 2 * steps)(lambda: work((v0, v1)))

    def part_spec(first):
        return pl.BlockSpec(
            (count, tile), lambda step, table: (0, jnp.clip(step - first, 0, steps - 1))
        )

    whole = pl.BlockSpec((count, width), lambda step, table: (0, 0))
    out_spec = pl.BlockSpec((blocks // 2, rows, tile), lambda step, table: (0, 0, step))
    out = jax.ShapeDtypeStruct((blocks // 2, rows, 3 * cols), low)
    return pl.pallas_call(
        body,
        grid_spec=pltpu.PrefetchScalarGridSpec(
            num_scalar_prefetch=1,
            grid=(3 * steps,),
            in_specs=[whole] * 4
            + [part_spec(0)] * 2
            + [part_spec(steps)] * 2
            + [part_spec(2 * steps)] * 2,
            out_specs=[out_spec, out_spec],
            scratch_shapes=[
                pltpu.VMEM((width, 2 * count), wide),
                pltpu.VMEM((width, 2 * count), low),
            ],
        ),
        out_shape=[out, out],
        cost_estimate=lasting(14.7),
        name="grads_mlp",
    )(table, *rows_two, *back_two, *gates, *ups, *hiddens)


def grads_att(rows_one, back_one, raws, attendeds, table, blocks):
    count, width = rows_one[0].shape
    rows, cols = width // blocks, attendeds[0].shape[1]

    def body(table_ref, h0, h1, b0, b1, r0, r1, a0, a1, own_ref, other_ref, flat, left):
        def work(rights, at, goal):
            for side, out in enumerate((own_ref, other_ref)):
                half = left[side * (width // 2) : (side + 1) * (width // 2), :]
                total = product_rows(half, rights, at, cols)
                out[:, :, goal : goal + cols] = total.reshape(blocks // 2, rows, cols).astype(low)

        turn((h0, h1), flat)
        sort_rows(flat, left, table_ref, blocks, rows)
        for third in range(3):
            work((r0, r1), third * cols, third * cols)
        turn((b0, b1), flat)
        sort_rows(flat, left, table_ref, 2 * blocks, rows)
        work((a0, a1), 0, 3 * cols)

    whole = pl.BlockSpec(memory_space=pltpu.VMEM)
    out = jax.ShapeDtypeStruct((blocks // 2, rows, 4 * cols), low)
    return pl.pallas_call(
        body,
        in_specs=[pl.BlockSpec(memory_space=pltpu.SMEM)] + [whole] * 8,
        out_specs=[whole, whole],
        out_shape=[out, out],
        scratch_shapes=[
            pltpu.VMEM((width, 2 * count), wide),
            pltpu.VMEM((width, 2 * count), low),
        ],
        cost_estimate=lasting(8.8),
        name="grads_att",
    )(table, *rows_one, *back_one, *raws, *attendeds)


def to_matrices(left_roots, right_roots):
    count = left_roots.shape[2]

    def body(left_ref, right_ref, left_out, right_out, scratch):
        for source, goal in ((left_ref, left_out), (right_ref, right_out)):
            size = source.shape[0]

            @pl.loop(0, size, unroll=8)
            def _(i):
                slab = source[i]
                slab = jnp.concatenate([slab, jnp.zeros((LANES - size, LANES), wide)], axis=0)
                scratch[pl.ds(i, LANES, stride=size), :] = slab.T

            @pl.loop(0, LANES, unroll=8)
            def _(b):
                start = pl.multiple_of(b * size, 8)
                goal[b] = scratch[pl.ds(start, size), :size].astype(low)

    def sides(of):
        return [of(left_roots.shape[0]), of(right_roots.shape[0])]

    return pl.pallas_call(
        body,
        grid=(pl.cdiv(count, LANES),),
        in_specs=sides(lambda size: pl.BlockSpec((size, size, LANES), lambda g: (0, 0, g))),
        out_specs=sides(lambda size: pl.BlockSpec((LANES, size, size), lambda g: (g, 0, 0))),
        out_shape=sides(lambda size: jax.ShapeDtypeStruct((count, size, size), low)),
        scratch_shapes=[pltpu.VMEM((LANES * left_roots.shape[0], LANES), wide)],
        cost_estimate=lasting(11.5),
        name="to_matrices",
    )(left_roots, right_roots)


def shampoo(sources, spans, master, mats, filled, group, stats=None, early=None):
    rows, cols = master.shape
    chunk = 8
    wide_cols = chunk * BLOCK_WIDTH
    start = group * LANES
    starts = [0]
    for _, _, number in spans:
        starts.append(starts[-1] + number // chunk)
    steps = starts[-1]
    early_spans, early_sums = early if early else ([], [])
    sizes = (rows, BLOCK_WIDTH)

    def place(step):
        index = step + spans[0][1] // chunk
        for at, (_, first, _) in zip(starts[1:], spans[1:]):
            index = jnp.where(step >= at, step - at + first // chunk, index)
        return index

    def body(*refs):
        source_refs, refs = refs[: len(sources)], refs[len(sources) :]
        master_ref, left_mat, right_mat = refs[:3]
        step = pl.program_id(0)
        if stats:
            stat_refs = refs[3:5]
            early_refs = refs[5 : 5 + len(early_sums)]
            tail = 4 if early_sums else 2
            grad_out, master_out, low_out, left_out, right_out = refs[-5 - tail : -tail]
            sums = refs[-tail:][:2]
            copies = []
            for sum_ref, early_ref, size, sem in zip(
                sums, early_refs, sizes, refs[-tail:][2:], strict=False
            ):
                at = 0
                for index, (_, first, number) in enumerate(early_spans):
                    copies.append(
                        pltpu.make_async_copy(
                            early_ref.at[pl.ds(at * size, number * size)],
                            sum_ref.at[pl.ds((first - start) * size, number * size)],
                            sem.at[index],
                        )
                    )
                    at += number

            @pl.when(step == 0)
            def _():
                for copy in copies:
                    copy.start()
        else:
            grad_out, master_out, low_out = refs[-5:-2]
            sums = refs[-2:]
        grad = source_refs[0][...]
        for at, ref in zip(starts[1:], source_refs[1:]):
            grad = jnp.where(step >= at, ref[...], grad)
        grad_out[...] = grad
        turned = grad.T.astype(low)
        grad = grad.astype(low)
        base = place(step) * chunk - start if stats else 0
        updates = []
        for b in range(chunk):
            side = turned[b * BLOCK_WIDTH : (b + 1) * BLOCK_WIDTH, :]
            upright = grad[:, b * BLOCK_WIDTH : (b + 1) * BLOCK_WIDTH]
            at = base + b
            if stats:
                left_rows = pl.ds(pl.multiple_of(at * rows, 8), rows)
                right_rows = pl.ds(pl.multiple_of(at * BLOCK_WIDTH, 8), BLOCK_WIDTH)
            else:
                left_rows = slice(b * rows, (b + 1) * rows)
                right_rows = slice(b * BLOCK_WIDTH, (b + 1) * BLOCK_WIDTH)
            sums[0][left_rows, :rows] = jnp.dot(upright, side, preferred_element_type=wide)
            sums[1][right_rows, :BLOCK_WIDTH] = lax.dot_general(
                side, side, (((1,), (1,)), ((), ())), preferred_element_type=wide
            )
            half = jnp.dot(right_mat[b], side, preferred_element_type=wide).astype(low)
            updates.append(jnp.dot(half, left_mat[b], preferred_element_type=wide))
        new = master_ref[...] - shampoo_rate * jnp.concatenate(updates, axis=0).T
        master_out[...] = new
        low_out[...] = new.astype(low)
        if stats:

            @pl.when(step == steps - 1)
            def _():
                for copy in copies:
                    copy.wait()
                for sum_ref, stat_ref, out in zip(
                    sums, stat_refs, (left_out, right_out), strict=True
                ):
                    size = out.shape[0]
                    here = min(LANES, stats[0].shape[2] - start)

                    @pl.loop(0, size, unroll=8)
                    def _(i):
                        slab = sum_ref[pl.ds(i, here, stride=size), :].T
                        out[i, :, :here] = 0.5 * stat_ref[i, :, :here] + 0.5 * slab[:size]

    def source_spec(index):
        first = spans[index][0] // chunk
        count = spans[index][2] // chunk

        def at(step):
            return (0, first + jnp.clip(step - starts[index], 0, count - 1))

        return pl.BlockSpec((rows, wide_cols), at)

    def lanes_spec(size):
        return pl.BlockSpec((size, size, LANES), lambda step: (0, 0, group))

    def mats_spec(size):
        return pl.BlockSpec((chunk, size, size), lambda step: (place(step), 0, 0))

    def sums_spec(size):
        return pl.BlockSpec((chunk * size, LANES), lambda step: (step, 0))

    own = pl.BlockSpec((rows, wide_cols), lambda step: (0, place(step)))
    anywhere = pl.BlockSpec(memory_space=pl.ANY)
    in_specs = [source_spec(i) for i in range(len(sources))] + [own] + [mats_spec(s) for s in sizes]
    out_specs = [own, own, own]
    outs = [jax.ShapeDtypeStruct((rows, cols), kind) for kind in (wide, wide, low)]
    scratch = []
    if stats:
        in_specs += [lanes_spec(s) for s in sizes] + [anywhere for _ in early_sums]
        out_specs += [lanes_spec(s) for s in sizes]
        outs += [jax.ShapeDtypeStruct(stat.shape, wide) for stat in stats]
        scratch = [pltpu.VMEM((LANES * s, LANES), wide) for s in sizes]
        if early_sums:
            scratch += [pltpu.SemaphoreType.DMA((len(early_spans),)) for _ in sizes]
    else:
        out_specs += [sums_spec(s) for s in sizes]
        outs += [jax.ShapeDtypeStruct((steps * chunk * s, LANES), wide) for s in sizes]
    operands = [*sources, master, *mats, *(stats or []), *early_sums]
    number = steps * chunk
    return pl.pallas_call(
        body,
        grid=(steps,),
        in_specs=in_specs + [anywhere for _ in filled],
        out_specs=out_specs,
        out_shape=outs,
        scratch_shapes=scratch,
        input_output_aliases={len(operands) + i: i for i in range(len(filled))},
        cost_estimate=lasting(number * 0.25),
        name="shampoo",
    )(*operands, *filled)


def local(
    block_input,
    cotangent,
    master,
    left_stats,
    right_stats,
    left_roots,
    right_roots,
    vec,
    vec_mom,
    time_table,
    class_table,
    bucket,
    label,
    owner,
):
    tensor_size = lax.axis_size("tensor")
    data_size = lax.axis_size("dp")
    rings = tensor_size == 2 and data_size == 2 * len(RING)
    tensor_index = lax.axis_index("tensor")
    data_index = lax.axis_index("dp")
    row_count, width = block_input.shape
    own_rows = master.shape[0]
    head_cols = width // tensor_size
    local_heads = head_cols // HEAD_DIM
    hidden_cols = FF // tensor_size
    group_images = row_count // PATCHES * tensor_size
    images_all = group_images * data_size
    scale_dot = HEAD_DIM ** (-0.5)
    widths = [6 * head_cols, 3 * head_cols, head_cols, hidden_cols, hidden_cols, hidden_cols]
    bounds = [0]
    for piece_width in widths:
        bounds.append(bounds[-1] + piece_width)
    devices = ("dp", "tensor")

    if rings:
        order = lax.dynamic_index_in_dim(relative_order(), data_index, 0, keepdims=False)
        table = ((order[None, :] - owner[:, None]) % data_size).reshape(-1)

        def ring_of(first, last, *ready):
            return RingGather(after(master[:, bounds[first] : bounds[last]].astype(low), *ready))

        def matrices(ring, first, last):
            return assemble(ring.pieces, table, first, widths[first:last], data_size)

        def spread(rows):
            return [rows, across_tensor(rows)]

        def gathered_sum(parts, *before):
            got = across_tensor(parts[1].astype(low))
            return parts[0] + after(got, *before).astype(wide)
    else:

        def weights(first, last):
            own = master[:, bounds[first] : bounds[last]].astype(low)
            gathered = lax.all_gather(own, "dp", axis=0, tiled=True)
            natural, at = [], 0
            for index in range(first, last):
                piece = gathered[:, at : at + widths[index]]
                natural.append(roll_blocks(piece, -owner[index], data_size))
                at += widths[index]
            return natural

        def to_owners(pairs, first):
            grads = [
                lax.dot_general(
                    left[0], right[0], (((0,), (0,)), ((), ())), preferred_element_type=wide
                ).astype(low)
                for left, right in pairs
            ]
            flat = [roll_blocks(grad, owner[first + i], data_size) for i, grad in enumerate(grads)]
            flat = jnp.concatenate(flat, axis=1)
            return lax.psum_scatter(flat, "dp", scatter_dimension=0, tiled=True).astype(wide)

        def spread(rows):
            return [lax.all_gather(rows, "tensor", axis=0, tiled=True)]

        def gathered_sum(parts):
            summed = lax.psum_scatter(
                parts[0].astype(low), "tensor", scatter_dimension=0, tiled=True
            )
            return summed.astype(wide)

    n_own = rms_norm(block_input)
    if rings:
        n_partner = across_tensor(n_own.astype(low))
        ring = ring_of(1, 3)
        hop = ring.hop()
    marks = jnp.stack([bucket, label], axis=1)
    marks = jnp.broadcast_to(marks[None], (data_size,) + marks.shape)
    marks = lax.all_to_all(marks, "dp", 0, 0, tiled=True).reshape(images_all, 2)
    if rings:
        marks = after(marks, hop)
        hop = ring.hop()
    cond = time_table[marks[:, 0]] + class_table[marks[:, 1]]
    cond = lax.dynamic_slice_in_dim(cond, tensor_index * head_cols, head_cols, 1)
    lifted = jax.nn.silu(cond).astype(low)
    if rings:
        lifted = after(lifted, hop, n_partner)
        hop = ring.hop(cond)
    ada = master[:, : bounds[1]].astype(low)
    row_map = lax.broadcasted_iota(jnp.int32, (6 * images_all, 6 * head_cols), 0) // images_all
    col_map = lax.broadcasted_iota(jnp.int32, (6 * images_all, 6 * head_cols), 1) // head_cols
    on_map = row_map == col_map
    lifted_maps = jnp.where(on_map, jnp.tile(lifted, (6, 6)), jnp.zeros((), low))
    partial_mod = lax.dot_general(
        lifted_maps, ada, (((1,), (1,)), ((), ())), preferred_element_type=wide
    )
    send = partial_mod.reshape(6, data_size, group_images, own_rows).transpose(1, 0, 2, 3)
    send = jnp.broadcast_to(send[:, None], (data_size, tensor_size) + send.shape[1:])
    send = send.reshape((data_size * tensor_size,) + send.shape[2:])
    if rings:
        send = after(send, hop)
        hop = ring.hop()
        ring_two = ring_of(3, 6, hop)
    got = lax.all_to_all(send, devices, 0, 0, tiled=True)
    if rings:
        got = after(got, hop)
        qkv_cols, proj_cols = matrices(ring, 1, 3)
        qkv_cols = lax.optimization_barrier(qkv_cols.T)
        ring = ring_two
        hop = ring.hop()
    got = got.reshape((data_size, tensor_size) + got.shape[1:]).sum(axis=1)
    got = jnp.roll(got, -owner[0], axis=0).transpose(2, 1, 0, 3)
    mods = got.reshape(group_images, 6, width) + vec[: 6 * width].reshape(6, width)

    mod = lax.dynamic_index_in_dim(mods, tensor_index, 0, keepdims=False)
    shift_one, scale_one, gate_one, shift_two, scale_two, gate_two = [
        mod[index][None, :] for index in range(6)
    ]
    gains = vec[6 * width :].reshape(2, HEAD_DIM)

    h_one = (n_own * (1.0 + scale_one) + shift_one).astype(low)
    if rings:
        mod_partner = lax.dynamic_index_in_dim(mods, 1 - tensor_index, 0, keepdims=False)
        h_partner = n_partner.astype(wide) * (1.0 + mod_partner[1][None]) + mod_partner[0][None]
        rows_one = [h_one, after(h_partner.astype(low), hop)]
        hop = ring.hop()
    else:
        rows_one = spread(h_one)
        qkv_cols, proj_cols = weights(1, 3)
        qkv_cols = qkv_cols.T
        w_one, w_three, w_two = weights(3, 6)
    send_two = (gate_two * cotangent).astype(low)
    back_two = spread(send_two)

    cosine, sine = rope_tables()
    kept = []
    branch_parts = []
    for part, rows in enumerate(reversed(rows_one)):
        if rings and part == 1:
            rows = after(rows, hop, branch_parts)
            roots = [
                after(side[0].transpose(1, 2, 0), hop) for side in (left_roots, right_roots)
            ]
            mats = to_matrices(*roots)
            stats = [left_stats[0].transpose(1, 2, 0), right_stats[0].transpose(1, 2, 0)]
            hop = ring.hop()
        raw = jnp.einsum("rd,cd->rc", rows, qkv_cols, preferred_element_type=wide)
        raw = raw.reshape(rows.shape[0] // PATCHES, PATCHES, 3, local_heads, HEAD_DIM)
        query_norm = rms_norm(raw[:, :, 0])
        key_norm = rms_norm(raw[:, :, 1])
        query = rotate(query_norm * gains[0], cosine, sine).astype(low)
        keys = rotate(key_norm * gains[1], cosine, sine).astype(low)
        values = raw[:, :, 2].astype(low)
        scores = jnp.einsum("gphd,gqhd->ghpq", query, keys, preferred_element_type=wide) * scale_dot
        peak = jnp.max(scores, axis=-1, keepdims=True)
        expo = jnp.exp(scores - peak)
        total = jnp.sum(expo, axis=-1, keepdims=True)
        logsum = peak + jnp.log(total)
        probs = (expo / total).astype(low)
        attended = jnp.einsum("ghpq,gqhd->gphd", probs, values, preferred_element_type=wide)
        attended = attended.astype(low).reshape(rows.shape[0], head_cols)
        kept.append((raw, query_norm, key_norm, query, keys, values, logsum, attended))
        branch_parts.append(
            jnp.einsum("rh,oh->ro", attended, proj_cols, preferred_element_type=wide)
        )
    kept.reverse()
    branch_parts.reverse()
    if rings:
        branch_one = gathered_sum(branch_parts, hop, branch_parts[0], mats)
        hop = ring.hop()
        attended_parts = lax.optimization_barrier([saved[-1] for saved in kept])
        lifted_late = after(lifted, branch_parts[0])
        lifted_maps = jnp.where(on_map, jnp.tile(lifted_late, (6, 6)), jnp.zeros((), low))
    else:
        branch_one = gathered_sum(branch_parts)
    middle = block_input + gate_one * branch_one
    n_two = rms_norm(middle)
    h_two = (n_two * (1.0 + scale_two) + shift_two).astype(low)
    rows_two = spread(h_two)
    if rings:
        rows_two[1] = after(rows_two[1], hop)
        w_one, w_three, w_two = matrices(ring, 3, 6)

    branch_parts, hidden_parts, gate_parts, up_parts, d_parts = [], [], [], [], []
    for rows, back in zip(rows_two, back_two, strict=True):
        gate_pre = jnp.dot(rows, w_one, preferred_element_type=wide)
        up_pre = jnp.dot(rows, w_three, preferred_element_type=wide)
        d_hidden = jnp.dot(back, w_two, preferred_element_type=wide)
        sigma = jax.nn.sigmoid(gate_pre)
        silu_gate = gate_pre * sigma
        hidden = (silu_gate * up_pre).astype(low)
        d_gate_pre = (d_hidden * up_pre * sigma * (1.0 + gate_pre * (1.0 - sigma))).astype(low)
        d_up_pre = (d_hidden * silu_gate).astype(low)
        hidden_parts.append(hidden)
        gate_parts.append(d_gate_pre)
        up_parts.append(d_up_pre)
        d_parts.append(
            jnp.einsum("rf,df->rd", d_gate_pre, w_one, preferred_element_type=wide)
            + jnp.einsum("rf,df->rd", d_up_pre, w_three, preferred_element_type=wide)
        )

    if rings:
        hidden_parts[0] = after(hidden_parts[0], d_parts)
        own, other = grads_mlp(
            rows_two, back_two, gate_parts, up_parts, hidden_parts, table, data_size
        )
        ring = RingScatter(own, other, True)
    else:
        grad_mlp = to_owners(
            [(rows_two, gate_parts), (rows_two, up_parts), (back_two, hidden_parts)], 3
        )
    d_h_two = gathered_sum(d_parts, own) if rings else gathered_sum(d_parts)
    if not rings:
        attended_parts = [saved[-1] for saved in kept]
    d_shift_two = jnp.sum(d_h_two, axis=0)
    d_scale_two = jnp.sum(d_h_two * n_two, axis=0)
    d_middle = cotangent + norm_back(middle, n_two, d_h_two * (1.0 + scale_two))
    d_gate_one = jnp.sum(d_middle * branch_one, axis=0)
    send_one = (gate_one * d_middle).astype(low)
    back_one = spread(send_one)
    if rings:
        hop = ring.hop()
        w_two = after(w_two, send_one)
    branch_parts = [
        jnp.einsum("rf,of->ro", hidden, w_two, preferred_element_type=wide)
        for hidden in hidden_parts
    ]
    if rings:
        back_one[0] = after(back_one[0], ring.sent, branch_parts[1])

    d_parts, raw_parts = [], []
    gain_grads = jnp.zeros((2, HEAD_DIM), wide)
    for part, (back, saved) in enumerate(zip(back_one, kept, strict=True)):
        if rings and part == 1:
            back = after(back, d_parts)
        raw, query_norm, key_norm, query, keys, values, logsum, attended = saved
        d_attended = jnp.dot(back, proj_cols, preferred_element_type=wide).astype(low)
        if rings:
            d_attended = after(d_attended, hop)
            hop = ring.hop()
        d_attended = d_attended.reshape(values.shape)
        scores = jnp.einsum("gphd,gqhd->ghpq", query, keys, preferred_element_type=wide) * scale_dot
        probs_full = jnp.exp(scores - logsum)
        d_values = jnp.einsum(
            "ghpq,gphd->gqhd", probs_full.astype(low), d_attended, preferred_element_type=wide
        )
        d_probs = jnp.einsum("gphd,gqhd->ghpq", d_attended, values, preferred_element_type=wide)
        d_scores = probs_full * (d_probs - jnp.sum(probs_full * d_probs, axis=-1, keepdims=True))
        d_scores = d_scores.astype(low)
        d_query = (
            jnp.einsum("ghpq,gqhd->gphd", d_scores, keys, preferred_element_type=wide) * scale_dot
        )
        d_keys = (
            jnp.einsum("ghpq,gphd->gqhd", d_scores, query, preferred_element_type=wide) * scale_dot
        )
        d_query_norm = rotate(d_query, cosine, -sine)
        d_key_norm = rotate(d_keys, cosine, -sine)
        gain_grads += jnp.stack(
            [
                jnp.sum(d_query_norm * query_norm, axis=(0, 1, 2)),
                jnp.sum(d_key_norm * key_norm, axis=(0, 1, 2)),
            ]
        )
        d_raw_query = norm_back(raw[:, :, 0], query_norm, d_query_norm * gains[0])
        d_raw_key = norm_back(raw[:, :, 1], key_norm, d_key_norm * gains[1])
        d_raw = jnp.stack([d_raw_query, d_raw_key, d_values], axis=2).astype(low)
        d_raw = d_raw.reshape(back.shape[0], 3 * head_cols)
        raw_parts.append(d_raw)
        d_parts.append(jnp.einsum("rc,cd->rd", d_raw, qkv_cols, preferred_element_type=wide))
    if rings:
        branch_two = gathered_sum(branch_parts, d_parts)
        held = after(raw_parts[1], hop, d_parts)
        hop = ring.hop()
        held = after(held, ring.sent)
        own, other = grads_att(
            rows_one, back_one, [raw_parts[0], held], attended_parts, table, data_size
        )
        ring_att = RingScatter(own, other, False)
        grad_mlp = ring.total()
        hop_one = ring_att.hop()
        d_h_one = gathered_sum(d_parts, own, hop, ring_att.sent)
    else:
        branch_two = gathered_sum(branch_parts)
        grad_att = to_owners([(rows_one, raw_parts), (back_one, attended_parts)], 1)
        d_h_one = gathered_sum(d_parts)
    output = middle + gate_two * branch_two
    d_gate_two = jnp.sum(cotangent * branch_two, axis=0)
    d_shift_one = jnp.sum(d_h_one, axis=0)
    d_scale_one = jnp.sum(d_h_one * n_own, axis=0)
    d_inputs = d_middle + norm_back(block_input, n_own, d_h_one * (1.0 + scale_one))

    d_mod = jnp.stack([d_shift_one, d_scale_one, d_gate_one, d_shift_two, d_scale_two, d_gate_two])
    d_mod = d_mod.reshape(6, data_size, own_rows).transpose(1, 0, 2)
    d_mod = jnp.roll(d_mod, owner[0], axis=0).reshape(data_size, 6 * own_rows)
    gain_row = jnp.broadcast_to(gain_grads.reshape(1, -1), (data_size, 2 * HEAD_DIM))
    send = jnp.concatenate([d_mod, gain_row], axis=1)
    send = jnp.broadcast_to(send[:, None], (data_size, tensor_size, send.shape[1]))
    send = send.reshape(data_size * tensor_size, send.shape[2])
    got = lax.all_to_all(send, devices, 0, 0, tiled=True)
    if rings:
        blocks_ada, blocks_att = bounds[1] // BLOCK_WIDTH, (bounds[3] - bounds[1]) // BLOCK_WIDTH
        skip = LANES - blocks_ada - blocks_att
        total = bounds[6] // BLOCK_WIDTH
        grad_mlp = after(grad_mlp, hop_one)
        hop = ring_att.hop()
        group_one = shampoo(
            [grad_mlp], [(skip, LANES, total - LANES)], master, mats, [], 1, stats=stats
        )
        got = after(got, output, group_one, hop)
        hop = ring_att.hop()
    gain_sum = jnp.sum(got[:, 6 * own_rows :], axis=0)
    d_own = got[:, : 6 * own_rows].reshape(images_all, 6, own_rows).transpose(1, 0, 2)
    row_sum = jnp.sum(d_own, axis=1).reshape(-1)
    d_own = d_own.reshape(6 * images_all, own_rows)
    grad_ada = lax.dot_general(
        d_own,
        lifted_maps.astype(wide),
        (((0,), (0,)), ((), ())),
        precision=precise,
        preferred_element_type=wide,
    )
    d_lifted = lax.dot_general(
        d_own,
        ada.astype(wide),
        (((1,), (0,)), ((), ())),
        precision=precise,
        preferred_element_type=wide,
    )
    d_lifted = jnp.where(on_map, d_lifted, 0.0).reshape(6, images_all, 6 * head_cols).sum(axis=0)
    d_lifted = sum(d_lifted[:, j * head_cols : (j + 1) * head_cols] for j in range(6))
    send = jnp.concatenate(
        [
            d_lifted.reshape(data_size, group_images * head_cols),
            jnp.broadcast_to(row_sum[None, :], (data_size, 6 * own_rows)),
        ],
        axis=1,
    )
    if rings:
        grad_ada = after(grad_ada, send, hop)
        hop = ring_att.hop()
    got = lax.all_to_all(send, "dp", 0, 0, tiled=True)
    if rings:
        early = [(0, 0, blocks_ada), (0, blocks_ada + blocks_att, LANES - blocks_ada - blocks_att)]
        part = shampoo([grad_ada, grad_mlp], early, master, mats, group_one[:3], 0)
        got = after(got, part[0], hop)
    d_lifted = jnp.sum(got[:, : group_images * head_cols], axis=0).reshape(group_images, head_cols)
    cond_here = lax.dynamic_slice_in_dim(cond, data_index * group_images, group_images, 0)
    d_cond = d_lifted * silu_slope(cond_here)
    vec_rows = got[:, group_images * head_cols :].reshape(data_size, 6, own_rows)
    vec_rows = jnp.roll(vec_rows, -owner[0], axis=0).transpose(1, 0, 2).reshape(-1)
    vec_grad = jnp.concatenate([vec_rows, gain_sum])

    if rings:
        grad_att = after(ring_att.total(), part[3])
        outs = shampoo(
            [grad_att],
            [(0, blocks_ada, blocks_att)],
            master,
            mats,
            [*part[:3], *group_one[3:]],
            0,
            stats=stats,
            early=(early, part[3:]),
        )
        grad_mine, master_new, weights_low = outs[:3]
        left_new, right_new = outs[3].transpose(2, 0, 1), outs[4].transpose(2, 0, 1)
    else:
        grad_mine = jnp.concatenate([grad_ada, grad_att, grad_mlp], axis=1)
        block_count = grad_mine.shape[1] // BLOCK_WIDTH
        pieces = grad_mine.astype(low).reshape(own_rows, block_count, BLOCK_WIDTH).transpose(1, 0, 2)
        left_new = 0.5 * left_stats[0] + 0.5 * jnp.einsum(
            "bij,bkj->bik", pieces, pieces, preferred_element_type=wide
        )
        right_new = 0.5 * right_stats[0] + 0.5 * jnp.einsum(
            "bji,bjk->bik", pieces, pieces, preferred_element_type=wide
        )
        update = jnp.einsum(
            "bij,bjk->bik", left_roots[0].astype(low), pieces, preferred_element_type=wide
        )
        update = jnp.einsum(
            "bik,bkl->bil",
            update.astype(low),
            right_roots[0].astype(low),
            preferred_element_type=wide,
        )
        update = update.transpose(1, 0, 2).reshape(own_rows, block_count * BLOCK_WIDTH)
        master_new = master - shampoo_rate * update
        weights_low = master_new.astype(low)
    tokens_all = row_count * data_size * tensor_size
    mom_new = momentum * vec_mom + vec_grad
    vec_new = vec - 0.1 / tokens_all**0.5 * mom_new
    return (
        output,
        d_inputs,
        d_cond,
        grad_mine,
        left_new[None],
        right_new[None],
        master_new,
        weights_low,
        vec_new,
        mom_new,
    )


def solution(mesh):
    placed = (
        P(("dp", "tensor"), None),
        P(("dp", "tensor"), None),
        P("dp", "tensor"),
        P("dp", "tensor", None, None),
        P("dp", "tensor", None, None),
        P("dp", "tensor", None, None),
        P("dp", "tensor", None, None),
        P(),
        P(),
        P(),
        P(),
        P("dp"),
        P("dp"),
        P(),
    )
    return jax.shard_map(
        local,
        mesh=mesh,
        in_specs=placed,
        out_specs=(
            P(("dp", "tensor"), None),
            P(("dp", "tensor"), None),
            P("dp", "tensor"),
            P("dp", "tensor"),
            P("dp", "tensor", None, None),
            P("dp", "tensor", None, None),
            P("dp", "tensor"),
            P("dp", "tensor"),
            P(),
            P(),
        ),
        check_vma=False,
    )
```

```python
import functools

import jax
import jax.numpy as jnp
from jax import lax
from jax.experimental import pallas as pl
from jax.experimental.pallas import tpu as pltpu
from jax.sharding import PartitionSpec as P

HEAD_DIM = 72
FF = 3072
PATCHES = 256
GRID = 16
BLOCK_WIDTH = 48
RING = (0, 1, 3, 5, 7, 6, 4, 2)
LANES = 128

epsilon = 1e-06
precise = lax.Precision.HIGHEST
shampoo_rate = 0.25
momentum = 0.9
low = jnp.bfloat16
wide = jnp.float32
BYTES_PER_US = 3_500_000


def lasting(microseconds):
    moved = int(microseconds * BYTES_PER_US)
    return pl.CostEstimate(flops=0, transcendentals=0, bytes_accessed=moved)


def rms_norm(values):
    return values * lax.rsqrt(jnp.mean(values * values, axis=-1, keepdims=True) + epsilon)


def norm_back(values, normed, upstream):
    factor = lax.rsqrt(jnp.mean(values * values, axis=-1, keepdims=True) + epsilon)
    return factor * (upstream - normed * jnp.mean(upstream * normed, axis=-1, keepdims=True))


def rope_tables():
    quarter = HEAD_DIM // 4
    freqs = 10000.0 ** (-jnp.arange(quarter, dtype=jnp.float32) / quarter)
    places = jnp.arange(PATCHES)
    coords = jnp.stack([places // GRID, places % GRID], axis=1).astype(jnp.float32)
    angles = coords[:, :, None] * freqs[None, None, :]
    return (jnp.cos(angles), jnp.sin(angles))


def rotate(values, cosine, sine):
    shape = values.shape
    halves = values.reshape(shape[:-1] + (2, 2, shape[-1] // 4))
    first_part = halves[..., 0, :]
    second_part = halves[..., 1, :]
    cosine = cosine[:, None]
    sine = sine[:, None]
    turned = jnp.stack(
        [first_part * cosine - second_part * sine, second_part * cosine + first_part * sine],
        axis=-2,
    )
    return turned.reshape(shape)


def roll_blocks(matrix, shift, groups):
    blocks = matrix.reshape((groups, matrix.shape[0] // groups) + matrix.shape[1:])
    return jnp.roll(blocks, shift, axis=0).reshape(matrix.shape)


def silu_slope(values):
    sigma = jax.nn.sigmoid(values)
    return sigma * (1.0 + values * (1.0 - sigma))


def ring_pairs(step):
    pairs = []
    for place, chip in enumerate(RING):
        goal = RING[(place + step) % len(RING)]
        pairs += [(chip * 2 + core, goal * 2 + core) for core in range(2)]
    return pairs


def around(value, step):
    return lax.ppermute(value, "dp", ring_pairs(step))


def across_cores(value):
    return lax.ppermute(value, "dp", [(i, i ^ 1) for i in range(2 * len(RING))])


def across_tensor(value):
    return lax.ppermute(value, "tensor", [(0, 1), (1, 0)])


def relative_order():
    rows = []
    for device in range(2 * len(RING)):
        place, core = RING.index(device // 2), device % 2
        chips = [RING[(place + offset) % len(RING)] for offset in range(len(RING))]
        rows.append([chip * 2 + core for chip in chips] + [chip * 2 + 1 - core for chip in chips])
    return jnp.array(rows, jnp.int32)


def after(value, *others):
    return lax.optimization_barrier((value, others))[0]


class RingGather:
    def __init__(self, shard):
        self.half = shard.shape[1] // 2
        self.right = self.left = shard
        self.hops = 0
        self.pieces = []
        self.keep(0, 0, shard)

    def keep(self, offset, start, piece):
        self.pieces.append((offset, start, piece))
        self.pieces.append((offset + len(RING), start, across_cores(piece)))

    def hop(self, *ready):
        self.hops += 1
        ready = (*ready, self.right, self.left)
        if self.hops < 4:
            self.right = around(after(self.right, *ready), 1)
            self.left = around(after(self.left, *ready), -1)
            self.keep(8 - self.hops, 0, self.right)
            self.keep(self.hops, 0, self.left)
        else:
            self.right = around(after(self.right[:, : self.half], *ready), 1)
            self.left = around(after(self.left[:, self.half :], *ready), -1)
            self.keep(4, 0, self.right)
            self.keep(4, self.half, self.left)
        return self.right, self.left


class RingScatter:
    def __init__(self, own, other, ahead):
        self.own = own
        self.half = own.shape[2] // 2
        self.farthest = None
        if ahead:
            self.farthest = across_cores(other[4])
            other = after(other, self.farthest)
        self.partner = across_cores(other)
        self.hops = 0

    def term(self, offset):
        partner = self.partner[offset]
        if offset == 4 and self.farthest is not None:
            partner = self.farthest
        return self.own[offset].astype(wide) + partner.astype(wide)

    def hop(self, *ready):
        half = self.half
        if self.hops == 0:
            start = self.term(4).astype(low)
            right, left = start[:, :half], start[:, half:]
        else:
            mine, other = self.term(4 - self.hops), self.term(4 + self.hops)
            right, left = self.right.astype(wide), self.left.astype(wide)
            if self.hops == 1:
                right = jnp.concatenate([mine[:, :half] + right, mine[:, half:]], axis=1)
                left = jnp.concatenate([other[:, :half], other[:, half:] + left], axis=1)
            else:
                right, left = right + mine, left + other
            right, left = right.astype(low), left.astype(low)
        self.hops += 1
        self.sent = right, left
        ready = (*ready, *self.sent)
        self.right = around(after(right, *ready), 1)
        self.left = around(after(left, *ready), -1)
        return self.right, self.left

    def total(self):
        return self.term(0) + self.right.astype(wide) + self.left.astype(wide)


def assemble(pieces, table, first, widths, blocks):
    rows = pieces[0][2].shape[0]
    starts = [sum(widths[:i]) for i in range(len(widths))]

    def body(table_ref, *refs):
        outs = refs[len(pieces) :]
        for (place, at, _), ref in zip(pieces, refs, strict=False):
            for index, (out, start, width) in enumerate(zip(outs, starts, widths, strict=True)):
                low_end = max(start, at)
                high_end = min(start + width, at + ref.shape[1])
                if low_end < high_end:
                    goal = table_ref[(first + index) * blocks + place]
                    out[goal, :, low_end - start : high_end - start] = ref[
                        :, low_end - at : high_end - at
                    ]

    whole = pl.BlockSpec(memory_space=pltpu.VMEM)
    outs = pl.pallas_call(
        body,
        in_specs=[pl.BlockSpec(memory_space=pltpu.SMEM)] + [whole for _ in pieces],
        out_specs=[whole for _ in widths],
        out_shape=[jax.ShapeDtypeStruct((blocks, rows, width), low) for width in widths],
        cost_estimate=lasting(blocks * rows * sum(widths) / 1.2e6),
        name="assemble",
    )(table, *[piece for _, _, piece in pieces])
    return [out.reshape(blocks * rows, width) for out, width in zip(outs, widths, strict=True)]


def turn(parts, flat_ref):
    at = 0
    for part in parts:
        flat_ref[:, at : at + part.shape[0]] = part[...].astype(wide).T
        at += part.shape[0]


def sort_rows(flat_ref, left_ref, table_ref, base, rows):
    for place in range(left_ref.shape[0] // rows):
        source = pl.multiple_of(table_ref[base + place] * rows, 8)
        left_ref[place * rows : (place + 1) * rows, :] = flat_ref[pl.ds(source, rows), :].astype(low)


def product_rows(left, rights, at, columns):
    total, start = None, 0
    for right in rights:
        piece = right[:, at : at + columns]
        term = jnp.dot(
            left[:, start : start + right.shape[0]], piece, preferred_element_type=wide
        )
        total = term if total is None else total + term
        start += right.shape[0]
    return total


def grads_mlp(rows_two, back_two, gates, ups, hiddens, table, blocks):
    count, width = rows_two[0].shape
    rows, cols = width // blocks, gates[0].shape[1]
    tile = 512
    steps = cols // tile

    def body(table_ref, h0, h1, b0, b1, g0, g1, u0, u1, v0, v1, own_ref, other_ref, flat, left):
        step = pl.program_id(0)

        @pl.when(step == 0)
        def _():
            turn((h0, h1), flat)
            sort_rows(flat, left, table_ref, 3 * blocks, rows)

        @pl.when(step == steps)
        def _():
            sort_rows(flat, left, table_ref, 4 * blocks, rows)

        @pl.when(step == 2 * steps)
        def _():
            turn((b0, b1), flat)
            sort_rows(flat, left, table_ref, 5 * blocks, rows)

        def work(rights):
            for side, out in enumerate((own_ref, other_ref)):
                half = left[side * (width // 2) : (side + 1) * (width // 2), :]
                total = product_rows(half, rights, 0, tile)
                out[...] = total.reshape(blocks // 2, rows, tile).astype(low)

        pl.when(step < steps)(lambda: work((g0, g1)))
        pl.when((step >= steps) & (step < 2 * steps))(lambda: work((u0, u1)))
        pl.when(step >= 2 * steps)(lambda: work((v0, v1)))

    def part_spec(first):
        return pl.BlockSpec(
            (count, tile), lambda step, table: (0, jnp.clip(step - first, 0, steps - 1))
        )

    whole = pl.BlockSpec((count, width), lambda step, table: (0, 0))
    out_spec = pl.BlockSpec((blocks // 2, rows, tile), lambda step, table: (0, 0, step))
    out = jax.ShapeDtypeStruct((blocks // 2, rows, 3 * cols), low)
    return pl.pallas_call(
        body,
        grid_spec=pltpu.PrefetchScalarGridSpec(
            num_scalar_prefetch=1,
            grid=(3 * steps,),
            in_specs=[whole] * 4
            + [part_spec(0)] * 2
            + [part_spec(steps)] * 2
            + [part_spec(2 * steps)] * 2,
            out_specs=[out_spec, out_spec],
            scratch_shapes=[
                pltpu.VMEM((width, 2 * count), wide),
                pltpu.VMEM((width, 2 * count), low),
            ],
        ),
        out_shape=[out, out],
        cost_estimate=lasting(14.7),
        name="grads_mlp",
    )(table, *rows_two, *back_two, *gates, *ups, *hiddens)


def grads_att(rows_one, back_one, raws, attendeds, table, blocks):
    count, width = rows_one[0].shape
    rows, cols = width // blocks, attendeds[0].shape[1]

    def body(table_ref, h0, h1, b0, b1, r0, r1, a0, a1, own_ref, other_ref, flat, left):
        def work(rights, at, goal):
            for side, out in enumerate((own_ref, other_ref)):
                half = left[side * (width // 2) : (side + 1) * (width // 2), :]
                total = product_rows(half, rights, at, cols)
                out[:, :, goal : goal + cols] = total.reshape(blocks // 2, rows, cols).astype(low)

        turn((h0, h1), flat)
        sort_rows(flat, left, table_ref, blocks, rows)
        for third in range(3):
            work((r0, r1), third * cols, third * cols)
        turn((b0, b1), flat)
        sort_rows(flat, left, table_ref, 2 * blocks, rows)
        work((a0, a1), 0, 3 * cols)

    whole = pl.BlockSpec(memory_space=pltpu.VMEM)
    out = jax.ShapeDtypeStruct((blocks // 2, rows, 4 * cols), low)
    return pl.pallas_call(
        body,
        in_specs=[pl.BlockSpec(memory_space=pltpu.SMEM)] + [whole] * 8,
        out_specs=[whole, whole],
        out_shape=[out, out],
        scratch_shapes=[
            pltpu.VMEM((width, 2 * count), wide),
            pltpu.VMEM((width, 2 * count), low),
        ],
        cost_estimate=lasting(8.8),
        name="grads_att",
    )(table, *rows_one, *back_one, *raws, *attendeds)


def to_matrices(left_roots, right_roots):
    count = left_roots.shape[2]

    def body(left_ref, right_ref, left_out, right_out, scratch):
        for source, goal in ((left_ref, left_out), (right_ref, right_out)):
            size = source.shape[0]

            @pl.loop(0, size, unroll=8)
            def _(i):
                slab = source[i]
                slab = jnp.concatenate([slab, jnp.zeros((LANES - size, LANES), wide)], axis=0)
                scratch[pl.ds(i, LANES, stride=size), :] = slab.T

            @pl.loop(0, LANES, unroll=8)
            def _(b):
                start = pl.multiple_of(b * size, 8)
                goal[b] = scratch[pl.ds(start, size), :size].astype(low)

    def sides(of):
        return [of(left_roots.shape[0]), of(right_roots.shape[0])]

    return pl.pallas_call(
        body,
        grid=(pl.cdiv(count, LANES),),
        in_specs=sides(lambda size: pl.BlockSpec((size, size, LANES), lambda g: (0, 0, g))),
        out_specs=sides(lambda size: pl.BlockSpec((LANES, size, size), lambda g: (g, 0, 0))),
        out_shape=sides(lambda size: jax.ShapeDtypeStruct((count, size, size), low)),
        scratch_shapes=[pltpu.VMEM((LANES * left_roots.shape[0], LANES), wide)],
        cost_estimate=lasting(11.5),
        name="to_matrices",
    )(left_roots, right_roots)


def shampoo(sources, spans, master, mats, filled, group, stats=None, early=None):
    rows, cols = master.shape
    chunk = 8
    wide_cols = chunk * BLOCK_WIDTH
    start = group * LANES
    starts = [0]
    for _, _, number in spans:
        starts.append(starts[-1] + number // chunk)
    steps = starts[-1]
    early_spans, early_sums = early if early else ([], [])
    sizes = (rows, BLOCK_WIDTH)

    def place(step):
        index = step + spans[0][1] // chunk
        for at, (_, first, _) in zip(starts[1:], spans[1:]):
            index = jnp.where(step >= at, step - at + first // chunk, index)
        return index

    def body(*refs):
        source_refs, refs = refs[: len(sources)], refs[len(sources) :]
        master_ref, left_mat, right_mat = refs[:3]
        step = pl.program_id(0)
        if stats:
            stat_refs = refs[3:5]
            early_refs = refs[5 : 5 + len(early_sums)]
            tail = 4 if early_sums else 2
            grad_out, master_out, low_out, left_out, right_out = refs[-5 - tail : -tail]
            sums = refs[-tail:][:2]
            copies = []
            for sum_ref, early_ref, size, sem in zip(
                sums, early_refs, sizes, refs[-tail:][2:], strict=False
            ):
                at = 0
                for index, (_, first, number) in enumerate(early_spans):
                    copies.append(
                        pltpu.make_async_copy(
                            early_ref.at[pl.ds(at * size, number * size)],
                            sum_ref.at[pl.ds((first - start) * size, number * size)],
                            sem.at[index],
                        )
                    )
                    at += number

            @pl.when(step == 0)
            def _():
                for copy in copies:
                    copy.start()
        else:
            grad_out, master_out, low_out = refs[-5:-2]
            sums = refs[-2:]
        grad = source_refs[0][...]
        for at, ref in zip(starts[1:], source_refs[1:]):
            grad = jnp.where(step >= at, ref[...], grad)
        grad_out[...] = grad
        turned = grad.T.astype(low)
        grad = grad.astype(low)
        base = place(step) * chunk - start if stats else 0
        updates = []
        for b in range(chunk):
            side = turned[b * BLOCK_WIDTH : (b + 1) * BLOCK_WIDTH, :]
            upright = grad[:, b * BLOCK_WIDTH : (b + 1) * BLOCK_WIDTH]
            at = base + b
            if stats:
                left_rows = pl.ds(pl.multiple_of(at * rows, 8), rows)
                right_rows = pl.ds(pl.multiple_of(at * BLOCK_WIDTH, 8), BLOCK_WIDTH)
            else:
                left_rows = slice(b * rows, (b + 1) * rows)
                right_rows = slice(b * BLOCK_WIDTH, (b + 1) * BLOCK_WIDTH)
            sums[0][left_rows, :rows] = jnp.dot(upright, side, preferred_element_type=wide)
            sums[1][right_rows, :BLOCK_WIDTH] = lax.dot_general(
                side, side, (((1,), (1,)), ((), ())), preferred_element_type=wide
            )
            half = jnp.dot(right_mat[b], side, preferred_element_type=wide).astype(low)
            updates.append(jnp.dot(half, left_mat[b], preferred_element_type=wide))
        new = master_ref[...] - shampoo_rate * jnp.concatenate(updates, axis=0).T
        master_out[...] = new
        low_out[...] = new.astype(low)
        if stats:

            @pl.when(step == steps - 1)
            def _():
                for copy in copies:
                    copy.wait()
                for sum_ref, stat_ref, out in zip(
                    sums, stat_refs, (left_out, right_out), strict=True
                ):
                    size = out.shape[0]
                    here = min(LANES, stats[0].shape[2] - start)

                    @pl.loop(0, size, unroll=8)
                    def _(i):
                        slab = sum_ref[pl.ds(i, here, stride=size), :].T
                        out[i, :, :here] = 0.5 * stat_ref[i, :, :here] + 0.5 * slab[:size]

    def source_spec(index):
        first = spans[index][0] // chunk
        count = spans[index][2] // chunk

        def at(step):
            return (0, first + jnp.clip(step - starts[index], 0, count - 1))

        return pl.BlockSpec((rows, wide_cols), at)

    def lanes_spec(size):
        return pl.BlockSpec((size, size, LANES), lambda step: (0, 0, group))

    def mats_spec(size):
        return pl.BlockSpec((chunk, size, size), lambda step: (place(step), 0, 0))

    def sums_spec(size):
        return pl.BlockSpec((chunk * size, LANES), lambda step: (step, 0))

    own = pl.BlockSpec((rows, wide_cols), lambda step: (0, place(step)))
    anywhere = pl.BlockSpec(memory_space=pl.ANY)
    in_specs = [source_spec(i) for i in range(len(sources))] + [own] + [mats_spec(s) for s in sizes]
    out_specs = [own, own, own]
    outs = [jax.ShapeDtypeStruct((rows, cols), kind) for kind in (wide, wide, low)]
    scratch = []
    if stats:
        in_specs += [lanes_spec(s) for s in sizes] + [anywhere for _ in early_sums]
        out_specs += [lanes_spec(s) for s in sizes]
        outs += [jax.ShapeDtypeStruct(stat.shape, wide) for stat in stats]
        scratch = [pltpu.VMEM((LANES * s, LANES), wide) for s in sizes]
        if early_sums:
            scratch += [pltpu.SemaphoreType.DMA((len(early_spans),)) for _ in sizes]
    else:
        out_specs += [sums_spec(s) for s in sizes]
        outs += [jax.ShapeDtypeStruct((steps * chunk * s, LANES), wide) for s in sizes]
    operands = [*sources, master, *mats, *(stats or []), *early_sums]
    number = steps * chunk
    return pl.pallas_call(
        body,
        grid=(steps,),
        in_specs=in_specs + [anywhere for _ in filled],
        out_specs=out_specs,
        out_shape=outs,
        scratch_shapes=scratch,
        input_output_aliases={len(operands) + i: i for i in range(len(filled))},
        cost_estimate=lasting(number * 0.25),
        name="shampoo",
    )(*operands, *filled)


def local(
    block_input,
    cotangent,
    master,
    left_stats,
    right_stats,
    left_roots,
    right_roots,
    vec,
    vec_mom,
    time_table,
    class_table,
    bucket,
    label,
    owner,
):
    tensor_size = lax.axis_size("tensor")
    data_size = lax.axis_size("dp")
    rings = tensor_size == 2 and data_size == 2 * len(RING)
    tensor_index = lax.axis_index("tensor")
    data_index = lax.axis_index("dp")
    row_count, width = block_input.shape
    own_rows = master.shape[0]
    head_cols = width // tensor_size
    local_heads = head_cols // HEAD_DIM
    hidden_cols = FF // tensor_size
    group_images = row_count // PATCHES * tensor_size
    images_all = group_images * data_size
    scale_dot = HEAD_DIM ** (-0.5)
    widths = [6 * head_cols, 3 * head_cols, head_cols, hidden_cols, hidden_cols, hidden_cols]
    bounds = [0]
    for piece_width in widths:
        bounds.append(bounds[-1] + piece_width)
    devices = ("dp", "tensor")

    if rings:
        order = lax.dynamic_index_in_dim(relative_order(), data_index, 0, keepdims=False)
        table = ((order[None, :] - owner[:, None]) % data_size).reshape(-1)

        def ring_of(first, last, *ready):
            return RingGather(after(master[:, bounds[first] : bounds[last]].astype(low), *ready))

        def matrices(ring, first, last):
            return assemble(ring.pieces, table, first, widths[first:last], data_size)

        def spread(rows):
            return [rows, across_tensor(rows)]

        def gathered_sum(parts, *before):
            got = across_tensor(parts[1].astype(low))
            return parts[0] + after(got, *before).astype(wide)
    else:

        def weights(first, last):
            own = master[:, bounds[first] : bounds[last]].astype(low)
            gathered = lax.all_gather(own, "dp", axis=0, tiled=True)
            natural, at = [], 0
            for index in range(first, last):
                piece = gathered[:, at : at + widths[index]]
                natural.append(roll_blocks(piece, -owner[index], data_size))
                at += widths[index]
            return natural

        def to_owners(pairs, first):
            grads = [
                lax.dot_general(
                    left[0], right[0], (((0,), (0,)), ((), ())), preferred_element_type=wide
                ).astype(low)
                for left, right in pairs
            ]
            flat = [roll_blocks(grad, owner[first + i], data_size) for i, grad in enumerate(grads)]
            flat = jnp.concatenate(flat, axis=1)
            return lax.psum_scatter(flat, "dp", scatter_dimension=0, tiled=True).astype(wide)

        def spread(rows):
            return [lax.all_gather(rows, "tensor", axis=0, tiled=True)]

        def gathered_sum(parts):
            summed = lax.psum_scatter(
                parts[0].astype(low), "tensor", scatter_dimension=0, tiled=True
            )
            return summed.astype(wide)

    n_own = rms_norm(block_input)
    if rings:
        n_partner = across_tensor(n_own.astype(low))
        ring = ring_of(1, 3)
        hop = ring.hop()
    marks = jnp.stack([bucket, label], axis=1)
    marks = jnp.broadcast_to(marks[None], (data_size,) + marks.shape)
    marks = lax.all_to_all(marks, "dp", 0, 0, tiled=True).reshape(images_all, 2)
    if rings:
        marks = after(marks, hop)
        hop = ring.hop()
    cond = time_table[marks[:, 0]] + class_table[marks[:, 1]]
    cond = lax.dynamic_slice_in_dim(cond, tensor_index * head_cols, head_cols, 1)
    lifted = jax.nn.silu(cond).astype(low)
    if rings:
        lifted = after(lifted, hop, n_partner)
        hop = ring.hop(cond)
        ring_two = ring_of(3, 6, lifted)
        hop_two = ring_two.hop()
    ada = master[:, : bounds[1]].astype(low)
    row_map = lax.broadcasted_iota(jnp.int32, (6 * images_all, 6 * head_cols), 0) // images_all
    col_map = lax.broadcasted_iota(jnp.int32, (6 * images_all, 6 * head_cols), 1) // head_cols
    on_map = row_map == col_map
    lifted_maps = jnp.where(on_map, jnp.tile(lifted, (6, 6)), jnp.zeros((), low))
    partial_mod = lax.dot_general(
        lifted_maps, ada, (((1,), (1,)), ((), ())), preferred_element_type=wide
    )
    send = partial_mod.reshape(6, data_size, group_images, own_rows).transpose(1, 0, 2, 3)
    send = jnp.broadcast_to(send[:, None], (data_size, tensor_size) + send.shape[1:])
    send = send.reshape((data_size * tensor_size,) + send.shape[2:])
    got = lax.all_to_all(send, devices, 0, 0, tiled=True)
    if rings:
        got = after(got, hop, hop_two)
        ring.hop()
        qkv_cols, proj_cols = matrices(ring, 1, 3)
        qkv_cols = lax.optimization_barrier(qkv_cols.T)
        ring = ring_two
        hop = ring.hop()
    got = got.reshape((data_size, tensor_size) + got.shape[1:]).sum(axis=1)
    got = jnp.roll(got, -owner[0], axis=0).transpose(2, 1, 0, 3)
    mods = got.reshape(group_images, 6, width) + vec[: 6 * width].reshape(6, width)

    mod = lax.dynamic_index_in_dim(mods, tensor_index, 0, keepdims=False)
    shift_one, scale_one, gate_one, shift_two, scale_two, gate_two = [
        mod[index][None, :] for index in range(6)
    ]
    gains = vec[6 * width :].reshape(2, HEAD_DIM)

    h_one = (n_own * (1.0 + scale_one) + shift_one).astype(low)
    if rings:
        mod_partner = lax.dynamic_index_in_dim(mods, 1 - tensor_index, 0, keepdims=False)
        h_partner = n_partner.astype(wide) * (1.0 + mod_partner[1][None]) + mod_partner[0][None]
        rows_one = [h_one, h_partner.astype(low)]
    else:
        rows_one = spread(h_one)
        qkv_cols, proj_cols = weights(1, 3)
        qkv_cols = qkv_cols.T
        w_one, w_three, w_two = weights(3, 6)
    send_two = (gate_two * cotangent).astype(low)
    back_two = spread(send_two)

    cosine, sine = rope_tables()
    kept = []
    branch_parts = []
    for part, rows in enumerate(reversed(rows_one)):
        if rings and part == 1:
            rows = after(rows, hop, branch_parts)
            roots = [
                after(side[0].transpose(1, 2, 0), hop) for side in (left_roots, right_roots)
            ]
            mats = to_matrices(*roots)
            stats = [left_stats[0].transpose(1, 2, 0), right_stats[0].transpose(1, 2, 0)]
            hop = ring.hop()
        raw = jnp.einsum("rd,cd->rc", rows, qkv_cols, preferred_element_type=wide)
        raw = raw.reshape(rows.shape[0] // PATCHES, PATCHES, 3, local_heads, HEAD_DIM)
        query_norm = rms_norm(raw[:, :, 0])
        key_norm = rms_norm(raw[:, :, 1])
        query = rotate(query_norm * gains[0], cosine, sine).astype(low)
        keys = rotate(key_norm * gains[1], cosine, sine).astype(low)
        values = raw[:, :, 2].astype(low)
        scores = jnp.einsum("gphd,gqhd->ghpq", query, keys, preferred_element_type=wide) * scale_dot
        peak = jnp.max(scores, axis=-1, keepdims=True)
        expo = jnp.exp(scores - peak)
        total = jnp.sum(expo, axis=-1, keepdims=True)
        logsum = peak + jnp.log(total)
        probs = (expo / total).astype(low)
        attended = jnp.einsum("ghpq,gqhd->gphd", probs, values, preferred_element_type=wide)
        attended = attended.astype(low).reshape(rows.shape[0], head_cols)
        kept.append((raw, query_norm, key_norm, query, keys, values, logsum, attended))
        branch_parts.append(
            jnp.einsum("rh,oh->ro", attended, proj_cols, preferred_element_type=wide)
        )
    kept.reverse()
    branch_parts.reverse()
    if rings:
        branch_one = gathered_sum(branch_parts, hop, branch_parts[0], mats)
        hop = ring.hop()
        attended_parts = lax.optimization_barrier([saved[-1] for saved in kept])
    else:
        branch_one = gathered_sum(branch_parts)
    middle = block_input + gate_one * branch_one
    n_two = rms_norm(middle)
    h_two = (n_two * (1.0 + scale_two) + shift_two).astype(low)
    rows_two = spread(h_two)
    if rings:
        rows_two[1] = after(rows_two[1], hop)
        w_one, w_three, w_two = matrices(ring, 3, 6)

    branch_parts, hidden_parts, gate_parts, up_parts, d_parts = [], [], [], [], []
    for rows, back in zip(rows_two, back_two, strict=True):
        gate_pre = jnp.dot(rows, w_one, preferred_element_type=wide)
        up_pre = jnp.dot(rows, w_three, preferred_element_type=wide)
        d_hidden = jnp.dot(back, w_two, preferred_element_type=wide)
        sigma = jax.nn.sigmoid(gate_pre)
        silu_gate = gate_pre * sigma
        hidden = (silu_gate * up_pre).astype(low)
        d_gate_pre = (d_hidden * up_pre * sigma * (1.0 + gate_pre * (1.0 - sigma))).astype(low)
        d_up_pre = (d_hidden * silu_gate).astype(low)
        hidden_parts.append(hidden)
        gate_parts.append(d_gate_pre)
        up_parts.append(d_up_pre)
        d_parts.append(
            jnp.einsum("rf,df->rd", d_gate_pre, w_one, preferred_element_type=wide)
            + jnp.einsum("rf,df->rd", d_up_pre, w_three, preferred_element_type=wide)
        )

    if rings:
        hidden_parts[0] = after(hidden_parts[0], d_parts)
        own, other = grads_mlp(
            rows_two, back_two, gate_parts, up_parts, hidden_parts, table, data_size
        )
        ring = RingScatter(own, other, True)
    else:
        grad_mlp = to_owners(
            [(rows_two, gate_parts), (rows_two, up_parts), (back_two, hidden_parts)], 3
        )
    d_h_two = gathered_sum(d_parts, own) if rings else gathered_sum(d_parts)
    if not rings:
        attended_parts = [saved[-1] for saved in kept]
    d_shift_two = jnp.sum(d_h_two, axis=0)
    d_scale_two = jnp.sum(d_h_two * n_two, axis=0)
    d_middle = cotangent + norm_back(middle, n_two, d_h_two * (1.0 + scale_two))
    d_gate_one = jnp.sum(d_middle * branch_one, axis=0)
    send_one = (gate_one * d_middle).astype(low)
    back_one = spread(send_one)
    if rings:
        hop = ring.hop()
        w_two = after(w_two, send_one)
    branch_parts = [
        jnp.einsum("rf,of->ro", hidden, w_two, preferred_element_type=wide)
        for hidden in hidden_parts
    ]
    if rings:
        back_one[0] = after(back_one[0], ring.sent, branch_parts[1])
        branch_got = across_tensor(branch_parts[1].astype(low))

    d_parts, raw_parts = [], []
    gain_grads = jnp.zeros((2, HEAD_DIM), wide)
    for part, (back, saved) in enumerate(zip(back_one, kept, strict=True)):
        if rings and part == 1:
            back = after(back, d_parts, branch_got)
        raw, query_norm, key_norm, query, keys, values, logsum, attended = saved
        d_attended = jnp.dot(back, proj_cols, preferred_element_type=wide).astype(low)
        if rings:
            d_attended = after(d_attended, hop)
            hop = ring.hop()
        d_attended = d_attended.reshape(values.shape)
        scores = jnp.einsum("gphd,gqhd->ghpq", query, keys, preferred_element_type=wide) * scale_dot
        probs_full = jnp.exp(scores - logsum)
        d_values = jnp.einsum(
            "ghpq,gphd->gqhd", probs_full.astype(low), d_attended, preferred_element_type=wide
        )
        d_probs = jnp.einsum("gphd,gqhd->ghpq", d_attended, values, preferred_element_type=wide)
        d_scores = probs_full * (d_probs - jnp.sum(probs_full * d_probs, axis=-1, keepdims=True))
        d_scores = d_scores.astype(low)
        d_query = (
            jnp.einsum("ghpq,gqhd->gphd", d_scores, keys, preferred_element_type=wide) * scale_dot
        )
        d_keys = (
            jnp.einsum("ghpq,gphd->gqhd", d_scores, query, preferred_element_type=wide) * scale_dot
        )
        d_query_norm = rotate(d_query, cosine, -sine)
        d_key_norm = rotate(d_keys, cosine, -sine)
        gain_grads += jnp.stack(
            [
                jnp.sum(d_query_norm * query_norm, axis=(0, 1, 2)),
                jnp.sum(d_key_norm * key_norm, axis=(0, 1, 2)),
            ]
        )
        d_raw_query = norm_back(raw[:, :, 0], query_norm, d_query_norm * gains[0])
        d_raw_key = norm_back(raw[:, :, 1], key_norm, d_key_norm * gains[1])
        d_raw = jnp.stack([d_raw_query, d_raw_key, d_values], axis=2).astype(low)
        d_raw = d_raw.reshape(back.shape[0], 3 * head_cols)
        raw_parts.append(d_raw)
        d_parts.append(jnp.einsum("rc,cd->rd", d_raw, qkv_cols, preferred_element_type=wide))
    if rings:
        held = after(raw_parts[1], hop, d_parts)
        hop = ring.hop()
        held = after(held, ring.sent)
        own, other = grads_att(
            rows_one, back_one, [raw_parts[0], held], attended_parts, table, data_size
        )
        ring_att = RingScatter(own, other, False)
        grad_mlp = ring.total()
        hop_one = ring_att.hop()
        d_h_one = gathered_sum(d_parts, own, hop)
        branch_two = after(branch_parts[0] , d_h_one) + branch_got.astype(wide)
        lifted_late = after(lifted, d_h_one)
        lifted_maps = jnp.where(on_map, jnp.tile(lifted_late, (6, 6)), jnp.zeros((), low))
    else:
        branch_two = gathered_sum(branch_parts)
        grad_att = to_owners([(rows_one, raw_parts), (back_one, attended_parts)], 1)
        d_h_one = gathered_sum(d_parts)
    output = middle + gate_two * branch_two
    d_gate_two = jnp.sum(cotangent * branch_two, axis=0)
    d_shift_one = jnp.sum(d_h_one, axis=0)
    d_scale_one = jnp.sum(d_h_one * n_own, axis=0)
    d_inputs = d_middle + norm_back(block_input, n_own, d_h_one * (1.0 + scale_one))

    d_mod = jnp.stack([d_shift_one, d_scale_one, d_gate_one, d_shift_two, d_scale_two, d_gate_two])
    d_mod = d_mod.reshape(6, data_size, own_rows).transpose(1, 0, 2)
    d_mod = jnp.roll(d_mod, owner[0], axis=0).reshape(data_size, 6 * own_rows)
    gain_row = jnp.broadcast_to(gain_grads.reshape(1, -1), (data_size, 2 * HEAD_DIM))
    send = jnp.concatenate([d_mod, gain_row], axis=1)
    send = jnp.broadcast_to(send[:, None], (data_size, tensor_size, send.shape[1]))
    send = send.reshape(data_size * tensor_size, send.shape[2])
    got = lax.all_to_all(send, devices, 0, 0, tiled=True)
    if rings:
        blocks_ada, blocks_att = bounds[1] // BLOCK_WIDTH, (bounds[3] - bounds[1]) // BLOCK_WIDTH
        skip = LANES - blocks_ada - blocks_att
        total = bounds[6] // BLOCK_WIDTH
        grad_mlp = after(grad_mlp, hop_one)
        hop = ring_att.hop()
        group_one = shampoo(
            [grad_mlp], [(skip, LANES, total - LANES)], master, mats, [], 1, stats=stats
        )
        got = after(got, output, group_one, hop)
        hop = ring_att.hop()
    gain_sum = jnp.sum(got[:, 6 * own_rows :], axis=0)
    d_own = got[:, : 6 * own_rows].reshape(images_all, 6, own_rows).transpose(1, 0, 2)
    row_sum = jnp.sum(d_own, axis=1).reshape(-1)
    d_own = d_own.reshape(6 * images_all, own_rows)
    grad_ada = lax.dot_general(
        d_own,
        lifted_maps.astype(wide),
        (((0,), (0,)), ((), ())),
        precision=precise,
        preferred_element_type=wide,
    )
    d_lifted = lax.dot_general(
        d_own,
        ada.astype(wide),
        (((1,), (0,)), ((), ())),
        precision=precise,
        preferred_element_type=wide,
    )
    d_lifted = jnp.where(on_map, d_lifted, 0.0).reshape(6, images_all, 6 * head_cols).sum(axis=0)
    d_lifted = sum(d_lifted[:, j * head_cols : (j + 1) * head_cols] for j in range(6))
    send = jnp.concatenate(
        [
            d_lifted.reshape(data_size, group_images * head_cols),
            jnp.broadcast_to(row_sum[None, :], (data_size, 6 * own_rows)),
        ],
        axis=1,
    )
    if rings:
        grad_ada = after(grad_ada, send, hop)
        hop = ring_att.hop()
    got = lax.all_to_all(send, "dp", 0, 0, tiled=True)
    if rings:
        early = [(0, 0, blocks_ada), (0, blocks_ada + blocks_att, LANES - blocks_ada - blocks_att)]
        part = shampoo([grad_ada, grad_mlp], early, master, mats, group_one[:3], 0)
        got = after(got, part[0], hop)
    d_lifted = jnp.sum(got[:, : group_images * head_cols], axis=0).reshape(group_images, head_cols)
    cond_here = lax.dynamic_slice_in_dim(cond, data_index * group_images, group_images, 0)
    d_cond = d_lifted * silu_slope(cond_here)
    vec_rows = got[:, group_images * head_cols :].reshape(data_size, 6, own_rows)
    vec_rows = jnp.roll(vec_rows, -owner[0], axis=0).transpose(1, 0, 2).reshape(-1)
    vec_grad = jnp.concatenate([vec_rows, gain_sum])

    if rings:
        grad_att = after(ring_att.total(), part[3])
        outs = shampoo(
            [grad_att],
            [(0, blocks_ada, blocks_att)],
            master,
            mats,
            [*part[:3], *group_one[3:]],
            0,
            stats=stats,
            early=(early, part[3:]),
        )
        grad_mine, master_new, weights_low = outs[:3]
        left_new, right_new = outs[3].transpose(2, 0, 1), outs[4].transpose(2, 0, 1)
    else:
        grad_mine = jnp.concatenate([grad_ada, grad_att, grad_mlp], axis=1)
        block_count = grad_mine.shape[1] // BLOCK_WIDTH
        pieces = grad_mine.astype(low).reshape(own_rows, block_count, BLOCK_WIDTH).transpose(1, 0, 2)
        left_new = 0.5 * left_stats[0] + 0.5 * jnp.einsum(
            "bij,bkj->bik", pieces, pieces, preferred_element_type=wide
        )
        right_new = 0.5 * right_stats[0] + 0.5 * jnp.einsum(
            "bji,bjk->bik", pieces, pieces, preferred_element_type=wide
        )
        update = jnp.einsum(
            "bij,bjk->bik", left_roots[0].astype(low), pieces, preferred_element_type=wide
        )
        update = jnp.einsum(
            "bik,bkl->bil",
            update.astype(low),
            right_roots[0].astype(low),
            preferred_element_type=wide,
        )
        update = update.transpose(1, 0, 2).reshape(own_rows, block_count * BLOCK_WIDTH)
        master_new = master - shampoo_rate * update
        weights_low = master_new.astype(low)
    tokens_all = row_count * data_size * tensor_size
    mom_new = momentum * vec_mom + vec_grad
    vec_new = vec - 0.1 / tokens_all**0.5 * mom_new
    return (
        output,
        d_inputs,
        d_cond,
        grad_mine,
        left_new[None],
        right_new[None],
        master_new,
        weights_low,
        vec_new,
        mom_new,
    )


def solution(mesh):
    placed = (
        P(("dp", "tensor"), None),
        P(("dp", "tensor"), None),
        P("dp", "tensor"),
        P("dp", "tensor", None, None),
        P("dp", "tensor", None, None),
        P("dp", "tensor", None, None),
        P("dp", "tensor", None, None),
        P(),
        P(),
        P(),
        P(),
        P("dp"),
        P("dp"),
        P(),
    )
    return jax.shard_map(
        local,
        mesh=mesh,
        in_specs=placed,
        out_specs=(
            P(("dp", "tensor"), None),
            P(("dp", "tensor"), None),
            P("dp", "tensor"),
            P("dp", "tensor"),
            P("dp", "tensor", None, None),
            P("dp", "tensor", None, None),
            P("dp", "tensor"),
            P("dp", "tensor"),
            P(),
            P(),
        ),
        check_vma=False,
    )
```

```python
import functools

import jax
import jax.numpy as jnp
from jax import lax
from jax.experimental import pallas as pl
from jax.experimental.pallas import tpu as pltpu
from jax.sharding import PartitionSpec as P

HEAD_DIM = 72
FF = 3072
PATCHES = 256
GRID = 16
BLOCK_WIDTH = 48
RING = (0, 1, 3, 5, 7, 6, 4, 2)
LANES = 128

epsilon = 1e-06
precise = lax.Precision.HIGHEST
shampoo_rate = 0.25
momentum = 0.9
low = jnp.bfloat16
wide = jnp.float32
BYTES_PER_US = 3_500_000


def lasting(microseconds):
    moved = int(microseconds * BYTES_PER_US)
    return pl.CostEstimate(flops=0, transcendentals=0, bytes_accessed=moved)


def rms_norm(values):
    return values * lax.rsqrt(jnp.mean(values * values, axis=-1, keepdims=True) + epsilon)


def norm_back(values, normed, upstream):
    factor = lax.rsqrt(jnp.mean(values * values, axis=-1, keepdims=True) + epsilon)
    return factor * (upstream - normed * jnp.mean(upstream * normed, axis=-1, keepdims=True))


def rope_tables():
    quarter = HEAD_DIM // 4
    freqs = 10000.0 ** (-jnp.arange(quarter, dtype=jnp.float32) / quarter)
    places = jnp.arange(PATCHES)
    coords = jnp.stack([places // GRID, places % GRID], axis=1).astype(jnp.float32)
    angles = coords[:, :, None] * freqs[None, None, :]
    return (jnp.cos(angles), jnp.sin(angles))


def rotate(values, cosine, sine):
    shape = values.shape
    halves = values.reshape(shape[:-1] + (2, 2, shape[-1] // 4))
    first_part = halves[..., 0, :]
    second_part = halves[..., 1, :]
    cosine = cosine[:, None]
    sine = sine[:, None]
    turned = jnp.stack(
        [first_part * cosine - second_part * sine, second_part * cosine + first_part * sine],
        axis=-2,
    )
    return turned.reshape(shape)


def roll_blocks(matrix, shift, groups):
    blocks = matrix.reshape((groups, matrix.shape[0] // groups) + matrix.shape[1:])
    return jnp.roll(blocks, shift, axis=0).reshape(matrix.shape)


def silu_slope(values):
    sigma = jax.nn.sigmoid(values)
    return sigma * (1.0 + values * (1.0 - sigma))


def ring_pairs(step):
    pairs = []
    for place, chip in enumerate(RING):
        goal = RING[(place + step) % len(RING)]
        pairs += [(chip * 2 + core, goal * 2 + core) for core in range(2)]
    return pairs


def around(value, step):
    return lax.ppermute(value, "dp", ring_pairs(step))


def across_cores(value):
    return lax.ppermute(value, "dp", [(i, i ^ 1) for i in range(2 * len(RING))])


def across_tensor(value):
    return lax.ppermute(value, "tensor", [(0, 1), (1, 0)])


def relative_order():
    rows = []
    for device in range(2 * len(RING)):
        place, core = RING.index(device // 2), device % 2
        chips = [RING[(place + offset) % len(RING)] for offset in range(len(RING))]
        rows.append([chip * 2 + core for chip in chips] + [chip * 2 + 1 - core for chip in chips])
    return jnp.array(rows, jnp.int32)


def after(value, *others):
    return lax.optimization_barrier((value, others))[0]


class RingGather:
    def __init__(self, shard):
        self.half = shard.shape[1] // 2
        self.right = self.left = shard
        self.hops = 0
        self.pieces = []
        self.keep(0, 0, shard)

    def keep(self, offset, start, piece):
        self.pieces.append((offset, start, piece))
        self.pieces.append((offset + len(RING), start, across_cores(piece)))

    def hop(self, *ready):
        self.hops += 1
        ready = (*ready, self.right, self.left)
        if self.hops < 4:
            self.right = around(after(self.right, *ready), 1)
            self.left = around(after(self.left, *ready), -1)
            self.keep(8 - self.hops, 0, self.right)
            self.keep(self.hops, 0, self.left)
        else:
            self.right = around(after(self.right[:, : self.half], *ready), 1)
            self.left = around(after(self.left[:, self.half :], *ready), -1)
            self.keep(4, 0, self.right)
            self.keep(4, self.half, self.left)
        return self.right, self.left


class RingScatter:
    def __init__(self, own, other, ahead):
        self.own = own
        self.half = own.shape[2] // 2
        self.farthest = None
        if ahead:
            self.farthest = across_cores(other[4])
            other = after(other, self.farthest)
        self.partner = across_cores(other)
        self.hops = 0

    def term(self, offset):
        partner = self.partner[offset]
        if offset == 4 and self.farthest is not None:
            partner = self.farthest
        return self.own[offset].astype(wide) + partner.astype(wide)

    def hop(self, *ready):
        half = self.half
        if self.hops == 0:
            start = self.term(4).astype(low)
            right, left = start[:, :half], start[:, half:]
        else:
            mine, other = self.term(4 - self.hops), self.term(4 + self.hops)
            right, left = self.right.astype(wide), self.left.astype(wide)
            if self.hops == 1:
                right = jnp.concatenate([mine[:, :half] + right, mine[:, half:]], axis=1)
                left = jnp.concatenate([other[:, :half], other[:, half:] + left], axis=1)
            else:
                right, left = right + mine, left + other
            right, left = right.astype(low), left.astype(low)
        self.hops += 1
        self.sent = right, left
        ready = (*ready, *self.sent)
        self.right = around(after(right, *ready), 1)
        self.left = around(after(left, *ready), -1)
        return self.right, self.left

    def total(self):
        return self.term(0) + self.right.astype(wide) + self.left.astype(wide)


def assemble(pieces, table, first, widths, blocks):
    rows = pieces[0][2].shape[0]
    starts = [sum(widths[:i]) for i in range(len(widths))]

    def body(table_ref, *refs):
        outs = refs[len(pieces) :]
        for (place, at, _), ref in zip(pieces, refs, strict=False):
            for index, (out, start, width) in enumerate(zip(outs, starts, widths, strict=True)):
                low_end = max(start, at)
                high_end = min(start + width, at + ref.shape[1])
                if low_end < high_end:
                    goal = table_ref[(first + index) * blocks + place]
                    out[goal, :, low_end - start : high_end - start] = ref[
                        :, low_end - at : high_end - at
                    ]

    whole = pl.BlockSpec(memory_space=pltpu.VMEM)
    outs = pl.pallas_call(
        body,
        in_specs=[pl.BlockSpec(memory_space=pltpu.SMEM)] + [whole for _ in pieces],
        out_specs=[whole for _ in widths],
        out_shape=[jax.ShapeDtypeStruct((blocks, rows, width), low) for width in widths],
        cost_estimate=lasting(blocks * rows * sum(widths) / 1.2e6),
        compiler_params=pltpu.CompilerParams(vmem_limit_bytes=26 * 2**20),
        name="assemble",
    )(table, *[piece for _, _, piece in pieces])
    return [out.reshape(blocks * rows, width) for out, width in zip(outs, widths, strict=True)]


def turn(parts, flat_ref):
    at = 0
    for part in parts:
        flat_ref[:, at : at + part.shape[0]] = part[...].astype(wide).T
        at += part.shape[0]


def sort_rows(flat_ref, left_ref, table_ref, base, rows):
    for place in range(left_ref.shape[0] // rows):
        source = pl.multiple_of(table_ref[base + place] * rows, 8)
        left_ref[place * rows : (place + 1) * rows, :] = flat_ref[pl.ds(source, rows), :].astype(low)


def product_rows(left, rights, at, columns):
    total, start = None, 0
    for right in rights:
        piece = right[:, at : at + columns]
        term = jnp.dot(
            left[:, start : start + right.shape[0]], piece, preferred_element_type=wide
        )
        total = term if total is None else total + term
        start += right.shape[0]
    return total


def grads_mlp(rows_two, back_two, gates, ups, hiddens, table, blocks):
    count, width = rows_two[0].shape
    rows, cols = width // blocks, gates[0].shape[1]
    tile = 512
    steps = cols // tile

    def body(table_ref, h0, h1, b0, b1, g0, g1, u0, u1, v0, v1, own_ref, other_ref, flat, left):
        step = pl.program_id(0)

        @pl.when(step == 0)
        def _():
            turn((h0, h1), flat)
            sort_rows(flat, left, table_ref, 3 * blocks, rows)

        @pl.when(step == steps)
        def _():
            sort_rows(flat, left, table_ref, 4 * blocks, rows)

        @pl.when(step == 2 * steps)
        def _():
            turn((b0, b1), flat)
            sort_rows(flat, left, table_ref, 5 * blocks, rows)

        def work(rights):
            for side, out in enumerate((own_ref, other_ref)):
                half = left[side * (width // 2) : (side + 1) * (width // 2), :]
                total = product_rows(half, rights, 0, tile)
                out[...] = total.reshape(blocks // 2, rows, tile).astype(low)

        pl.when(step < steps)(lambda: work((g0, g1)))
        pl.when((step >= steps) & (step < 2 * steps))(lambda: work((u0, u1)))
        pl.when(step >= 2 * steps)(lambda: work((v0, v1)))

    def part_spec(first):
        return pl.BlockSpec(
            (count, tile), lambda step, table: (0, jnp.clip(step - first, 0, steps - 1))
        )

    whole = pl.BlockSpec((count, width), lambda step, table: (0, 0))
    out_spec = pl.BlockSpec((blocks // 2, rows, tile), lambda step, table: (0, 0, step))
    out = jax.ShapeDtypeStruct((blocks // 2, rows, 3 * cols), low)
    return pl.pallas_call(
        body,
        grid_spec=pltpu.PrefetchScalarGridSpec(
            num_scalar_prefetch=1,
            grid=(3 * steps,),
            in_specs=[whole] * 4
            + [part_spec(0)] * 2
            + [part_spec(steps)] * 2
            + [part_spec(2 * steps)] * 2,
            out_specs=[out_spec, out_spec],
            scratch_shapes=[
                pltpu.VMEM((width, 2 * count), wide),
                pltpu.VMEM((width, 2 * count), low),
            ],
        ),
        out_shape=[out, out],
        cost_estimate=lasting(14.7),
        compiler_params=pltpu.CompilerParams(vmem_limit_bytes=32 * 2**20),
        name="grads_mlp",
    )(table, *rows_two, *back_two, *gates, *ups, *hiddens)


def grads_att(rows_one, back_one, raws, attendeds, table, blocks):
    count, width = rows_one[0].shape
    rows, cols = width // blocks, attendeds[0].shape[1]

    def body(table_ref, h0, h1, b0, b1, r0, r1, a0, a1, own_ref, other_ref, flat, left):
        def work(rights, at, goal):
            for side, out in enumerate((own_ref, other_ref)):
                half = left[side * (width // 2) : (side + 1) * (width // 2), :]
                total = product_rows(half, rights, at, cols)
                out[:, :, goal : goal + cols] = total.reshape(blocks // 2, rows, cols).astype(low)

        turn((h0, h1), flat)
        sort_rows(flat, left, table_ref, blocks, rows)
        for third in range(3):
            work((r0, r1), third * cols, third * cols)
        turn((b0, b1), flat)
        sort_rows(flat, left, table_ref, 2 * blocks, rows)
        work((a0, a1), 0, 3 * cols)

    whole = pl.BlockSpec(memory_space=pltpu.VMEM)
    out = jax.ShapeDtypeStruct((blocks // 2, rows, 4 * cols), low)
    return pl.pallas_call(
        body,
        in_specs=[pl.BlockSpec(memory_space=pltpu.SMEM)] + [whole] * 8,
        out_specs=[whole, whole],
        out_shape=[out, out],
        scratch_shapes=[
            pltpu.VMEM((width, 2 * count), wide),
            pltpu.VMEM((width, 2 * count), low),
        ],
        cost_estimate=lasting(8.8),
        compiler_params=pltpu.CompilerParams(vmem_limit_bytes=26 * 2**20),
        name="grads_att",
    )(table, *rows_one, *back_one, *raws, *attendeds)


def to_matrices(left_roots, right_roots):
    count = left_roots.shape[2]

    def body(left_ref, right_ref, left_out, right_out, scratch):
        for source, goal in ((left_ref, left_out), (right_ref, right_out)):
            size = source.shape[0]

            @pl.loop(0, size, unroll=8)
            def _(i):
                slab = source[i]
                slab = jnp.concatenate([slab, jnp.zeros((LANES - size, LANES), wide)], axis=0)
                scratch[pl.ds(i, LANES, stride=size), :] = slab.T

            @pl.loop(0, LANES, unroll=8)
            def _(b):
                start = pl.multiple_of(b * size, 8)
                goal[b] = scratch[pl.ds(start, size), :size].astype(low)

    def sides(of):
        return [of(left_roots.shape[0]), of(right_roots.shape[0])]

    return pl.pallas_call(
        body,
        grid=(pl.cdiv(count, LANES),),
        in_specs=sides(lambda size: pl.BlockSpec((size, size, LANES), lambda g: (0, 0, g))),
        out_specs=sides(lambda size: pl.BlockSpec((LANES, size, size), lambda g: (g, 0, 0))),
        out_shape=sides(lambda size: jax.ShapeDtypeStruct((count, size, size), low)),
        scratch_shapes=[pltpu.VMEM((LANES * left_roots.shape[0], LANES), wide)],
        cost_estimate=lasting(11.5),
        compiler_params=pltpu.CompilerParams(vmem_limit_bytes=34 * 2**20),
        name="to_matrices",
    )(left_roots, right_roots)


def shampoo(sources, spans, master, mats, filled, group, stats=None, early=None):
    rows, cols = master.shape
    chunk = 8
    wide_cols = chunk * BLOCK_WIDTH
    start = group * LANES
    starts = [0]
    for _, _, number in spans:
        starts.append(starts[-1] + number // chunk)
    steps = starts[-1]
    early_spans, early_sums = early if early else ([], [])
    sizes = (rows, BLOCK_WIDTH)

    def place(step):
        index = step + spans[0][1] // chunk
        for at, (_, first, _) in zip(starts[1:], spans[1:]):
            index = jnp.where(step >= at, step - at + first // chunk, index)
        return index

    def body(*refs):
        source_refs, refs = refs[: len(sources)], refs[len(sources) :]
        master_ref, left_mat, right_mat = refs[:3]
        step = pl.program_id(0)
        if stats:
            stat_refs = refs[3:5]
            early_refs = refs[5 : 5 + len(early_sums)]
            tail = 4 if early_sums else 2
            grad_out, master_out, low_out, left_out, right_out = refs[-5 - tail : -tail]
            sums = refs[-tail:][:2]
            copies = []
            for sum_ref, early_ref, size, sem in zip(
                sums, early_refs, sizes, refs[-tail:][2:], strict=False
            ):
                at = 0
                for index, (_, first, number) in enumerate(early_spans):
                    copies.append(
                        pltpu.make_async_copy(
                            early_ref.at[pl.ds(at * size, number * size)],
                            sum_ref.at[pl.ds((first - start) * size, number * size)],
                            sem.at[index],
                        )
                    )
                    at += number

            @pl.when(step == 0)
            def _():
                for copy in copies:
                    copy.start()
        else:
            grad_out, master_out, low_out = refs[-5:-2]
            sums = refs[-2:]
        grad = source_refs[0][...]
        for at, ref in zip(starts[1:], source_refs[1:]):
            grad = jnp.where(step >= at, ref[...], grad)
        grad_out[...] = grad
        turned = grad.T.astype(low)
        grad = grad.astype(low)
        base = place(step) * chunk - start if stats else 0
        updates = []
        for b in range(chunk):
            side = turned[b * BLOCK_WIDTH : (b + 1) * BLOCK_WIDTH, :]
            upright = grad[:, b * BLOCK_WIDTH : (b + 1) * BLOCK_WIDTH]
            at = base + b
            if stats:
                left_rows = pl.ds(pl.multiple_of(at * rows, 8), rows)
                right_rows = pl.ds(pl.multiple_of(at * BLOCK_WIDTH, 8), BLOCK_WIDTH)
            else:
                left_rows = slice(b * rows, (b + 1) * rows)
                right_rows = slice(b * BLOCK_WIDTH, (b + 1) * BLOCK_WIDTH)
            sums[0][left_rows, :rows] = jnp.dot(upright, side, preferred_element_type=wide)
            sums[1][right_rows, :BLOCK_WIDTH] = lax.dot_general(
                side, side, (((1,), (1,)), ((), ())), preferred_element_type=wide
            )
            half = jnp.dot(right_mat[b], side, preferred_element_type=wide).astype(low)
            updates.append(jnp.dot(half, left_mat[b], preferred_element_type=wide))
        new = master_ref[...] - shampoo_rate * jnp.concatenate(updates, axis=0).T
        master_out[...] = new
        low_out[...] = new.astype(low)
        if stats:

            @pl.when(step == steps - 1)
            def _():
                for copy in copies:
                    copy.wait()
                for sum_ref, stat_ref, out in zip(
                    sums, stat_refs, (left_out, right_out), strict=True
                ):
                    size = out.shape[0]
                    here = min(LANES, stats[0].shape[2] - start)

                    @pl.loop(0, size, unroll=8)
                    def _(i):
                        slab = sum_ref[pl.ds(i, here, stride=size), :].T
                        out[i, :, :here] = 0.5 * stat_ref[i, :, :here] + 0.5 * slab[:size]

    def source_spec(index):
        first = spans[index][0] // chunk
        count = spans[index][2] // chunk

        def at(step):
            return (0, first + jnp.clip(step - starts[index], 0, count - 1))

        return pl.BlockSpec((rows, wide_cols), at)

    def lanes_spec(size):
        return pl.BlockSpec((size, size, LANES), lambda step: (0, 0, group))

    def mats_spec(size):
        return pl.BlockSpec((chunk, size, size), lambda step: (place(step), 0, 0))

    def sums_spec(size):
        return pl.BlockSpec((chunk * size, LANES), lambda step: (step, 0))

    own = pl.BlockSpec((rows, wide_cols), lambda step: (0, place(step)))
    anywhere = pl.BlockSpec(memory_space=pl.ANY)
    in_specs = [source_spec(i) for i in range(len(sources))] + [own] + [mats_spec(s) for s in sizes]
    out_specs = [own, own, own]
    outs = [jax.ShapeDtypeStruct((rows, cols), kind) for kind in (wide, wide, low)]
    scratch = []
    if stats:
        in_specs += [lanes_spec(s) for s in sizes] + [anywhere for _ in early_sums]
        out_specs += [lanes_spec(s) for s in sizes]
        outs += [jax.ShapeDtypeStruct(stat.shape, wide) for stat in stats]
        scratch = [pltpu.VMEM((LANES * s, LANES), wide) for s in sizes]
        if early_sums:
            scratch += [pltpu.SemaphoreType.DMA((len(early_spans),)) for _ in sizes]
    else:
        out_specs += [sums_spec(s) for s in sizes]
        outs += [jax.ShapeDtypeStruct((steps * chunk * s, LANES), wide) for s in sizes]
    operands = [*sources, master, *mats, *(stats or []), *early_sums]
    number = steps * chunk
    return pl.pallas_call(
        body,
        grid=(steps,),
        in_specs=in_specs + [anywhere for _ in filled],
        out_specs=out_specs,
        out_shape=outs,
        scratch_shapes=scratch,
        input_output_aliases={len(operands) + i: i for i in range(len(filled))},
        cost_estimate=lasting(number * 0.25),
        name="shampoo",
    )(*operands, *filled)


def local(
    block_input,
    cotangent,
    master,
    left_stats,
    right_stats,
    left_roots,
    right_roots,
    vec,
    vec_mom,
    time_table,
    class_table,
    bucket,
    label,
    owner,
):
    tensor_size = lax.axis_size("tensor")
    data_size = lax.axis_size("dp")
    rings = tensor_size == 2 and data_size == 2 * len(RING)
    tensor_index = lax.axis_index("tensor")
    data_index = lax.axis_index("dp")
    row_count, width = block_input.shape
    own_rows = master.shape[0]
    head_cols = width // tensor_size
    local_heads = head_cols // HEAD_DIM
    hidden_cols = FF // tensor_size
    group_images = row_count // PATCHES * tensor_size
    images_all = group_images * data_size
    scale_dot = HEAD_DIM ** (-0.5)
    widths = [6 * head_cols, 3 * head_cols, head_cols, hidden_cols, hidden_cols, hidden_cols]
    bounds = [0]
    for piece_width in widths:
        bounds.append(bounds[-1] + piece_width)
    devices = ("dp", "tensor")

    if rings:
        order = lax.dynamic_index_in_dim(relative_order(), data_index, 0, keepdims=False)
        table = ((order[None, :] - owner[:, None]) % data_size).reshape(-1)

        def ring_of(first, last, *ready):
            return RingGather(after(master[:, bounds[first] : bounds[last]].astype(low), *ready))

        def matrices(ring, first, last):
            return assemble(ring.pieces, table, first, widths[first:last], data_size)

        def spread(rows):
            return [rows, across_tensor(rows)]

        def gathered_sum(parts, *before):
            got = across_tensor(parts[1].astype(low))
            return parts[0] + after(got, *before).astype(wide)
    else:

        def weights(first, last):
            own = master[:, bounds[first] : bounds[last]].astype(low)
            gathered = lax.all_gather(own, "dp", axis=0, tiled=True)
            natural, at = [], 0
            for index in range(first, last):
                piece = gathered[:, at : at + widths[index]]
                natural.append(roll_blocks(piece, -owner[index], data_size))
                at += widths[index]
            return natural

        def to_owners(pairs, first):
            grads = [
                lax.dot_general(
                    left[0], right[0], (((0,), (0,)), ((), ())), preferred_element_type=wide
                ).astype(low)
                for left, right in pairs
            ]
            flat = [roll_blocks(grad, owner[first + i], data_size) for i, grad in enumerate(grads)]
            flat = jnp.concatenate(flat, axis=1)
            return lax.psum_scatter(flat, "dp", scatter_dimension=0, tiled=True).astype(wide)

        def spread(rows):
            return [lax.all_gather(rows, "tensor", axis=0, tiled=True)]

        def gathered_sum(parts):
            summed = lax.psum_scatter(
                parts[0].astype(low), "tensor", scatter_dimension=0, tiled=True
            )
            return summed.astype(wide)

    n_own = rms_norm(block_input)
    if rings:
        n_partner = across_tensor(n_own.astype(low))
        ring = ring_of(1, 3)
        hop = ring.hop()
    marks = jnp.stack([bucket, label], axis=1)
    marks = jnp.broadcast_to(marks[None], (data_size,) + marks.shape)
    marks = lax.all_to_all(marks, "dp", 0, 0, tiled=True).reshape(images_all, 2)
    if rings:
        marks = after(marks, hop)
        hop = ring.hop()
    cond = time_table[marks[:, 0]] + class_table[marks[:, 1]]
    cond = lax.dynamic_slice_in_dim(cond, tensor_index * head_cols, head_cols, 1)
    lifted = jax.nn.silu(cond).astype(low)
    if rings:
        lifted = after(lifted, hop, n_partner)
        hop = ring.hop(cond)
    ada = master[:, : bounds[1]].astype(low)
    row_map = lax.broadcasted_iota(jnp.int32, (6 * images_all, 6 * head_cols), 0) // images_all
    col_map = lax.broadcasted_iota(jnp.int32, (6 * images_all, 6 * head_cols), 1) // head_cols
    on_map = row_map == col_map
    lifted_maps = jnp.where(on_map, jnp.tile(lifted, (6, 6)), jnp.zeros((), low))
    partial_mod = lax.dot_general(
        lifted_maps, ada, (((1,), (1,)), ((), ())), preferred_element_type=wide
    )
    send = partial_mod.reshape(6, data_size, group_images, own_rows).transpose(1, 0, 2, 3)
    send = jnp.broadcast_to(send[:, None], (data_size, tensor_size) + send.shape[1:])
    send = send.reshape((data_size * tensor_size,) + send.shape[2:])
    if rings:
        send = after(send, hop)
        ring_two = ring_of(3, 6, hop)
        hop = ring.hop()
        hop_two = ring_two.hop()
    got = lax.all_to_all(send, devices, 0, 0, tiled=True)
    if rings:
        got = after(got, hop)
        qkv_cols, proj_cols = matrices(ring, 1, 3)
        qkv_cols = lax.optimization_barrier(qkv_cols.T)
        ring = ring_two
        hop = ring.hop()
    got = got.reshape((data_size, tensor_size) + got.shape[1:]).sum(axis=1)
    got = jnp.roll(got, -owner[0], axis=0).transpose(2, 1, 0, 3)
    mods = got.reshape(group_images, 6, width) + vec[: 6 * width].reshape(6, width)

    mod = lax.dynamic_index_in_dim(mods, tensor_index, 0, keepdims=False)
    shift_one, scale_one, gate_one, shift_two, scale_two, gate_two = [
        mod[index][None, :] for index in range(6)
    ]
    gains = vec[6 * width :].reshape(2, HEAD_DIM)

    h_one = (n_own * (1.0 + scale_one) + shift_one).astype(low)
    if rings:
        mod_partner = lax.dynamic_index_in_dim(mods, 1 - tensor_index, 0, keepdims=False)
        h_partner = n_partner.astype(wide) * (1.0 + mod_partner[1][None]) + mod_partner[0][None]
        rows_one = [h_one, after(h_partner.astype(low), hop_two)]
    else:
        rows_one = spread(h_one)
        qkv_cols, proj_cols = weights(1, 3)
        qkv_cols = qkv_cols.T
        w_one, w_three, w_two = weights(3, 6)
    send_two = (gate_two * cotangent).astype(low)
    back_two = spread(send_two)

    cosine, sine = rope_tables()
    kept = []
    branch_parts = []
    for part, rows in enumerate(reversed(rows_one)):
        if rings and part == 1:
            rows = after(rows, hop, branch_parts)
            roots = [
                after(side[0].transpose(1, 2, 0), hop) for side in (left_roots, right_roots)
            ]
            mats = to_matrices(*roots)
            stats = [left_stats[0].transpose(1, 2, 0), right_stats[0].transpose(1, 2, 0)]
            hop = ring.hop()
        raw = jnp.einsum("rd,cd->rc", rows, qkv_cols, preferred_element_type=wide)
        raw = raw.reshape(rows.shape[0] // PATCHES, PATCHES, 3, local_heads, HEAD_DIM)
        query_norm = rms_norm(raw[:, :, 0])
        key_norm = rms_norm(raw[:, :, 1])
        query = rotate(query_norm * gains[0], cosine, sine).astype(low)
        keys = rotate(key_norm * gains[1], cosine, sine).astype(low)
        values = raw[:, :, 2].astype(low)
        scores = jnp.einsum("gphd,gqhd->ghpq", query, keys, preferred_element_type=wide) * scale_dot
        peak = jnp.max(scores, axis=-1, keepdims=True)
        expo = jnp.exp(scores - peak)
        total = jnp.sum(expo, axis=-1, keepdims=True)
        logsum = peak + jnp.log(total)
        probs = (expo / total).astype(low)
        attended = jnp.einsum("ghpq,gqhd->gphd", probs, values, preferred_element_type=wide)
        attended = attended.astype(low).reshape(rows.shape[0], head_cols)
        kept.append((raw, query_norm, key_norm, query, keys, values, logsum, attended))
        branch_parts.append(
            jnp.einsum("rh,oh->ro", attended, proj_cols, preferred_element_type=wide)
        )
    kept.reverse()
    branch_parts.reverse()
    if rings:
        branch_one = gathered_sum(branch_parts, hop, branch_parts[0], mats)
        hop = ring.hop()
        attended_parts = lax.optimization_barrier([saved[-1] for saved in kept])
    else:
        branch_one = gathered_sum(branch_parts)
    middle = block_input + gate_one * branch_one
    n_two = rms_norm(middle)
    h_two = (n_two * (1.0 + scale_two) + shift_two).astype(low)
    rows_two = spread(h_two)
    if rings:
        rows_two[1] = after(rows_two[1], hop)
        w_one, w_three, w_two = matrices(ring, 3, 6)

    branch_parts, hidden_parts, gate_parts, up_parts, d_parts = [], [], [], [], []
    for rows, back in zip(rows_two, back_two, strict=True):
        gate_pre = jnp.dot(rows, w_one, preferred_element_type=wide)
        up_pre = jnp.dot(rows, w_three, preferred_element_type=wide)
        d_hidden = jnp.dot(back, w_two, preferred_element_type=wide)
        sigma = jax.nn.sigmoid(gate_pre)
        silu_gate = gate_pre * sigma
        hidden = (silu_gate * up_pre).astype(low)
        d_gate_pre = (d_hidden * up_pre * sigma * (1.0 + gate_pre * (1.0 - sigma))).astype(low)
        d_up_pre = (d_hidden * silu_gate).astype(low)
        hidden_parts.append(hidden)
        gate_parts.append(d_gate_pre)
        up_parts.append(d_up_pre)
        d_parts.append(
            jnp.einsum("rf,df->rd", d_gate_pre, w_one, preferred_element_type=wide)
            + jnp.einsum("rf,df->rd", d_up_pre, w_three, preferred_element_type=wide)
        )

    if rings:
        hidden_parts[0] = after(hidden_parts[0], d_parts)
        own, other = grads_mlp(
            rows_two, back_two, gate_parts, up_parts, hidden_parts, table, data_size
        )
        ring = RingScatter(own, other, True)
    else:
        grad_mlp = to_owners(
            [(rows_two, gate_parts), (rows_two, up_parts), (back_two, hidden_parts)], 3
        )
    d_h_two = gathered_sum(d_parts, own) if rings else gathered_sum(d_parts)
    if not rings:
        attended_parts = [saved[-1] for saved in kept]
    d_shift_two = jnp.sum(d_h_two, axis=0)
    d_scale_two = jnp.sum(d_h_two * n_two, axis=0)
    d_middle = cotangent + norm_back(middle, n_two, d_h_two * (1.0 + scale_two))
    d_gate_one = jnp.sum(d_middle * branch_one, axis=0)
    send_one = (gate_one * d_middle).astype(low)
    back_one = spread(send_one)
    if rings:
        hop = ring.hop()
        w_two = after(w_two, send_one)
    branch_parts = [
        jnp.einsum("rf,of->ro", hidden, w_two, preferred_element_type=wide)
        for hidden in hidden_parts
    ]
    if rings:
        back_one[0] = after(back_one[0], ring.sent, branch_parts[1])
        branch_got = across_tensor(branch_parts[1].astype(low))

    d_parts, raw_parts = [], []
    gain_grads = jnp.zeros((2, HEAD_DIM), wide)
    for part, (back, saved) in enumerate(zip(back_one, kept, strict=True)):
        if rings and part == 1:
            back = after(back, d_parts, branch_got)
        raw, query_norm, key_norm, query, keys, values, logsum, attended = saved
        d_attended = jnp.dot(back, proj_cols, preferred_element_type=wide).astype(low)
        if rings:
            d_attended = after(d_attended, hop)
            hop = ring.hop()
        d_attended = d_attended.reshape(values.shape)
        scores = jnp.einsum("gphd,gqhd->ghpq", query, keys, preferred_element_type=wide) * scale_dot
        probs_full = jnp.exp(scores - logsum)
        d_values = jnp.einsum(
            "ghpq,gphd->gqhd", probs_full.astype(low), d_attended, preferred_element_type=wide
        )
        d_probs = jnp.einsum("gphd,gqhd->ghpq", d_attended, values, preferred_element_type=wide)
        d_scores = probs_full * (d_probs - jnp.sum(probs_full * d_probs, axis=-1, keepdims=True))
        d_scores = d_scores.astype(low)
        d_query = (
            jnp.einsum("ghpq,gqhd->gphd", d_scores, keys, preferred_element_type=wide) * scale_dot
        )
        d_keys = (
            jnp.einsum("ghpq,gphd->gqhd", d_scores, query, preferred_element_type=wide) * scale_dot
        )
        d_query_norm = rotate(d_query, cosine, -sine)
        d_key_norm = rotate(d_keys, cosine, -sine)
        gain_grads += jnp.stack(
            [
                jnp.sum(d_query_norm * query_norm, axis=(0, 1, 2)),
                jnp.sum(d_key_norm * key_norm, axis=(0, 1, 2)),
            ]
        )
        d_raw_query = norm_back(raw[:, :, 0], query_norm, d_query_norm * gains[0])
        d_raw_key = norm_back(raw[:, :, 1], key_norm, d_key_norm * gains[1])
        d_raw = jnp.stack([d_raw_query, d_raw_key, d_values], axis=2).astype(low)
        d_raw = d_raw.reshape(back.shape[0], 3 * head_cols)
        raw_parts.append(d_raw)
        d_parts.append(jnp.einsum("rc,cd->rd", d_raw, qkv_cols, preferred_element_type=wide))
    if rings:
        held = after(raw_parts[1], hop, d_parts)
        hop = ring.hop()
        held = after(held, ring.sent)
        own, other = grads_att(
            rows_one, back_one, [raw_parts[0], held], attended_parts, table, data_size
        )
        ring_att = RingScatter(own, other, False)
        grad_mlp = ring.total()
        hop_one = ring_att.hop()
        d_h_one = gathered_sum(d_parts, own, hop)
        branch_two = after(branch_parts[0] , d_h_one) + branch_got.astype(wide)
        lifted_late = after(lifted, d_h_one)
        lifted_maps = jnp.where(on_map, jnp.tile(lifted_late, (6, 6)), jnp.zeros((), low))
    else:
        branch_two = gathered_sum(branch_parts)
        grad_att = to_owners([(rows_one, raw_parts), (back_one, attended_parts)], 1)
        d_h_one = gathered_sum(d_parts)
    output = middle + gate_two * branch_two
    d_gate_two = jnp.sum(cotangent * branch_two, axis=0)
    d_shift_one = jnp.sum(d_h_one, axis=0)
    d_scale_one = jnp.sum(d_h_one * n_own, axis=0)
    d_inputs = d_middle + norm_back(block_input, n_own, d_h_one * (1.0 + scale_one))

    d_mod = jnp.stack([d_shift_one, d_scale_one, d_gate_one, d_shift_two, d_scale_two, d_gate_two])
    d_mod = d_mod.reshape(6, data_size, own_rows).transpose(1, 0, 2)
    d_mod = jnp.roll(d_mod, owner[0], axis=0).reshape(data_size, 6 * own_rows)
    gain_row = jnp.broadcast_to(gain_grads.reshape(1, -1), (data_size, 2 * HEAD_DIM))
    send = jnp.concatenate([d_mod, gain_row], axis=1)
    send = jnp.broadcast_to(send[:, None], (data_size, tensor_size, send.shape[1]))
    send = send.reshape(data_size * tensor_size, send.shape[2])
    got = lax.all_to_all(send, devices, 0, 0, tiled=True)
    if rings:
        blocks_ada, blocks_att = bounds[1] // BLOCK_WIDTH, (bounds[3] - bounds[1]) // BLOCK_WIDTH
        skip = LANES - blocks_ada - blocks_att
        total = bounds[6] // BLOCK_WIDTH
        grad_mlp = after(grad_mlp, hop_one)
        hop = ring_att.hop()
        group_one = shampoo(
            [grad_mlp], [(skip, LANES, total - LANES)], master, mats, [], 1, stats=stats
        )
        got = after(got, output, group_one, hop)
        hop = ring_att.hop()
    gain_sum = jnp.sum(got[:, 6 * own_rows :], axis=0)
    d_own = got[:, : 6 * own_rows].reshape(images_all, 6, own_rows).transpose(1, 0, 2)
    row_sum = jnp.sum(d_own, axis=1).reshape(-1)
    d_own = d_own.reshape(6 * images_all, own_rows)
    grad_ada = lax.dot_general(
        d_own,
        lifted_maps.astype(wide),
        (((0,), (0,)), ((), ())),
        precision=precise,
        preferred_element_type=wide,
    )
    d_lifted = lax.dot_general(
        d_own,
        ada.astype(wide),
        (((1,), (0,)), ((), ())),
        precision=precise,
        preferred_element_type=wide,
    )
    d_lifted = jnp.where(on_map, d_lifted, 0.0).reshape(6, images_all, 6 * head_cols).sum(axis=0)
    d_lifted = sum(d_lifted[:, j * head_cols : (j + 1) * head_cols] for j in range(6))
    send = jnp.concatenate(
        [
            d_lifted.reshape(data_size, group_images * head_cols),
            jnp.broadcast_to(row_sum[None, :], (data_size, 6 * own_rows)),
        ],
        axis=1,
    )
    if rings:
        grad_ada = after(grad_ada, send, hop)
        hop = ring_att.hop()
    got = lax.all_to_all(send, "dp", 0, 0, tiled=True)
    if rings:
        early = [(0, 0, blocks_ada), (0, blocks_ada + blocks_att, LANES - blocks_ada - blocks_att)]
        part = shampoo([grad_ada, grad_mlp], early, master, mats, group_one[:3], 0)
        got = after(got, part[0], hop)
    d_lifted = jnp.sum(got[:, : group_images * head_cols], axis=0).reshape(group_images, head_cols)
    cond_here = lax.dynamic_slice_in_dim(cond, data_index * group_images, group_images, 0)
    d_cond = d_lifted * silu_slope(cond_here)
    vec_rows = got[:, group_images * head_cols :].reshape(data_size, 6, own_rows)
    vec_rows = jnp.roll(vec_rows, -owner[0], axis=0).transpose(1, 0, 2).reshape(-1)
    vec_grad = jnp.concatenate([vec_rows, gain_sum])

    if rings:
        grad_att = after(ring_att.total(), part[3])
        outs = shampoo(
            [grad_att],
            [(0, blocks_ada, blocks_att)],
            master,
            mats,
            [*part[:3], *group_one[3:]],
            0,
            stats=stats,
            early=(early, part[3:]),
        )
        grad_mine, master_new, weights_low = outs[:3]
        left_new, right_new = outs[3].transpose(2, 0, 1), outs[4].transpose(2, 0, 1)
    else:
        grad_mine = jnp.concatenate([grad_ada, grad_att, grad_mlp], axis=1)
        block_count = grad_mine.shape[1] // BLOCK_WIDTH
        pieces = grad_mine.astype(low).reshape(own_rows, block_count, BLOCK_WIDTH).transpose(1, 0, 2)
        left_new = 0.5 * left_stats[0] + 0.5 * jnp.einsum(
            "bij,bkj->bik", pieces, pieces, preferred_element_type=wide
        )
        right_new = 0.5 * right_stats[0] + 0.5 * jnp.einsum(
            "bji,bjk->bik", pieces, pieces, preferred_element_type=wide
        )
        update = jnp.einsum(
            "bij,bjk->bik", left_roots[0].astype(low), pieces, preferred_element_type=wide
        )
        update = jnp.einsum(
            "bik,bkl->bil",
            update.astype(low),
            right_roots[0].astype(low),
            preferred_element_type=wide,
        )
        update = update.transpose(1, 0, 2).reshape(own_rows, block_count * BLOCK_WIDTH)
        master_new = master - shampoo_rate * update
        weights_low = master_new.astype(low)
    tokens_all = row_count * data_size * tensor_size
    mom_new = momentum * vec_mom + vec_grad
    vec_new = vec - 0.1 / tokens_all**0.5 * mom_new
    return (
        output,
        d_inputs,
        d_cond,
        grad_mine,
        left_new[None],
        right_new[None],
        master_new,
        weights_low,
        vec_new,
        mom_new,
    )


def solution(mesh):
    placed = (
        P(("dp", "tensor"), None),
        P(("dp", "tensor"), None),
        P("dp", "tensor"),
        P("dp", "tensor", None, None),
        P("dp", "tensor", None, None),
        P("dp", "tensor", None, None),
        P("dp", "tensor", None, None),
        P(),
        P(),
        P(),
        P(),
        P("dp"),
        P("dp"),
        P(),
    )
    return jax.shard_map(
        local,
        mesh=mesh,
        in_specs=placed,
        out_specs=(
            P(("dp", "tensor"), None),
            P(("dp", "tensor"), None),
            P("dp", "tensor"),
            P("dp", "tensor"),
            P("dp", "tensor", None, None),
            P("dp", "tensor", None, None),
            P("dp", "tensor"),
            P("dp", "tensor"),
            P(),
            P(),
        ),
        check_vma=False,
    )
```

```python
import functools

import jax
import jax.numpy as jnp
from jax import lax
from jax.experimental import pallas as pl
from jax.experimental.pallas import tpu as pltpu
from jax.sharding import PartitionSpec as P

HEAD_DIM = 72
FF = 3072
PATCHES = 256
GRID = 16
BLOCK_WIDTH = 48
RING = (0, 1, 3, 5, 7, 6, 4, 2)
LANES = 128

epsilon = 1e-06
precise = lax.Precision.HIGHEST
shampoo_rate = 0.25
momentum = 0.9
low = jnp.bfloat16
wide = jnp.float32
BYTES_PER_US = 3_500_000


def lasting(microseconds):
    moved = int(microseconds * BYTES_PER_US)
    return pl.CostEstimate(flops=0, transcendentals=0, bytes_accessed=moved)


def rms_norm(values):
    return values * lax.rsqrt(jnp.mean(values * values, axis=-1, keepdims=True) + epsilon)


def norm_back(values, normed, upstream):
    factor = lax.rsqrt(jnp.mean(values * values, axis=-1, keepdims=True) + epsilon)
    return factor * (upstream - normed * jnp.mean(upstream * normed, axis=-1, keepdims=True))


def rope_tables():
    quarter = HEAD_DIM // 4
    freqs = 10000.0 ** (-jnp.arange(quarter, dtype=jnp.float32) / quarter)
    places = jnp.arange(PATCHES)
    coords = jnp.stack([places // GRID, places % GRID], axis=1).astype(jnp.float32)
    angles = coords[:, :, None] * freqs[None, None, :]
    return (jnp.cos(angles), jnp.sin(angles))


def rotate(values, cosine, sine):
    shape = values.shape
    halves = values.reshape(shape[:-1] + (2, 2, shape[-1] // 4))
    first_part = halves[..., 0, :]
    second_part = halves[..., 1, :]
    cosine = cosine[:, None]
    sine = sine[:, None]
    turned = jnp.stack(
        [first_part * cosine - second_part * sine, second_part * cosine + first_part * sine],
        axis=-2,
    )
    return turned.reshape(shape)


def roll_blocks(matrix, shift, groups):
    blocks = matrix.reshape((groups, matrix.shape[0] // groups) + matrix.shape[1:])
    return jnp.roll(blocks, shift, axis=0).reshape(matrix.shape)


def silu_slope(values):
    sigma = jax.nn.sigmoid(values)
    return sigma * (1.0 + values * (1.0 - sigma))


def ring_pairs(step):
    pairs = []
    for place, chip in enumerate(RING):
        goal = RING[(place + step) % len(RING)]
        pairs += [(chip * 2 + core, goal * 2 + core) for core in range(2)]
    return pairs


def around(value, step):
    return lax.ppermute(value, "dp", ring_pairs(step))


def across_cores(value):
    return lax.ppermute(value, "dp", [(i, i ^ 1) for i in range(2 * len(RING))])


def across_tensor(value):
    return lax.ppermute(value, "tensor", [(0, 1), (1, 0)])


def relative_order():
    rows = []
    for device in range(2 * len(RING)):
        place, core = RING.index(device // 2), device % 2
        chips = [RING[(place + offset) % len(RING)] for offset in range(len(RING))]
        rows.append([chip * 2 + core for chip in chips] + [chip * 2 + 1 - core for chip in chips])
    return jnp.array(rows, jnp.int32)


def after(value, *others):
    return lax.optimization_barrier((value, others))[0]


class RingGather:
    def __init__(self, shard):
        self.half = shard.shape[1] // 2
        self.right = self.left = shard
        self.hops = 0
        self.pieces = []
        self.keep(0, 0, shard)

    def keep(self, offset, start, piece):
        self.pieces.append((offset, start, piece))
        self.pieces.append((offset + len(RING), start, across_cores(piece)))

    def hop(self, *ready):
        self.hops += 1
        ready = (*ready, self.right, self.left)
        if self.hops < 4:
            self.right = around(after(self.right, *ready), 1)
            self.left = around(after(self.left, *ready), -1)
            self.keep(8 - self.hops, 0, self.right)
            self.keep(self.hops, 0, self.left)
        else:
            self.right = around(after(self.right[:, : self.half], *ready), 1)
            self.left = around(after(self.left[:, self.half :], *ready), -1)
            self.keep(4, 0, self.right)
            self.keep(4, self.half, self.left)
        return self.right, self.left


class RingScatter:
    def __init__(self, own, other, ahead):
        self.own = own
        self.half = own.shape[2] // 2
        self.farthest = None
        if ahead:
            self.farthest = across_cores(other[4])
            other = after(other, self.farthest)
        self.partner = across_cores(other)
        self.hops = 0

    def term(self, offset):
        partner = self.partner[offset]
        if offset == 4 and self.farthest is not None:
            partner = self.farthest
        return self.own[offset].astype(wide) + partner.astype(wide)

    def hop(self, *ready):
        half = self.half
        if self.hops == 0:
            start = self.term(4).astype(low)
            right, left = start[:, :half], start[:, half:]
        else:
            mine, other = self.term(4 - self.hops), self.term(4 + self.hops)
            right, left = self.right.astype(wide), self.left.astype(wide)
            if self.hops == 1:
                right = jnp.concatenate([mine[:, :half] + right, mine[:, half:]], axis=1)
                left = jnp.concatenate([other[:, :half], other[:, half:] + left], axis=1)
            else:
                right, left = right + mine, left + other
            right, left = right.astype(low), left.astype(low)
        self.hops += 1
        self.sent = right, left
        ready = (*ready, *self.sent)
        self.right = around(after(right, *ready), 1)
        self.left = around(after(left, *ready), -1)
        return self.right, self.left

    def total(self):
        return self.term(0) + self.right.astype(wide) + self.left.astype(wide)


def assemble(pieces, table, first, widths, blocks):
    rows = pieces[0][2].shape[0]
    starts = [sum(widths[:i]) for i in range(len(widths))]

    def body(table_ref, *refs):
        outs = refs[len(pieces) :]
        for (place, at, _), ref in zip(pieces, refs, strict=False):
            for index, (out, start, width) in enumerate(zip(outs, starts, widths, strict=True)):
                low_end = max(start, at)
                high_end = min(start + width, at + ref.shape[1])
                if low_end < high_end:
                    goal = table_ref[(first + index) * blocks + place]
                    out[goal, :, low_end - start : high_end - start] = ref[
                        :, low_end - at : high_end - at
                    ]

    whole = pl.BlockSpec(memory_space=pltpu.VMEM)
    outs = pl.pallas_call(
        body,
        in_specs=[pl.BlockSpec(memory_space=pltpu.SMEM)] + [whole for _ in pieces],
        out_specs=[whole for _ in widths],
        out_shape=[jax.ShapeDtypeStruct((blocks, rows, width), low) for width in widths],
        cost_estimate=lasting(blocks * rows * sum(widths) / 1.2e6),
        compiler_params=pltpu.CompilerParams(vmem_limit_bytes=4 * blocks * rows * sum(widths) + 2 * 2**20),
        name="assemble",
    )(table, *[piece for _, _, piece in pieces])
    return [out.reshape(blocks * rows, width) for out, width in zip(outs, widths, strict=True)]


def turn(parts, flat_ref):
    at = 0
    for part in parts:
        flat_ref[:, at : at + part.shape[0]] = part[...].astype(wide).T
        at += part.shape[0]


def sort_rows(flat_ref, left_ref, table_ref, base, rows):
    for place in range(left_ref.shape[0] // rows):
        source = pl.multiple_of(table_ref[base + place] * rows, 8)
        left_ref[place * rows : (place + 1) * rows, :] = flat_ref[pl.ds(source, rows), :].astype(low)


def product_rows(left, rights, at, columns):
    total, start = None, 0
    for right in rights:
        piece = right[:, at : at + columns]
        term = jnp.dot(
            left[:, start : start + right.shape[0]], piece, preferred_element_type=wide
        )
        total = term if total is None else total + term
        start += right.shape[0]
    return total


def grads_mlp(rows_two, back_two, gates, ups, hiddens, table, blocks):
    count, width = rows_two[0].shape
    rows, cols = width // blocks, gates[0].shape[1]
    tile = 512
    steps = cols // tile

    def body(table_ref, h0, h1, b0, b1, g0, g1, u0, u1, v0, v1, own_ref, other_ref, flat, left):
        step = pl.program_id(0)

        @pl.when(step == 0)
        def _():
            turn((h0, h1), flat)
            sort_rows(flat, left, table_ref, 3 * blocks, rows)

        @pl.when(step == steps)
        def _():
            sort_rows(flat, left, table_ref, 4 * blocks, rows)

        @pl.when(step == 2 * steps)
        def _():
            turn((b0, b1), flat)
            sort_rows(flat, left, table_ref, 5 * blocks, rows)

        def work(rights):
            for side, out in enumerate((own_ref, other_ref)):
                half = left[side * (width // 2) : (side + 1) * (width // 2), :]
                total = product_rows(half, rights, 0, tile)
                out[...] = total.reshape(blocks // 2, rows, tile).astype(low)

        pl.when(step < steps)(lambda: work((g0, g1)))
        pl.when((step >= steps) & (step < 2 * steps))(lambda: work((u0, u1)))
        pl.when(step >= 2 * steps)(lambda: work((v0, v1)))

    def part_spec(first):
        return pl.BlockSpec(
            (count, tile), lambda step, table: (0, jnp.clip(step - first, 0, steps - 1))
        )

    whole = pl.BlockSpec((count, width), lambda step, table: (0, 0))
    out_spec = pl.BlockSpec((blocks // 2, rows, tile), lambda step, table: (0, 0, step))
    out = jax.ShapeDtypeStruct((blocks // 2, rows, 3 * cols), low)
    return pl.pallas_call(
        body,
        grid_spec=pltpu.PrefetchScalarGridSpec(
            num_scalar_prefetch=1,
            grid=(3 * steps,),
            in_specs=[whole] * 4
            + [part_spec(0)] * 2
            + [part_spec(steps)] * 2
            + [part_spec(2 * steps)] * 2,
            out_specs=[out_spec, out_spec],
            scratch_shapes=[
                pltpu.VMEM((width, 2 * count), wide),
                pltpu.VMEM((width, 2 * count), low),
            ],
        ),
        out_shape=[out, out],
        cost_estimate=lasting(14.7),
        compiler_params=pltpu.CompilerParams(vmem_limit_bytes=32 * 2**20),
        name="grads_mlp",
    )(table, *rows_two, *back_two, *gates, *ups, *hiddens)


def grads_att(rows_one, back_one, raws, attendeds, table, blocks):
    count, width = rows_one[0].shape
    rows, cols = width // blocks, attendeds[0].shape[1]

    def body(table_ref, h0, h1, b0, b1, r0, r1, a0, a1, own_ref, other_ref, flat, left):
        def work(rights, at, goal):
            for side, out in enumerate((own_ref, other_ref)):
                half = left[side * (width // 2) : (side + 1) * (width // 2), :]
                total = product_rows(half, rights, at, cols)
                out[:, :, goal : goal + cols] = total.reshape(blocks // 2, rows, cols).astype(low)

        turn((h0, h1), flat)
        sort_rows(flat, left, table_ref, blocks, rows)
        for third in range(3):
            work((r0, r1), third * cols, third * cols)
        turn((b0, b1), flat)
        sort_rows(flat, left, table_ref, 2 * blocks, rows)
        work((a0, a1), 0, 3 * cols)

    whole = pl.BlockSpec(memory_space=pltpu.VMEM)
    out = jax.ShapeDtypeStruct((blocks // 2, rows, 4 * cols), low)
    return pl.pallas_call(
        body,
        in_specs=[pl.BlockSpec(memory_space=pltpu.SMEM)] + [whole] * 8,
        out_specs=[whole, whole],
        out_shape=[out, out],
        scratch_shapes=[
            pltpu.VMEM((width, 2 * count), wide),
            pltpu.VMEM((width, 2 * count), low),
        ],
        cost_estimate=lasting(8.8),
        compiler_params=pltpu.CompilerParams(vmem_limit_bytes=26 * 2**20),
        name="grads_att",
    )(table, *rows_one, *back_one, *raws, *attendeds)


def to_matrices(left_roots, right_roots):
    count = left_roots.shape[2]

    def body(left_ref, right_ref, left_out, right_out, scratch):
        for source, goal in ((left_ref, left_out), (right_ref, right_out)):
            size = source.shape[0]

            @pl.loop(0, size, unroll=8)
            def _(i):
                slab = source[i]
                slab = jnp.concatenate([slab, jnp.zeros((LANES - size, LANES), wide)], axis=0)
                scratch[pl.ds(i, LANES, stride=size), :] = slab.T

            @pl.loop(0, LANES, unroll=8)
            def _(b):
                start = pl.multiple_of(b * size, 8)
                goal[b] = scratch[pl.ds(start, size), :size].astype(low)

    def sides(of):
        return [of(left_roots.shape[0]), of(right_roots.shape[0])]

    return pl.pallas_call(
        body,
        grid=(pl.cdiv(count, LANES),),
        in_specs=sides(lambda size: pl.BlockSpec((size, size, LANES), lambda g: (0, 0, g))),
        out_specs=sides(lambda size: pl.BlockSpec((LANES, size, size), lambda g: (g, 0, 0))),
        out_shape=sides(lambda size: jax.ShapeDtypeStruct((count, size, size), low)),
        scratch_shapes=[pltpu.VMEM((LANES * left_roots.shape[0], LANES), wide)],
        cost_estimate=lasting(11.5),
        compiler_params=pltpu.CompilerParams(vmem_limit_bytes=34 * 2**20),
        name="to_matrices",
    )(left_roots, right_roots)


def shampoo(sources, spans, master, mats, filled, group, stats=None, early=None):
    rows, cols = master.shape
    chunk = 8
    wide_cols = chunk * BLOCK_WIDTH
    start = group * LANES
    starts = [0]
    for _, _, number in spans:
        starts.append(starts[-1] + number // chunk)
    steps = starts[-1]
    early_spans, early_sums = early if early else ([], [])
    sizes = (rows, BLOCK_WIDTH)

    def place(step):
        index = step + spans[0][1] // chunk
        for at, (_, first, _) in zip(starts[1:], spans[1:]):
            index = jnp.where(step >= at, step - at + first // chunk, index)
        return index

    def body(*refs):
        source_refs, refs = refs[: len(sources)], refs[len(sources) :]
        master_ref, left_mat, right_mat = refs[:3]
        step = pl.program_id(0)
        if stats:
            stat_refs = refs[3:5]
            early_refs = refs[5 : 5 + len(early_sums)]
            tail = 4 if early_sums else 2
            grad_out, master_out, low_out, left_out, right_out = refs[-5 - tail : -tail]
            sums = refs[-tail:][:2]
            copies = []
            for sum_ref, early_ref, size, sem in zip(
                sums, early_refs, sizes, refs[-tail:][2:], strict=False
            ):
                at = 0
                for index, (_, first, number) in enumerate(early_spans):
                    copies.append(
                        pltpu.make_async_copy(
                            early_ref.at[pl.ds(at * size, number * size)],
                            sum_ref.at[pl.ds((first - start) * size, number * size)],
                            sem.at[index],
                        )
                    )
                    at += number

            @pl.when(step == 0)
            def _():
                for copy in copies:
                    copy.start()
        else:
            grad_out, master_out, low_out = refs[-5:-2]
            sums = refs[-2:]
        grad = source_refs[0][...]
        for at, ref in zip(starts[1:], source_refs[1:]):
            grad = jnp.where(step >= at, ref[...], grad)
        grad_out[...] = grad
        turned = grad.T.astype(low)
        grad = grad.astype(low)
        base = place(step) * chunk - start if stats else 0
        updates = []
        for b in range(chunk):
            side = turned[b * BLOCK_WIDTH : (b + 1) * BLOCK_WIDTH, :]
            upright = grad[:, b * BLOCK_WIDTH : (b + 1) * BLOCK_WIDTH]
            at = base + b
            if stats:
                left_rows = pl.ds(pl.multiple_of(at * rows, 8), rows)
                right_rows = pl.ds(pl.multiple_of(at * BLOCK_WIDTH, 8), BLOCK_WIDTH)
            else:
                left_rows = slice(b * rows, (b + 1) * rows)
                right_rows = slice(b * BLOCK_WIDTH, (b + 1) * BLOCK_WIDTH)
            sums[0][left_rows, :rows] = jnp.dot(upright, side, preferred_element_type=wide)
            sums[1][right_rows, :BLOCK_WIDTH] = lax.dot_general(
                side, side, (((1,), (1,)), ((), ())), preferred_element_type=wide
            )
            half = jnp.dot(right_mat[b], side, preferred_element_type=wide).astype(low)
            updates.append(jnp.dot(half, left_mat[b], preferred_element_type=wide))
        new = master_ref[...] - shampoo_rate * jnp.concatenate(updates, axis=0).T
        master_out[...] = new
        low_out[...] = new.astype(low)
        if stats:

            @pl.when(step == steps - 1)
            def _():
                for copy in copies:
                    copy.wait()
                for sum_ref, stat_ref, out in zip(
                    sums, stat_refs, (left_out, right_out), strict=True
                ):
                    size = out.shape[0]
                    here = min(LANES, stats[0].shape[2] - start)

                    @pl.loop(0, size, unroll=8)
                    def _(i):
                        slab = sum_ref[pl.ds(i, here, stride=size), :].T
                        out[i, :, :here] = 0.5 * stat_ref[i, :, :here] + 0.5 * slab[:size]

    def source_spec(index):
        first = spans[index][0] // chunk
        count = spans[index][2] // chunk

        def at(step):
            return (0, first + jnp.clip(step - starts[index], 0, count - 1))

        return pl.BlockSpec((rows, wide_cols), at)

    def lanes_spec(size):
        return pl.BlockSpec((size, size, LANES), lambda step: (0, 0, group))

    def mats_spec(size):
        return pl.BlockSpec((chunk, size, size), lambda step: (place(step), 0, 0))

    def sums_spec(size):
        return pl.BlockSpec((chunk * size, LANES), lambda step: (step, 0))

    own = pl.BlockSpec((rows, wide_cols), lambda step: (0, place(step)))
    anywhere = pl.BlockSpec(memory_space=pl.ANY)
    in_specs = [source_spec(i) for i in range(len(sources))] + [own] + [mats_spec(s) for s in sizes]
    out_specs = [own, own, own]
    outs = [jax.ShapeDtypeStruct((rows, cols), kind) for kind in (wide, wide, low)]
    scratch = []
    if stats:
        in_specs += [lanes_spec(s) for s in sizes] + [anywhere for _ in early_sums]
        out_specs += [lanes_spec(s) for s in sizes]
        outs += [jax.ShapeDtypeStruct(stat.shape, wide) for stat in stats]
        scratch = [pltpu.VMEM((LANES * s, LANES), wide) for s in sizes]
        if early_sums:
            scratch += [pltpu.SemaphoreType.DMA((len(early_spans),)) for _ in sizes]
    else:
        out_specs += [sums_spec(s) for s in sizes]
        outs += [jax.ShapeDtypeStruct((steps * chunk * s, LANES), wide) for s in sizes]
    operands = [*sources, master, *mats, *(stats or []), *early_sums]
    number = steps * chunk
    return pl.pallas_call(
        body,
        grid=(steps,),
        in_specs=in_specs + [anywhere for _ in filled],
        out_specs=out_specs,
        out_shape=outs,
        scratch_shapes=scratch,
        input_output_aliases={len(operands) + i: i for i in range(len(filled))},
        cost_estimate=lasting(number * 0.25),
        name="shampoo",
    )(*operands, *filled)


def local(
    block_input,
    cotangent,
    master,
    left_stats,
    right_stats,
    left_roots,
    right_roots,
    vec,
    vec_mom,
    time_table,
    class_table,
    bucket,
    label,
    owner,
):
    tensor_size = lax.axis_size("tensor")
    data_size = lax.axis_size("dp")
    rings = tensor_size == 2 and data_size == 2 * len(RING)
    tensor_index = lax.axis_index("tensor")
    data_index = lax.axis_index("dp")
    row_count, width = block_input.shape
    own_rows = master.shape[0]
    head_cols = width // tensor_size
    local_heads = head_cols // HEAD_DIM
    hidden_cols = FF // tensor_size
    group_images = row_count // PATCHES * tensor_size
    images_all = group_images * data_size
    scale_dot = HEAD_DIM ** (-0.5)
    widths = [6 * head_cols, 3 * head_cols, head_cols, hidden_cols, hidden_cols, hidden_cols]
    bounds = [0]
    for piece_width in widths:
        bounds.append(bounds[-1] + piece_width)
    devices = ("dp", "tensor")

    if rings:
        order = lax.dynamic_index_in_dim(relative_order(), data_index, 0, keepdims=False)
        table = ((order[None, :] - owner[:, None]) % data_size).reshape(-1)

        def ring_of(first, last, *ready):
            return RingGather(after(master[:, bounds[first] : bounds[last]].astype(low), *ready))

        def matrices(ring, first, last):
            return assemble(ring.pieces, table, first, widths[first:last], data_size)

        def spread(rows):
            return [rows, across_tensor(rows)]

        def gathered_sum(parts, *before):
            got = across_tensor(parts[1].astype(low))
            return parts[0] + after(got, *before).astype(wide)
    else:

        def weights(first, last):
            own = master[:, bounds[first] : bounds[last]].astype(low)
            gathered = lax.all_gather(own, "dp", axis=0, tiled=True)
            natural, at = [], 0
            for index in range(first, last):
                piece = gathered[:, at : at + widths[index]]
                natural.append(roll_blocks(piece, -owner[index], data_size))
                at += widths[index]
            return natural

        def to_owners(pairs, first):
            grads = [
                lax.dot_general(
                    left[0], right[0], (((0,), (0,)), ((), ())), preferred_element_type=wide
                ).astype(low)
                for left, right in pairs
            ]
            flat = [roll_blocks(grad, owner[first + i], data_size) for i, grad in enumerate(grads)]
            flat = jnp.concatenate(flat, axis=1)
            return lax.psum_scatter(flat, "dp", scatter_dimension=0, tiled=True).astype(wide)

        def spread(rows):
            return [lax.all_gather(rows, "tensor", axis=0, tiled=True)]

        def gathered_sum(parts):
            summed = lax.psum_scatter(
                parts[0].astype(low), "tensor", scatter_dimension=0, tiled=True
            )
            return summed.astype(wide)

    n_own = rms_norm(block_input)
    if rings:
        n_partner = across_tensor(n_own.astype(low))
        ring = ring_of(1, 3)
        hop = ring.hop()
    marks = jnp.stack([bucket, label], axis=1)
    marks = jnp.broadcast_to(marks[None], (data_size,) + marks.shape)
    marks = lax.all_to_all(marks, "dp", 0, 0, tiled=True).reshape(images_all, 2)
    if rings:
        marks = after(marks, hop)
        hop = ring.hop()
    cond = time_table[marks[:, 0]] + class_table[marks[:, 1]]
    cond = lax.dynamic_slice_in_dim(cond, tensor_index * head_cols, head_cols, 1)
    lifted = jax.nn.silu(cond).astype(low)
    if rings:
        lifted = after(lifted, hop, n_partner)
        hop = ring.hop(cond)
    ada = master[:, : bounds[1]].astype(low)
    row_map = lax.broadcasted_iota(jnp.int32, (6 * images_all, 6 * head_cols), 0) // images_all
    col_map = lax.broadcasted_iota(jnp.int32, (6 * images_all, 6 * head_cols), 1) // head_cols
    on_map = row_map == col_map
    lifted_maps = jnp.where(on_map, jnp.tile(lifted, (6, 6)), jnp.zeros((), low))
    partial_mod = lax.dot_general(
        lifted_maps, ada, (((1,), (1,)), ((), ())), preferred_element_type=wide
    )
    send = partial_mod.reshape(6, data_size, group_images, own_rows).transpose(1, 0, 2, 3)
    send = jnp.broadcast_to(send[:, None], (data_size, tensor_size) + send.shape[1:])
    send = send.reshape((data_size * tensor_size,) + send.shape[2:])
    if rings:
        send = after(send, hop)
        ring_two = ring_of(3, 6, hop)
        hop = ring.hop()
        hop_two = ring_two.hop()
    got = lax.all_to_all(send, devices, 0, 0, tiled=True)
    if rings:
        got = after(got, hop)
        qkv_cols, proj_cols = matrices(ring, 1, 3)
        qkv_cols = lax.optimization_barrier(qkv_cols.T)
        ring = ring_two
        hop = ring.hop()
    got = got.reshape((data_size, tensor_size) + got.shape[1:]).sum(axis=1)
    got = jnp.roll(got, -owner[0], axis=0).transpose(2, 1, 0, 3)
    mods = got.reshape(group_images, 6, width) + vec[: 6 * width].reshape(6, width)

    mod = lax.dynamic_index_in_dim(mods, tensor_index, 0, keepdims=False)
    shift_one, scale_one, gate_one, shift_two, scale_two, gate_two = [
        mod[index][None, :] for index in range(6)
    ]
    gains = vec[6 * width :].reshape(2, HEAD_DIM)

    h_one = (n_own * (1.0 + scale_one) + shift_one).astype(low)
    if rings:
        mod_partner = lax.dynamic_index_in_dim(mods, 1 - tensor_index, 0, keepdims=False)
        h_partner = n_partner.astype(wide) * (1.0 + mod_partner[1][None]) + mod_partner[0][None]
        rows_one = [h_one, after(h_partner.astype(low), hop_two)]
    else:
        rows_one = spread(h_one)
        qkv_cols, proj_cols = weights(1, 3)
        qkv_cols = qkv_cols.T
        w_one, w_three, w_two = weights(3, 6)
    send_two = (gate_two * cotangent).astype(low)
    back_two = spread(send_two)

    cosine, sine = rope_tables()
    kept = []
    branch_parts = []
    for part, rows in enumerate(reversed(rows_one)):
        if rings and part == 1:
            rows = after(rows, hop, branch_parts)
            roots = [
                after(side[0].transpose(1, 2, 0), hop) for side in (left_roots, right_roots)
            ]
            mats = to_matrices(*roots)
            stats = [left_stats[0].transpose(1, 2, 0), right_stats[0].transpose(1, 2, 0)]
            hop = ring.hop()
        raw = jnp.einsum("rd,cd->rc", rows, qkv_cols, preferred_element_type=wide)
        raw = raw.reshape(rows.shape[0] // PATCHES, PATCHES, 3, local_heads, HEAD_DIM)
        query_norm = rms_norm(raw[:, :, 0])
        key_norm = rms_norm(raw[:, :, 1])
        query = rotate(query_norm * gains[0], cosine, sine).astype(low)
        keys = rotate(key_norm * gains[1], cosine, sine).astype(low)
        values = raw[:, :, 2].astype(low)
        scores = jnp.einsum("gphd,gqhd->ghpq", query, keys, preferred_element_type=wide) * scale_dot
        peak = jnp.max(scores, axis=-1, keepdims=True)
        expo = jnp.exp(scores - peak)
        total = jnp.sum(expo, axis=-1, keepdims=True)
        logsum = peak + jnp.log(total)
        probs = (expo / total).astype(low)
        attended = jnp.einsum("ghpq,gqhd->gphd", probs, values, preferred_element_type=wide)
        attended = attended.astype(low).reshape(rows.shape[0], head_cols)
        kept.append((raw, query_norm, key_norm, query, keys, values, logsum, attended))
        branch_parts.append(
            jnp.einsum("rh,oh->ro", attended, proj_cols, preferred_element_type=wide)
        )
    kept.reverse()
    branch_parts.reverse()
    if rings:
        branch_one = gathered_sum(branch_parts, hop, branch_parts[0], mats)
        hop = ring.hop()
        attended_parts = lax.optimization_barrier([saved[-1] for saved in kept])
    else:
        branch_one = gathered_sum(branch_parts)
    middle = block_input + gate_one * branch_one
    n_two = rms_norm(middle)
    h_two = (n_two * (1.0 + scale_two) + shift_two).astype(low)
    rows_two = spread(h_two)
    if rings:
        rows_two[1] = after(rows_two[1], hop)
        w_one, w_three, w_two = matrices(ring, 3, 6)

    branch_parts, hidden_parts, gate_parts, up_parts, d_parts = [], [], [], [], []
    for rows, back in zip(rows_two, back_two, strict=True):
        gate_pre = jnp.dot(rows, w_one, preferred_element_type=wide)
        up_pre = jnp.dot(rows, w_three, preferred_element_type=wide)
        d_hidden = jnp.dot(back, w_two, preferred_element_type=wide)
        sigma = jax.nn.sigmoid(gate_pre)
        silu_gate = gate_pre * sigma
        hidden = (silu_gate * up_pre).astype(low)
        d_gate_pre = (d_hidden * up_pre * sigma * (1.0 + gate_pre * (1.0 - sigma))).astype(low)
        d_up_pre = (d_hidden * silu_gate).astype(low)
        hidden_parts.append(hidden)
        gate_parts.append(d_gate_pre)
        up_parts.append(d_up_pre)
        d_parts.append(
            jnp.einsum("rf,df->rd", d_gate_pre, w_one, preferred_element_type=wide)
            + jnp.einsum("rf,df->rd", d_up_pre, w_three, preferred_element_type=wide)
        )

    if rings:
        hidden_parts[0] = after(hidden_parts[0], d_parts)
        own, other = grads_mlp(
            rows_two, back_two, gate_parts, up_parts, hidden_parts, table, data_size
        )
        ring = RingScatter(own, other, True)
    else:
        grad_mlp = to_owners(
            [(rows_two, gate_parts), (rows_two, up_parts), (back_two, hidden_parts)], 3
        )
    d_h_two = gathered_sum(d_parts, own) if rings else gathered_sum(d_parts)
    if not rings:
        attended_parts = [saved[-1] for saved in kept]
    d_shift_two = jnp.sum(d_h_two, axis=0)
    d_scale_two = jnp.sum(d_h_two * n_two, axis=0)
    d_middle = cotangent + norm_back(middle, n_two, d_h_two * (1.0 + scale_two))
    d_gate_one = jnp.sum(d_middle * branch_one, axis=0)
    send_one = (gate_one * d_middle).astype(low)
    back_one = spread(send_one)
    if rings:
        hop = ring.hop()
        w_two = after(w_two, send_one)
    branch_parts = [
        jnp.einsum("rf,of->ro", hidden, w_two, preferred_element_type=wide)
        for hidden in hidden_parts
    ]
    if rings:
        back_one[0] = after(back_one[0], ring.sent, branch_parts[1])
        branch_got = across_tensor(branch_parts[1].astype(low))

    d_parts, raw_parts = [], []
    gain_grads = jnp.zeros((2, HEAD_DIM), wide)
    for part, (back, saved) in enumerate(zip(back_one, kept, strict=True)):
        if rings and part == 1:
            back = after(back, d_parts, branch_got)
        raw, query_norm, key_norm, query, keys, values, logsum, attended = saved
        d_attended = jnp.dot(back, proj_cols, preferred_element_type=wide).astype(low)
        if rings:
            d_attended = after(d_attended, hop)
            hop = ring.hop()
        d_attended = d_attended.reshape(values.shape)
        scores = jnp.einsum("gphd,gqhd->ghpq", query, keys, preferred_element_type=wide) * scale_dot
        probs_full = jnp.exp(scores - logsum)
        d_values = jnp.einsum(
            "ghpq,gphd->gqhd", probs_full.astype(low), d_attended, preferred_element_type=wide
        )
        d_probs = jnp.einsum("gphd,gqhd->ghpq", d_attended, values, preferred_element_type=wide)
        d_scores = probs_full * (d_probs - jnp.sum(probs_full * d_probs, axis=-1, keepdims=True))
        d_scores = d_scores.astype(low)
        d_query = (
            jnp.einsum("ghpq,gqhd->gphd", d_scores, keys, preferred_element_type=wide) * scale_dot
        )
        d_keys = (
            jnp.einsum("ghpq,gphd->gqhd", d_scores, query, preferred_element_type=wide) * scale_dot
        )
        d_query_norm = rotate(d_query, cosine, -sine)
        d_key_norm = rotate(d_keys, cosine, -sine)
        gain_grads += jnp.stack(
            [
                jnp.sum(d_query_norm * query_norm, axis=(0, 1, 2)),
                jnp.sum(d_key_norm * key_norm, axis=(0, 1, 2)),
            ]
        )
        d_raw_query = norm_back(raw[:, :, 0], query_norm, d_query_norm * gains[0])
        d_raw_key = norm_back(raw[:, :, 1], key_norm, d_key_norm * gains[1])
        d_raw = jnp.stack([d_raw_query, d_raw_key, d_values], axis=2).astype(low)
        d_raw = d_raw.reshape(back.shape[0], 3 * head_cols)
        raw_parts.append(d_raw)
        d_parts.append(jnp.einsum("rc,cd->rd", d_raw, qkv_cols, preferred_element_type=wide))
    if rings:
        held = after(raw_parts[1], hop, d_parts)
        hop = ring.hop()
        held = after(held, ring.sent)
        own, other = grads_att(
            rows_one, back_one, [raw_parts[0], held], attended_parts, table, data_size
        )
        ring_att = RingScatter(own, other, False)
        grad_mlp = ring.total()
        hop_one = ring_att.hop()
        d_h_one = gathered_sum(d_parts, own, hop)
        branch_two = after(branch_parts[0] , d_h_one) + branch_got.astype(wide)
        lifted_late = after(lifted, d_h_one)
        lifted_maps = jnp.where(on_map, jnp.tile(lifted_late, (6, 6)), jnp.zeros((), low))
    else:
        branch_two = gathered_sum(branch_parts)
        grad_att = to_owners([(rows_one, raw_parts), (back_one, attended_parts)], 1)
        d_h_one = gathered_sum(d_parts)
    output = middle + gate_two * branch_two
    d_gate_two = jnp.sum(cotangent * branch_two, axis=0)
    d_shift_one = jnp.sum(d_h_one, axis=0)
    d_scale_one = jnp.sum(d_h_one * n_own, axis=0)
    d_inputs = d_middle + norm_back(block_input, n_own, d_h_one * (1.0 + scale_one))

    d_mod = jnp.stack([d_shift_one, d_scale_one, d_gate_one, d_shift_two, d_scale_two, d_gate_two])
    d_mod = d_mod.reshape(6, data_size, own_rows).transpose(1, 0, 2)
    d_mod = jnp.roll(d_mod, owner[0], axis=0).reshape(data_size, 6 * own_rows)
    gain_row = jnp.broadcast_to(gain_grads.reshape(1, -1), (data_size, 2 * HEAD_DIM))
    send = jnp.concatenate([d_mod, gain_row], axis=1)
    send = jnp.broadcast_to(send[:, None], (data_size, tensor_size, send.shape[1]))
    send = send.reshape(data_size * tensor_size, send.shape[2])
    got = lax.all_to_all(send, devices, 0, 0, tiled=True)
    if rings:
        blocks_ada, blocks_att = bounds[1] // BLOCK_WIDTH, (bounds[3] - bounds[1]) // BLOCK_WIDTH
        skip = LANES - blocks_ada - blocks_att
        total = bounds[6] // BLOCK_WIDTH
        grad_mlp = after(grad_mlp, hop_one)
        hop = ring_att.hop()
        group_one = shampoo(
            [grad_mlp], [(skip, LANES, total - LANES)], master, mats, [], 1, stats=stats
        )
        got = after(got, output, group_one, hop)
        hop = ring_att.hop()
    gain_sum = jnp.sum(got[:, 6 * own_rows :], axis=0)
    d_own = got[:, : 6 * own_rows].reshape(images_all, 6, own_rows).transpose(1, 0, 2)
    row_sum = jnp.sum(d_own, axis=1).reshape(-1)
    d_own = d_own.reshape(6 * images_all, own_rows)
    grad_ada = lax.dot_general(
        d_own,
        lifted_maps.astype(wide),
        (((0,), (0,)), ((), ())),
        precision=precise,
        preferred_element_type=wide,
    )
    d_lifted = lax.dot_general(
        d_own,
        ada.astype(wide),
        (((1,), (0,)), ((), ())),
        precision=precise,
        preferred_element_type=wide,
    )
    d_lifted = jnp.where(on_map, d_lifted, 0.0).reshape(6, images_all, 6 * head_cols).sum(axis=0)
    d_lifted = sum(d_lifted[:, j * head_cols : (j + 1) * head_cols] for j in range(6))
    send = jnp.concatenate(
        [
            d_lifted.reshape(data_size, group_images * head_cols),
            jnp.broadcast_to(row_sum[None, :], (data_size, 6 * own_rows)),
        ],
        axis=1,
    )
    if rings:
        grad_ada = after(grad_ada, send, hop)
        hop = ring_att.hop()
    got = lax.all_to_all(send, "dp", 0, 0, tiled=True)
    if rings:
        early = [(0, 0, blocks_ada), (0, blocks_ada + blocks_att, LANES - blocks_ada - blocks_att)]
        part = shampoo([grad_ada, grad_mlp], early, master, mats, group_one[:3], 0)
        got = after(got, part[0], hop)
    d_lifted = jnp.sum(got[:, : group_images * head_cols], axis=0).reshape(group_images, head_cols)
    cond_here = lax.dynamic_slice_in_dim(cond, data_index * group_images, group_images, 0)
    d_cond = d_lifted * silu_slope(cond_here)
    vec_rows = got[:, group_images * head_cols :].reshape(data_size, 6, own_rows)
    vec_rows = jnp.roll(vec_rows, -owner[0], axis=0).transpose(1, 0, 2).reshape(-1)
    vec_grad = jnp.concatenate([vec_rows, gain_sum])

    if rings:
        grad_att = after(ring_att.total(), part[3])
        outs = shampoo(
            [grad_att],
            [(0, blocks_ada, blocks_att)],
            master,
            mats,
            [*part[:3], *group_one[3:]],
            0,
            stats=stats,
            early=(early, part[3:]),
        )
        grad_mine, master_new, weights_low = outs[:3]
        left_new, right_new = outs[3].transpose(2, 0, 1), outs[4].transpose(2, 0, 1)
    else:
        grad_mine = jnp.concatenate([grad_ada, grad_att, grad_mlp], axis=1)
        block_count = grad_mine.shape[1] // BLOCK_WIDTH
        pieces = grad_mine.astype(low).reshape(own_rows, block_count, BLOCK_WIDTH).transpose(1, 0, 2)
        left_new = 0.5 * left_stats[0] + 0.5 * jnp.einsum(
            "bij,bkj->bik", pieces, pieces, preferred_element_type=wide
        )
        right_new = 0.5 * right_stats[0] + 0.5 * jnp.einsum(
            "bji,bjk->bik", pieces, pieces, preferred_element_type=wide
        )
        update = jnp.einsum(
            "bij,bjk->bik", left_roots[0].astype(low), pieces, preferred_element_type=wide
        )
        update = jnp.einsum(
            "bik,bkl->bil",
            update.astype(low),
            right_roots[0].astype(low),
            preferred_element_type=wide,
        )
        update = update.transpose(1, 0, 2).reshape(own_rows, block_count * BLOCK_WIDTH)
        master_new = master - shampoo_rate * update
        weights_low = master_new.astype(low)
    tokens_all = row_count * data_size * tensor_size
    mom_new = momentum * vec_mom + vec_grad
    vec_new = vec - 0.1 / tokens_all**0.5 * mom_new
    return (
        output,
        d_inputs,
        d_cond,
        grad_mine,
        left_new[None],
        right_new[None],
        master_new,
        weights_low,
        vec_new,
        mom_new,
    )


def solution(mesh):
    placed = (
        P(("dp", "tensor"), None),
        P(("dp", "tensor"), None),
        P("dp", "tensor"),
        P("dp", "tensor", None, None),
        P("dp", "tensor", None, None),
        P("dp", "tensor", None, None),
        P("dp", "tensor", None, None),
        P(),
        P(),
        P(),
        P(),
        P("dp"),
        P("dp"),
        P(),
    )
    return jax.shard_map(
        local,
        mesh=mesh,
        in_specs=placed,
        out_specs=(
            P(("dp", "tensor"), None),
            P(("dp", "tensor"), None),
            P("dp", "tensor"),
            P("dp", "tensor"),
            P("dp", "tensor", None, None),
            P("dp", "tensor", None, None),
            P("dp", "tensor"),
            P("dp", "tensor"),
            P(),
            P(),
        ),
        check_vma=False,
    )
```
